256 devices in a mesh: row: 8 (over y_lo, x), col: 16 (over z, y_hi), lag: 2 (over core).
Axes of the slice: x: 4, y: 4 (y_hi: 2, y_lo: 2; y = y_hi * 2 + y_lo), z: 8, core: 2. Of those that a mesh axis runs over, the one named last changes fastest.
Arguments:
- history: bfloat16 [8, 16, 128, 4096], P('lag', 'col', None, 'row'), may hold values from -6 to 6
- kernel_tiles: bfloat16 [8, 16, 8, 12, 256, 256], P('row', 'col', 'lag'), may hold values from -0.046875 to 0.046875
- tile_rows: int32 [8, 16, 8, 12], P('row', 'col', 'lag'), may hold values from 0 to 31
- tile_cols: int32 [8, 16, 8, 12], P('row', 'col', 'lag'), may hold values from 0 to 15
- tile_count: int32 [8, 16, 8], P('row', 'col', 'lag'), may hold values from 3 to 12, as said below
- base_stress: float32 [128, 65536], P(None, ('row', 'col', 'lag')), may hold values from -6 to 6
- prev_rate: float32 [128, 65536], P(None, ('row', 'col', 'lag')), may hold values from -6 to 6
- direct_effect: float32 [128, 65536], P(None, ('row', 'col', 'lag')), may hold values from 0.5 to 2
- state_var: float32 [128, 65536], P(None, ('row', 'col', 'lag')), may hold values from -2 to 2
Outputs:
- stress_change: float32 [128, 65536], P(None, ('row', 'col', 'lag'))
- new_rate: float32 [128, 65536], P(None, ('row', 'col', 'lag'))
The draws below stay inside these ranges and needn't reach their ends.
Inputs may be any that keep to these rules, and one draw needn't show every extreme that they name: `tile_count`: every draw has some device and lag with all 12 slots live.
All inputs are finite; a program needn't handle non-finite values.
Results may differ from the reference program's by a relative error of at most 0.0003.
Values may be sent and summed in bfloat16 or wider, within the bound.
A program may use at most 64 MiB of HBM per device.

```python
import math
import jax
import jax.numpy as jnp
from jax import lax

TILE = 256
REC_DEV = 8192
SIMS = 128
LAGS = 8
NT = 12
NEWTON = 4
ELEMS = 65536
SRC_DEV = 4096
RB = 32
CB = 16
N_ROW = 8
N_COL = 16


def draw_tile_count(key, part):
    first_key, second_key = jax.random.split(jax.random.fold_in(key, 17))
    counts = jax.random.randint(first_key, (N_ROW * N_COL * LAGS,), max(1, NT // 4), NT + 1)
    chosen = jax.random.randint(second_key, (), 0, N_ROW * N_COL * LAGS)
    counts = jnp.where(jnp.arange(N_ROW * N_COL * LAGS) == chosen, NT, counts)
    return counts.reshape(N_ROW, N_COL, LAGS).astype(jnp.int32)


def touch_ends(entries, key, least, largest):
    spot = [jax.random.randint(jax.random.fold_in(key, axis), (), 0, length) for axis, length in enumerate(entries.shape)]
    widest = entries.shape.index(max(entries.shape))
    beside = spot[:widest] + [(spot[widest] + 1) % entries.shape[widest]] + spot[widest + 1:]
    return entries.at[tuple(spot)].set(least).at[tuple(beside)].set(largest)


def block_scale(stream_key, extent, pieces, smallest, largest):
    def one(axis_at, blocks):
        heights = jax.random.uniform(jax.random.fold_in(jax.random.fold_in(stream_key, 6), axis_at), (blocks,), jnp.float32, smallest / len(pieces), largest / len(pieces))
        return jnp.repeat(jnp.exp(heights), extent[axis_at] // blocks).reshape((-1,) + (1,) * (len(extent) - axis_at - 1))

    level = one(*pieces[0])
    for cut in pieces[1:]:
        level = level * one(*cut)
    return level


def bell_draw(own_key, shape, deviation, most, shards=(), held_as=jnp.bfloat16):
    entries = jax.random.normal(own_key, shape, jnp.float32) * deviation
    if len(shards) > 0:
        entries = block_scale(own_key, shape, shards, -0.22, 0.18) * entries
    return jnp.clip(entries, min=-most, max=most).astype(held_as)


def setup_inputs(seed: int = 0) -> dict:
    key_list = jax.random.split(jax.random.key(seed), 10)
    history = bell_draw(key_list[0], (LAGS, N_COL, SIMS, SRC_DEV), 1.0, 6.0, ((0, 2), (1, 16), (3, 8)))
    kernel_tiles = bell_draw(key_list[1], (N_ROW, N_COL, LAGS, NT, TILE, TILE), (TILE * LAGS * N_COL // 2) ** -0.5, 0.046875, ((0, 8), (1, 16), (2, 2)))
    tile_rows = touch_ends(jax.random.randint(key_list[2], (N_ROW, N_COL, LAGS, NT), 0, RB), jax.random.fold_in(key_list[2], 1), 0, RB - 1).astype(jnp.int32)
    tile_cols = touch_ends(jax.random.randint(key_list[3], (N_ROW, N_COL, LAGS, NT), 0, CB), jax.random.fold_in(key_list[3], 1), 0, CB - 1).astype(jnp.int32)
    tile_count = draw_tile_count(jax.random.fold_in(key_list[9], 71), 0)
    base_stress = bell_draw(key_list[5], (SIMS, ELEMS), 1.0, 6.0, ((1, 256),), jnp.float32)
    prev_rate = bell_draw(key_list[6], (SIMS, ELEMS), 1.0, 6.0, ((1, 256),), jnp.float32)
    direct_effect = jnp.clip(jnp.exp(math.log(2.0) - 1.3862944 * jax.random.uniform(key_list[7], (SIMS, ELEMS), jnp.float32) ** block_scale(key_list[7], (SIMS, ELEMS), ((1, 256),), -0.2, 0.2)), 0.5, 2.0)
    state_var = jnp.clip(jax.random.uniform(key_list[8], (SIMS, ELEMS), jnp.float32, -2.0, 2.0) * block_scale(key_list[8], (SIMS, ELEMS), ((1, 256),), -0.4, 0.0), -2.0, 2.0)
    return dict(history=history, kernel_tiles=kernel_tiles, tile_rows=tile_rows, tile_cols=tile_cols, tile_count=tile_count, base_stress=base_stress, prev_rate=prev_rate, direct_effect=direct_effect, state_var=state_var)


def inverse_sinh(value):
    magnitude = jnp.abs(value)
    return jnp.sign(value) * jnp.log(magnitude + jnp.sqrt(1.0 + magnitude * magnitude))

def reference(history, kernel_tiles, tile_rows, tile_cols, tile_count, base_stress, prev_rate, direct_effect, state_var):
    col_blocks = SRC_DEV // TILE
    row_blocks = REC_DEV // TILE

    def one_row(row_index):

        def one_col(running, col_index):
            blocks = history[:, col_index].astype(jnp.float32).reshape(LAGS, SIMS, col_blocks, TILE)
            choose = jax.nn.one_hot(tile_cols[row_index, col_index], col_blocks, dtype=jnp.float32)
            picked = jnp.einsum('lkb,lsbj->lksj', choose, blocks, precision=lax.Precision.HIGHEST)
            weights = kernel_tiles[row_index, col_index].astype(jnp.float32)
            contrib = jnp.einsum('lksj,lkij->lksi', picked, weights, precision=lax.Precision.HIGHEST)
            alive_mask = (jnp.arange(NT)[None, :] < tile_count[row_index, col_index][:, None]).astype(jnp.float32)
            placing = jax.nn.one_hot(tile_rows[row_index, col_index], row_blocks, dtype=jnp.float32) * alive_mask[:, :, None]
            added = jnp.einsum('lkb,lksi->sbi', placing, contrib, precision=lax.Precision.HIGHEST)
            return (running + added.reshape(SIMS, REC_DEV), None)
        summed, unused = lax.scan(one_col, jnp.zeros((SIMS, REC_DEV), jnp.float32), jnp.arange(N_COL))
        return summed
    blocks_all = lax.map(one_row, jnp.arange(N_ROW))
    stress_change = jnp.transpose(blocks_all, (1, 0, 2)).reshape(SIMS, N_ROW * REC_DEV)
    driving = base_stress + stress_change
    factor = jnp.exp(state_var) / 2.0
    velocity = prev_rate
    for step in range(NEWTON):
        scaled = velocity * factor
        misfit = direct_effect * inverse_sinh(scaled) + 0.5 * velocity - driving
        slope = direct_effect * factor / jnp.sqrt(1.0 + scaled * scaled) + 0.5
        velocity = velocity - misfit / slope
    return (stress_change, velocity)
```

```python
import jax
import jax.numpy as jnp
from jax import lax
from jax.sharding import PartitionSpec as P

NEWTON = 4


def inverse_sinh(value):
    magnitude = jnp.abs(value)
    return jnp.sign(value) * jnp.log(magnitude + jnp.sqrt(1.0 + magnitude * magnitude))


def local(
    history,
    kernel_tiles,
    tile_rows,
    tile_cols,
    tile_count,
    base_stress,
    prev_rate,
    direct_effect,
    state_var,
):
    gathered = lax.all_gather(history, "row", axis=3, tiled=True)
    lag_local = gathered.shape[0]
    sims_count = gathered.shape[2]
    tile_side = kernel_tiles.shape[4]
    slots = kernel_tiles.shape[3]
    col_blocks = gathered.shape[3] // tile_side
    blocks = gathered.reshape(lag_local, sims_count, col_blocks, tile_side)
    choose = jax.nn.one_hot(tile_cols[0, 0], col_blocks, dtype=jnp.bfloat16)
    picked = jnp.einsum(
        "lkb,lsbj->lksj", choose, blocks, preferred_element_type=jnp.float32
    ).astype(jnp.bfloat16)
    contrib = jnp.einsum(
        "lksj,lkij->slki", picked, kernel_tiles[0, 0], preferred_element_type=jnp.float32
    )
    rec_local = base_stress.shape[1] * lax.axis_size(("col", "lag"))
    row_blocks = rec_local // tile_side
    alive_mask = (jnp.arange(slots)[None, :] < tile_count[0, 0][:, None]).astype(jnp.float32)
    masked = (contrib * alive_mask[None, :, :, None]).reshape(
        sims_count, lag_local * slots, tile_side
    )
    targets = tile_rows[0, 0].reshape(lag_local * slots)
    placed = (
        jnp.zeros((sims_count, row_blocks, tile_side), jnp.float32).at[:, targets, :].add(masked)
    )
    partial_stress = placed.reshape(sims_count, rec_local)
    stress_change = lax.psum_scatter(
        partial_stress, ("col", "lag"), scatter_dimension=1, tiled=True
    )
    driving = base_stress + stress_change
    factor = jnp.exp(state_var) / 2.0
    velocity = prev_rate
    for step in range(NEWTON):
        scaled = velocity * factor
        misfit = direct_effect * inverse_sinh(scaled) + 0.5 * velocity - driving
        slope = direct_effect * factor / jnp.sqrt(1.0 + scaled * scaled) + 0.5
        velocity = velocity - misfit / slope
    return (stress_change, velocity)


def solution(mesh):
    return jax.shard_map(
        local,
        mesh=mesh,
        in_specs=(
            P("lag", "col", None, "row"),
            P("row", "col", "lag", None, None, None),
            P("row", "col", "lag", None),
            P("row", "col", "lag", None),
            P("row", "col", "lag"),
            P(None, ("row", "col", "lag")),
            P(None, ("row", "col", "lag")),
            P(None, ("row", "col", "lag")),
            P(None, ("row", "col", "lag")),
        ),
        out_specs=(P(None, ("row", "col", "lag")), P(None, ("row", "col", "lag"))),
        check_vma=False,
    )
```

```python
import functools

import jax
import jax.numpy as jnp
from jax import lax
from jax.experimental import pallas as pl
from jax.experimental.pallas import tpu as pltpu
from jax.sharding import PartitionSpec as P

NEWTON = 4
MESH = pl.DeviceIdType.MESH


def inverse_sinh(value):
    magnitude = jnp.abs(value)
    return jnp.sign(value) * jnp.log(magnitude + jnp.sqrt(1.0 + magnitude * magnitude))


def scatter_kernel(n_col, n_lag, part_ref, out_ref, slots, send_sem, recv_sem):
    row = lax.axis_index("row")
    me = lax.axis_index("col") * n_lag + lax.axis_index("lag")
    group = n_col * n_lag

    def peer(t):
        return (row, t // n_lag, t % n_lag)

    barrier = pltpu.get_barrier_semaphore()
    for d in range(1, group):
        t = lax.rem(me + d, group)
        pl.semaphore_signal(barrier, inc=1, device_id=peer(t), device_id_type=MESH)
    pl.semaphore_wait(barrier, group - 1)

    sends = []
    for d in range(1, group):
        t = lax.rem(me + d, group)
        copy = pltpu.make_async_remote_copy(
            src_ref=part_ref.at[t],
            dst_ref=slots.at[me],
            send_sem=send_sem.at[t],
            recv_sem=recv_sem.at[me],
            device_id=peer(t),
            device_id_type=MESH,
        )
        copy.start()
        sends.append(copy)

    total = part_ref[me]
    for d in range(1, group):
        s = lax.rem(me + group - d, group)
        incoming = pltpu.make_async_remote_copy(
            src_ref=part_ref.at[s],
            dst_ref=slots.at[s],
            send_sem=send_sem.at[s],
            recv_sem=recv_sem.at[s],
            device_id=peer(s),
            device_id_type=MESH,
        )
        incoming.wait_recv()
        total = total + slots[s]
    out_ref[...] = total
    for copy in sends:
        copy.wait_send()


def reduce_scatter(part, n_col, n_lag):
    group, sims, tile = part.shape
    return pl.pallas_call(
        functools.partial(scatter_kernel, n_col, n_lag),
        out_shape=jax.ShapeDtypeStruct((sims, tile), jnp.float32),
        in_specs=[pl.BlockSpec(memory_space=pltpu.VMEM)],
        out_specs=pl.BlockSpec(memory_space=pltpu.VMEM),
        scratch_shapes=[
            pltpu.VMEM((group, sims, tile), jnp.float32),
            pltpu.SemaphoreType.DMA((group,)),
            pltpu.SemaphoreType.DMA((group,)),
        ],
        compiler_params=pltpu.CompilerParams(
            collective_id=0, has_side_effects=True, vmem_limit_bytes=48 * 1024 * 1024
        ),
    )(part)


def local(
    n_col,
    n_lag,
    history,
    kernel_tiles,
    tile_rows,
    tile_cols,
    tile_count,
    base_stress,
    prev_rate,
    direct_effect,
    state_var,
):
    gathered = lax.all_gather(history, "row", axis=3, tiled=True)
    lag_local = gathered.shape[0]
    sims_count = gathered.shape[2]
    tile_side = kernel_tiles.shape[4]
    slots = kernel_tiles.shape[3]
    col_blocks = gathered.shape[3] // tile_side
    blocks = gathered.reshape(lag_local, sims_count, col_blocks, tile_side)
    choose = jax.nn.one_hot(tile_cols[0, 0], col_blocks, dtype=jnp.bfloat16)
    picked = jnp.einsum(
        "lkb,lsbj->lksj", choose, blocks, preferred_element_type=jnp.float32
    ).astype(jnp.bfloat16)
    contrib = jnp.einsum(
        "lksj,lkij->lksi", picked, kernel_tiles[0, 0], preferred_element_type=jnp.float32
    )
    row_blocks = n_col * n_lag
    alive_mask = (jnp.arange(slots)[None, :] < tile_count[0, 0][:, None]).astype(jnp.float32)
    masked = (contrib * alive_mask[:, :, None, None]).reshape(
        lag_local * slots, sims_count, tile_side
    )
    targets = tile_rows[0, 0].reshape(lag_local * slots)
    placed = (
        jnp.zeros((row_blocks, sims_count, tile_side), jnp.float32).at[targets].add(masked)
    )
    stress_change = reduce_scatter(placed, n_col, n_lag)
    driving = base_stress + stress_change
    factor = jnp.exp(state_var) / 2.0
    velocity = prev_rate
    for step in range(NEWTON):
        scaled = velocity * factor
        misfit = direct_effect * inverse_sinh(scaled) + 0.5 * velocity - driving
        slope = direct_effect * factor / jnp.sqrt(1.0 + scaled * scaled) + 0.5
        velocity = velocity - misfit / slope
    return (stress_change, velocity)


def solution(mesh):
    return jax.shard_map(
        functools.partial(local, mesh.shape["col"], mesh.shape["lag"]),
        mesh=mesh,
        in_specs=(
            P("lag", "col", None, "row"),
            P("row", "col", "lag", None, None, None),
            P("row", "col", "lag", None),
            P("row", "col", "lag", None),
            P("row", "col", "lag"),
            P(None, ("row", "col", "lag")),
            P(None, ("row", "col", "lag")),
            P(None, ("row", "col", "lag")),
            P(None, ("row", "col", "lag")),
        ),
        out_specs=(P(None, ("row", "col", "lag")), P(None, ("row", "col", "lag"))),
        check_vma=False,
    )
```

```python
import functools

import jax
import jax.numpy as jnp
from jax import lax
from jax.experimental import pallas as pl
from jax.experimental.pallas import tpu as pltpu
from jax.sharding import PartitionSpec as P

NEWTON = 4
MESH = pl.DeviceIdType.MESH


def inverse_sinh(value):
    magnitude = jnp.abs(value)
    return jnp.sign(value) * jnp.log(magnitude + jnp.sqrt(1.0 + magnitude * magnitude))


def scatter_kernel(n_col, part_ref, out_ref, slots, send_sem, recv_sem):
    row = lax.axis_index("row")
    me = lax.axis_index("col")
    lag = lax.axis_index("lag")

    def peer(t):
        return (row, t, lag)

    barrier = pltpu.get_barrier_semaphore()
    for d in range(1, n_col):
        t = lax.rem(me + d, n_col)
        pl.semaphore_signal(barrier, inc=1, device_id=peer(t), device_id_type=MESH)
    pl.semaphore_wait(barrier, n_col - 1)

    sends = []
    for d in range(1, n_col):
        t = lax.rem(me + d, n_col)
        copy = pltpu.make_async_remote_copy(
            src_ref=part_ref.at[t],
            dst_ref=slots.at[me],
            send_sem=send_sem.at[t],
            recv_sem=recv_sem.at[me],
            device_id=peer(t),
            device_id_type=MESH,
        )
        copy.start()
        sends.append(copy)

    total = part_ref[me]
    for d in range(1, n_col):
        s = lax.rem(me + n_col - d, n_col)
        incoming = pltpu.make_async_remote_copy(
            src_ref=part_ref.at[s],
            dst_ref=slots.at[s],
            send_sem=send_sem.at[s],
            recv_sem=recv_sem.at[s],
            device_id=peer(s),
            device_id_type=MESH,
        )
        incoming.wait_recv()
        total = total + slots[s]
    out_ref[...] = total
    for copy in sends:
        copy.wait_send()


def reduce_scatter(part, n_col):
    group, sims, tile = part.shape
    return pl.pallas_call(
        functools.partial(scatter_kernel, n_col),
        out_shape=jax.ShapeDtypeStruct((sims, tile), jnp.float32),
        in_specs=[pl.BlockSpec(memory_space=pltpu.VMEM)],
        out_specs=pl.BlockSpec(memory_space=pltpu.VMEM),
        scratch_shapes=[
            pltpu.VMEM((group, sims, tile), jnp.float32),
            pltpu.SemaphoreType.DMA((group,)),
            pltpu.SemaphoreType.DMA((group,)),
        ],
        compiler_params=pltpu.CompilerParams(
            collective_id=0, has_side_effects=True, vmem_limit_bytes=48 * 1024 * 1024
        ),
    )(part)


def local(
    n_col,
    n_lag,
    history,
    kernel_tiles,
    tile_rows,
    tile_cols,
    tile_count,
    base_stress,
    prev_rate,
    direct_effect,
    state_var,
):
    gathered = lax.all_gather(history, "row", axis=3, tiled=True)
    lag_local = gathered.shape[0]
    sims_count = gathered.shape[2]
    tile_side = kernel_tiles.shape[4]
    slots = kernel_tiles.shape[3]
    col_blocks = gathered.shape[3] // tile_side
    blocks = gathered.reshape(lag_local, sims_count, col_blocks, tile_side)
    choose = jax.nn.one_hot(tile_cols[0, 0], col_blocks, dtype=jnp.bfloat16)
    picked = jnp.einsum(
        "lkb,lsbj->lksj", choose, blocks, preferred_element_type=jnp.float32
    ).astype(jnp.bfloat16)
    contrib = jnp.einsum(
        "lksj,lkij->lksi", picked, kernel_tiles[0, 0], preferred_element_type=jnp.float32
    )
    row_blocks = n_col * n_lag
    alive_mask = (jnp.arange(slots)[None, :] < tile_count[0, 0][:, None]).astype(jnp.float32)
    masked = (contrib * alive_mask[:, :, None, None]).reshape(
        lag_local * slots, sims_count, tile_side
    )
    targets = tile_rows[0, 0].reshape(lag_local * slots)
    placed = (
        jnp.zeros((row_blocks, sims_count, tile_side), jnp.float32).at[targets].add(masked)
    )
    by_chip = placed.reshape(n_col, n_lag, sims_count, tile_side)
    lag = lax.axis_index("lag")
    own = lax.dynamic_index_in_dim(by_chip, lag, axis=1, keepdims=False)
    other = lax.dynamic_index_in_dim(by_chip, n_lag - 1 - lag, axis=1, keepdims=False)
    from_partner = lax.ppermute(other, "lag", perm=[(0, 1), (1, 0)])
    stress_change = reduce_scatter(own + from_partner, n_col)
    driving = base_stress + stress_change
    factor = jnp.exp(state_var) / 2.0
    velocity = prev_rate
    for step in range(NEWTON):
        scaled = velocity * factor
        misfit = direct_effect * inverse_sinh(scaled) + 0.5 * velocity - driving
        slope = direct_effect * factor / jnp.sqrt(1.0 + scaled * scaled) + 0.5
        velocity = velocity - misfit / slope
    return (stress_change, velocity)


def solution(mesh):
    return jax.shard_map(
        functools.partial(local, mesh.shape["col"], mesh.shape["lag"]),
        mesh=mesh,
        in_specs=(
            P("lag", "col", None, "row"),
            P("row", "col", "lag", None, None, None),
            P("row", "col", "lag", None),
            P("row", "col", "lag", None),
            P("row", "col", "lag"),
            P(None, ("row", "col", "lag")),
            P(None, ("row", "col", "lag")),
            P(None, ("row", "col", "lag")),
            P(None, ("row", "col", "lag")),
        ),
        out_specs=(P(None, ("row", "col", "lag")), P(None, ("row", "col", "lag"))),
        check_vma=False,
    )
```

```python
import functools

import jax
import jax.numpy as jnp
from jax import lax
from jax.experimental import pallas as pl
from jax.experimental.pallas import tpu as pltpu
from jax.sharding import PartitionSpec as P

NEWTON = 4
MESH = pl.DeviceIdType.MESH


def inverse_sinh(value):
    magnitude = jnp.abs(value)
    return jnp.sign(value) * jnp.log(magnitude + jnp.sqrt(1.0 + magnitude * magnitude))


def scatter_kernel(n_col, part_ref, out_ref, slots, send_sem, recv_sem):
    row = lax.axis_index("row")
    me = lax.axis_index("col")
    lag = lax.axis_index("lag")

    def peer(t):
        return (row, t, lag)

    barrier = pltpu.get_barrier_semaphore()
    for d in range(1, n_col):
        t = lax.rem(me + d, n_col)
        pl.semaphore_signal(barrier, inc=1, device_id=peer(t), device_id_type=MESH)
    pl.semaphore_wait(barrier, n_col - 1)

    sends = []
    for d in range(1, n_col):
        t = lax.rem(me + d, n_col)
        copy = pltpu.make_async_remote_copy(
            src_ref=part_ref.at[t],
            dst_ref=slots.at[me],
            send_sem=send_sem.at[t],
            recv_sem=recv_sem.at[me],
            device_id=peer(t),
            device_id_type=MESH,
        )
        copy.start()
        sends.append(copy)

    total = part_ref[me]
    for d in range(1, n_col):
        s = lax.rem(me + n_col - d, n_col)
        incoming = pltpu.make_async_remote_copy(
            src_ref=part_ref.at[s],
            dst_ref=slots.at[s],
            send_sem=send_sem.at[s],
            recv_sem=recv_sem.at[s],
            device_id=peer(s),
            device_id_type=MESH,
        )
        incoming.wait_recv()
        total = total + slots[s]
    out_ref[...] = total
    for copy in sends:
        copy.wait_send()


def reduce_scatter(part, n_col):
    group, sims, tile = part.shape
    return pl.pallas_call(
        functools.partial(scatter_kernel, n_col),
        out_shape=jax.ShapeDtypeStruct((sims, tile), jnp.float32),
        in_specs=[pl.BlockSpec(memory_space=pltpu.VMEM)],
        out_specs=pl.BlockSpec(memory_space=pltpu.VMEM),
        scratch_shapes=[
            pltpu.VMEM((group, sims, tile), jnp.float32),
            pltpu.SemaphoreType.DMA((group,)),
            pltpu.SemaphoreType.DMA((group,)),
        ],
        compiler_params=pltpu.CompilerParams(
            collective_id=0, has_side_effects=True, vmem_limit_bytes=48 * 1024 * 1024
        ),
    )(part)


def parts_kernel(n_lag, rows_ref, cols_ref, count_ref, lag_ref, hist_ref, tiles_ref, out_ref):
    lag = pl.program_id(0)
    slots = tiles_ref.shape[1]
    side = tiles_ref.shape[2]

    @pl.when(lag == 0)
    def _():
        out_ref[...] = jnp.zeros_like(out_ref)

    for k in range(slots):
        @pl.when(k < count_ref[lag])
        def _():
            col = cols_ref[lag * slots + k]
            row = rows_ref[lag * slots + k]
            start = pl.multiple_of(col * side, side)
            history = hist_ref[0, :, pl.ds(start, side)]
            contrib = lax.dot_general(
                history, tiles_ref[0, k], (((1,), (1,)), ((), ())),
                preferred_element_type=jnp.float32,
            )
            half = jnp.where(row % n_lag == lag_ref[0], 0, 1)
            out_ref[half, row // n_lag] += contrib


def stress_parts(history, tiles, rows, cols, count, n_col, n_lag):
    lags, sims, sources = history.shape
    _, slots, side, _ = tiles.shape
    lag = lax.axis_index("lag").astype(jnp.int32).reshape(1)
    grid_spec = pltpu.PrefetchScalarGridSpec(
        num_scalar_prefetch=4,
        grid=(lags,),
        in_specs=[
            pl.BlockSpec((1, sims, sources), lambda l, *_: (l, 0, 0)),
            pl.BlockSpec((1, slots, side, side), lambda l, *_: (l, 0, 0, 0)),
        ],
        out_specs=pl.BlockSpec((2, n_col, sims, side), lambda l, *_: (0, 0, 0, 0)),
    )
    return pl.pallas_call(
        functools.partial(parts_kernel, n_lag),
        out_shape=jax.ShapeDtypeStruct((2, n_col, sims, side), jnp.float32),
        grid_spec=grid_spec,
        compiler_params=pltpu.CompilerParams(vmem_limit_bytes=48 * 1024 * 1024),
    )(rows.reshape(-1), cols.reshape(-1), count, lag, history, tiles)


def local(
    n_col,
    n_lag,
    history,
    kernel_tiles,
    tile_rows,
    tile_cols,
    tile_count,
    base_stress,
    prev_rate,
    direct_effect,
    state_var,
):
    gathered = lax.all_gather(history, "row", axis=3, tiled=True)
    tile_side = kernel_tiles.shape[4]
    parts = stress_parts(gathered[:, 0], kernel_tiles[0, 0], tile_rows[0, 0],
                         tile_cols[0, 0], tile_count[0, 0], n_col, n_lag)
    own, other = parts[0], parts[1]
    from_partner = lax.ppermute(other, "lag", perm=[(0, 1), (1, 0)])
    stress_change = reduce_scatter(own + from_partner, n_col)
    driving = base_stress + stress_change
    factor = jnp.exp(state_var) / 2.0
    velocity = prev_rate
    for step in range(NEWTON):
        scaled = velocity * factor
        misfit = direct_effect * inverse_sinh(scaled) + 0.5 * velocity - driving
        slope = direct_effect * factor / jnp.sqrt(1.0 + scaled * scaled) + 0.5
        velocity = velocity - misfit / slope
    return (stress_change, velocity)


def solution(mesh):
    return jax.shard_map(
        functools.partial(local, mesh.shape["col"], mesh.shape["lag"]),
        mesh=mesh,
        in_specs=(
            P("lag", "col", None, "row"),
            P("row", "col", "lag", None, None, None),
            P("row", "col", "lag", None),
            P("row", "col", "lag", None),
            P("row", "col", "lag"),
            P(None, ("row", "col", "lag")),
            P(None, ("row", "col", "lag")),
            P(None, ("row", "col", "lag")),
            P(None, ("row", "col", "lag")),
        ),
        out_specs=(P(None, ("row", "col", "lag")), P(None, ("row", "col", "lag"))),
        check_vma=False,
    )
```

```python
import functools

import jax
import jax.numpy as jnp
from jax import lax
from jax.experimental import pallas as pl
from jax.experimental.pallas import tpu as pltpu
from jax.sharding import PartitionSpec as P

NEWTON = 4
MESH = pl.DeviceIdType.MESH


def inverse_sinh(value):
    magnitude = jnp.abs(value)
    return jnp.sign(value) * jnp.log(magnitude + jnp.sqrt(1.0 + magnitude * magnitude))


def scatter_kernel(n_col, part_ref, out_ref, slots, send_sem, recv_sem):
    row = lax.axis_index("row")
    me = lax.axis_index("col")
    lag = lax.axis_index("lag")

    def peer(t):
        return (row, t, lag)

    barrier = pltpu.get_barrier_semaphore()
    for d in range(1, n_col):
        t = lax.rem(me + d, n_col)
        pl.semaphore_signal(barrier, inc=1, device_id=peer(t), device_id_type=MESH)
    pl.semaphore_wait(barrier, n_col - 1)

    sends = []
    for d in range(1, n_col):
        t = lax.rem(me + d, n_col)
        copy = pltpu.make_async_remote_copy(
            src_ref=part_ref.at[t],
            dst_ref=slots.at[me],
            send_sem=send_sem.at[t],
            recv_sem=recv_sem.at[me],
            device_id=peer(t),
            device_id_type=MESH,
        )
        copy.start()
        sends.append(copy)

    total = part_ref[me]
    for d in range(1, n_col):
        s = lax.rem(me + n_col - d, n_col)
        incoming = pltpu.make_async_remote_copy(
            src_ref=part_ref.at[s],
            dst_ref=slots.at[s],
            send_sem=send_sem.at[s],
            recv_sem=recv_sem.at[s],
            device_id=peer(s),
            device_id_type=MESH,
        )
        incoming.wait_recv()
        total = total + slots[s]
    out_ref[...] = total
    for copy in sends:
        copy.wait_send()


def reduce_scatter(part, n_col, collective_id):
    group, sims, tile = part.shape
    return pl.pallas_call(
        functools.partial(scatter_kernel, n_col),
        out_shape=jax.ShapeDtypeStruct((sims, tile), jnp.float32),
        in_specs=[pl.BlockSpec(memory_space=pltpu.VMEM)],
        out_specs=pl.BlockSpec(memory_space=pltpu.VMEM),
        scratch_shapes=[
            pltpu.VMEM((group, sims, tile), jnp.float32),
            pltpu.SemaphoreType.DMA((group,)),
            pltpu.SemaphoreType.DMA((group,)),
        ],
        compiler_params=pltpu.CompilerParams(
            collective_id=collective_id, has_side_effects=True, vmem_limit_bytes=48 * 1024 * 1024
        ),
    )(part)


def parts_kernel(n_lag, rows_ref, cols_ref, count_ref, lag_ref, hist_ref, tiles_ref, *rest):
    out_ref = rest[-1]
    lag = pl.program_id(0)
    slots = tiles_ref.shape[1]
    side = tiles_ref.shape[2]

    @pl.when(lag == 0)
    def _():
        out_ref[...] = jnp.zeros_like(out_ref)

    for k in range(slots):
        @pl.when(k < count_ref[lag])
        def _():
            col = cols_ref[lag * slots + k]
            row = rows_ref[lag * slots + k]
            start = pl.multiple_of(col * side, side)
            history = hist_ref[0, :, pl.ds(start, side)]
            contrib = lax.dot_general(
                history, tiles_ref[0, k], (((1,), (1,)), ((), ())),
                preferred_element_type=jnp.float32,
            )
            half = jnp.where(row % n_lag == lag_ref[0], 0, 1)
            out_ref[half, row // n_lag] += contrib


def stress_parts(history, tiles, rows, cols, count, n_col, n_lag, after=()):
    lags, sims, sources = history.shape
    _, slots, side, _ = tiles.shape
    lag = lax.axis_index("lag").astype(jnp.int32).reshape(1)
    grid_spec = pltpu.PrefetchScalarGridSpec(
        num_scalar_prefetch=4,
        grid=(lags,),
        in_specs=[
            pl.BlockSpec((1, sims, sources), lambda l, *_: (l, 0, 0)),
            pl.BlockSpec((1, slots, side, side), lambda l, *_: (l, 0, 0, 0)),
        ] + [pl.BlockSpec(memory_space=pl.ANY) for _ in after],
        out_specs=pl.BlockSpec((2, n_col, sims, side), lambda l, *_: (0, 0, 0, 0)),
    )
    return pl.pallas_call(
        functools.partial(parts_kernel, n_lag),
        out_shape=jax.ShapeDtypeStruct((2, n_col, sims, side), jnp.float32),
        grid_spec=grid_spec,
        compiler_params=pltpu.CompilerParams(vmem_limit_bytes=48 * 1024 * 1024),
    )(rows.reshape(-1), cols.reshape(-1), count, lag, history, tiles, *after)


def local(
    n_col,
    n_lag,
    history,
    kernel_tiles,
    tile_rows,
    tile_cols,
    tile_count,
    base_stress,
    prev_rate,
    direct_effect,
    state_var,
):
    n_chunks = 2
    chunk = history.shape[2] // n_chunks
    pieces = []
    for index in range(n_chunks):
        sims = slice(index * chunk, (index + 1) * chunk)
        gathered = lax.all_gather(history[:, :, sims], "row", axis=3, tiled=True)
        parts = stress_parts(gathered[:, 0], kernel_tiles[0, 0], tile_rows[0, 0],
                             tile_cols[0, 0], tile_count[0, 0], n_col, n_lag,
                             after=tuple(pieces[-1:]))
        from_partner = lax.ppermute(parts[1], "lag", perm=[(0, 1), (1, 0)])
        pieces.append(reduce_scatter(parts[0] + from_partner, n_col, index))
    stress_change = jnp.concatenate(pieces, axis=0)
    driving = base_stress + stress_change
    factor = jnp.exp(state_var) / 2.0
    velocity = prev_rate
    for step in range(NEWTON):
        scaled = velocity * factor
        misfit = direct_effect * inverse_sinh(scaled) + 0.5 * velocity - driving
        slope = direct_effect * factor / jnp.sqrt(1.0 + scaled * scaled) + 0.5
        velocity = velocity - misfit / slope
    return (stress_change, velocity)


def solution(mesh):
    return jax.shard_map(
        functools.partial(local, mesh.shape["col"], mesh.shape["lag"]),
        mesh=mesh,
        in_specs=(
            P("lag", "col", None, "row"),
            P("row", "col", "lag", None, None, None),
            P("row", "col", "lag", None),
            P("row", "col", "lag", None),
            P("row", "col", "lag"),
            P(None, ("row", "col", "lag")),
            P(None, ("row", "col", "lag")),
            P(None, ("row", "col", "lag")),
            P(None, ("row", "col", "lag")),
        ),
        out_specs=(P(None, ("row", "col", "lag")), P(None, ("row", "col", "lag"))),
        check_vma=False,
    )
```

```python
import functools

import jax
import jax.numpy as jnp
from jax import lax
from jax.experimental import pallas as pl
from jax.experimental.pallas import tpu as pltpu
from jax.sharding import PartitionSpec as P

NEWTON = 4
MESH = pl.DeviceIdType.MESH


def inverse_sinh(value):
    magnitude = jnp.abs(value)
    return jnp.sign(value) * jnp.log(magnitude + jnp.sqrt(1.0 + magnitude * magnitude))


def ring_kernel(n_z, part_ref, out_ref, recv, forward, final, cross,
                send_sem, recv_sem, cross_sem):
    row = lax.axis_index("row")
    col = lax.axis_index("col")
    lag = lax.axis_index("lag")
    z = col // 2
    y_hi = col % 2
    up = lax.rem(z + 1, n_z)
    down = lax.rem(z + n_z - 1, n_z)

    def device(zz, yy):
        return (row, zz * 2 + yy, lag)

    barrier = pltpu.get_barrier_semaphore()
    for peer in (device(up, y_hi), device(down, y_hi), device(z, 1 - y_hi)):
        pl.semaphore_signal(barrier, inc=1, device_id=peer, device_id_type=MESH)
    pl.semaphore_wait(barrier, 3)

    steps = n_z - 1
    copies = [[], []]
    for step in range(steps):
        for way in range(2):
            if way == 0:
                target = lax.rem(z + n_z - 1 - step, n_z)
                dest = device(up, y_hi)
            else:
                target = lax.rem(z + 1 + step, n_z)
                dest = device(down, y_hi)
            block = target * 2 + way
            if step == 0:
                source = part_ref.at[block]
            else:
                copies[way][step - 1].wait_recv()
                forward[way, step] = recv[way, step - 1] + part_ref[block]
                source = forward.at[way, step]
            copy = pltpu.make_async_remote_copy(
                src_ref=source,
                dst_ref=recv.at[way, step],
                send_sem=send_sem.at[way, step],
                recv_sem=recv_sem.at[way, step],
                device_id=dest,
                device_id_type=MESH,
            )
            copy.start()
            copies[way].append(copy)

    for way in range(2):
        copies[way][steps - 1].wait_recv()
        final[way] = recv[way, steps - 1] + part_ref[z * 2 + way]
    handoff = pltpu.make_async_remote_copy(
        src_ref=final.at[1 - y_hi],
        dst_ref=cross,
        send_sem=cross_sem.at[0],
        recv_sem=cross_sem.at[1],
        device_id=device(z, 1 - y_hi),
        device_id_type=MESH,
    )
    handoff.start()
    handoff.wait_recv()
    out_ref[...] = final[y_hi] + cross[...]
    handoff.wait_send()
    for way in range(2):
        for copy in copies[way]:
            copy.wait_send()


def reduce_scatter(part, n_col):
    group, sims, tile = part.shape
    n_z = n_col // 2
    steps = n_z - 1
    return pl.pallas_call(
        functools.partial(ring_kernel, n_z),
        out_shape=jax.ShapeDtypeStruct((sims, tile), jnp.float32),
        in_specs=[pl.BlockSpec(memory_space=pltpu.VMEM)],
        out_specs=pl.BlockSpec(memory_space=pltpu.VMEM),
        scratch_shapes=[
            pltpu.VMEM((2, steps, sims, tile), jnp.float32),
            pltpu.VMEM((2, steps, sims, tile), jnp.float32),
            pltpu.VMEM((2, sims, tile), jnp.float32),
            pltpu.VMEM((sims, tile), jnp.float32),
            pltpu.SemaphoreType.DMA((2, steps)),
            pltpu.SemaphoreType.DMA((2, steps)),
            pltpu.SemaphoreType.DMA((2,)),
        ],
        compiler_params=pltpu.CompilerParams(
            collective_id=0, has_side_effects=True, vmem_limit_bytes=48 * 1024 * 1024
        ),
    )(part)


def parts_kernel(n_lag, rows_ref, cols_ref, count_ref, lag_ref, hist_ref, tiles_ref, out_ref):
    lag = pl.program_id(0)
    slots = tiles_ref.shape[1]
    side = tiles_ref.shape[2]

    @pl.when(lag == 0)
    def _():
        out_ref[...] = jnp.zeros_like(out_ref)

    for k in range(slots):
        @pl.when(k < count_ref[lag])
        def _():
            col = cols_ref[lag * slots + k]
            row = rows_ref[lag * slots + k]
            start = pl.multiple_of(col * side, side)
            history = hist_ref[0, :, pl.ds(start, side)]
            contrib = lax.dot_general(
                history, tiles_ref[0, k], (((1,), (1,)), ((), ())),
                preferred_element_type=jnp.float32,
            )
            half = jnp.where(row % n_lag == lag_ref[0], 0, 1)
            out_ref[half, row // n_lag] += contrib


def stress_parts(history, tiles, rows, cols, count, n_col, n_lag):
    lags, sims, sources = history.shape
    _, slots, side, _ = tiles.shape
    lag = lax.axis_index("lag").astype(jnp.int32).reshape(1)
    grid_spec = pltpu.PrefetchScalarGridSpec(
        num_scalar_prefetch=4,
        grid=(lags,),
        in_specs=[
            pl.BlockSpec((1, sims, sources), lambda l, *_: (l, 0, 0)),
            pl.BlockSpec((1, slots, side, side), lambda l, *_: (l, 0, 0, 0)),
        ],
        out_specs=pl.BlockSpec((2, n_col, sims, side), lambda l, *_: (0, 0, 0, 0)),
    )
    return pl.pallas_call(
        functools.partial(parts_kernel, n_lag),
        out_shape=jax.ShapeDtypeStruct((2, n_col, sims, side), jnp.float32),
        grid_spec=grid_spec,
        compiler_params=pltpu.CompilerParams(vmem_limit_bytes=48 * 1024 * 1024),
    )(rows.reshape(-1), cols.reshape(-1), count, lag, history, tiles)


def local(
    n_col,
    n_lag,
    history,
    kernel_tiles,
    tile_rows,
    tile_cols,
    tile_count,
    base_stress,
    prev_rate,
    direct_effect,
    state_var,
):
    gathered = lax.all_gather(history, "row", axis=3, tiled=True)
    tile_side = kernel_tiles.shape[4]
    parts = stress_parts(gathered[:, 0], kernel_tiles[0, 0], tile_rows[0, 0],
                         tile_cols[0, 0], tile_count[0, 0], n_col, n_lag)
    own, other = parts[0], parts[1]
    from_partner = lax.ppermute(other, "lag", perm=[(0, 1), (1, 0)])
    stress_change = reduce_scatter(own + from_partner, n_col)
    driving = base_stress + stress_change
    factor = jnp.exp(state_var) / 2.0
    velocity = prev_rate
    for step in range(NEWTON):
        scaled = velocity * factor
        misfit = direct_effect * inverse_sinh(scaled) + 0.5 * velocity - driving
        slope = direct_effect * factor / jnp.sqrt(1.0 + scaled * scaled) + 0.5
        velocity = velocity - misfit / slope
    return (stress_change, velocity)


def solution(mesh):
    return jax.shard_map(
        functools.partial(local, mesh.shape["col"], mesh.shape["lag"]),
        mesh=mesh,
        in_specs=(
            P("lag", "col", None, "row"),
            P("row", "col", "lag", None, None, None),
            P("row", "col", "lag", None),
            P("row", "col", "lag", None),
            P("row", "col", "lag"),
            P(None, ("row", "col", "lag")),
            P(None, ("row", "col", "lag")),
            P(None, ("row", "col", "lag")),
            P(None, ("row", "col", "lag")),
        ),
        out_specs=(P(None, ("row", "col", "lag")), P(None, ("row", "col", "lag"))),
        check_vma=False,
    )
```

```python
import functools

import jax
import jax.numpy as jnp
from jax import lax
from jax.experimental import pallas as pl
from jax.experimental.pallas import tpu as pltpu
from jax.sharding import PartitionSpec as P

NEWTON = 4
MESH = pl.DeviceIdType.MESH


def inverse_sinh(value):
    magnitude = jnp.abs(value)
    return jnp.sign(value) * jnp.log(magnitude + jnp.sqrt(1.0 + magnitude * magnitude))


def ring_kernel(n_z, part_ref, out_ref, recv, forward, final, cross,
                send_sem, recv_sem, cross_sem):
    row = lax.axis_index("row")
    col = lax.axis_index("col")
    lag = lax.axis_index("lag")
    z = col // 2
    y_hi = col % 2
    up = lax.rem(z + 1, n_z)
    down = lax.rem(z + n_z - 1, n_z)

    def device(zz, yy):
        return (row, zz * 2 + yy, lag)

    barrier = pltpu.get_barrier_semaphore()
    for peer in (device(up, y_hi), device(down, y_hi), device(z, 1 - y_hi)):
        pl.semaphore_signal(barrier, inc=1, device_id=peer, device_id_type=MESH)
    pl.semaphore_wait(barrier, 3)

    steps = n_z - 1
    copies = [[], []]
    for step in range(steps):
        for way in range(2):
            if way == 0:
                target = lax.rem(z + n_z - 1 - step, n_z)
                dest = device(up, y_hi)
            else:
                target = lax.rem(z + 1 + step, n_z)
                dest = device(down, y_hi)
            block = target * 2 + way
            if step == 0:
                source = part_ref.at[block]
            else:
                copies[way][step - 1].wait_recv()
                forward[way, step] = recv[way, step - 1] + part_ref[block]
                source = forward.at[way, step]
            copy = pltpu.make_async_remote_copy(
                src_ref=source,
                dst_ref=recv.at[way, step],
                send_sem=send_sem.at[way, step],
                recv_sem=recv_sem.at[way, step],
                device_id=dest,
                device_id_type=MESH,
            )
            copy.start()
            copies[way].append(copy)

    for way in range(2):
        copies[way][steps - 1].wait_recv()
        final[way] = recv[way, steps - 1] + part_ref[z * 2 + way]
    handoff = pltpu.make_async_remote_copy(
        src_ref=final.at[1 - y_hi],
        dst_ref=cross,
        send_sem=cross_sem.at[0],
        recv_sem=cross_sem.at[1],
        device_id=device(z, 1 - y_hi),
        device_id_type=MESH,
    )
    handoff.start()
    handoff.wait_recv()
    out_ref[...] = final[y_hi] + cross[...]
    handoff.wait_send()
    for way in range(2):
        for copy in copies[way]:
            copy.wait_send()


def reduce_scatter(part, n_col):
    group, sims, tile = part.shape
    n_z = n_col // 2
    steps = n_z - 1
    return pl.pallas_call(
        functools.partial(ring_kernel, n_z),
        out_shape=jax.ShapeDtypeStruct((sims, tile), jnp.float32),
        in_specs=[pl.BlockSpec(memory_space=pltpu.VMEM)],
        out_specs=pl.BlockSpec(memory_space=pltpu.VMEM),
        scratch_shapes=[
            pltpu.VMEM((2, steps, sims, tile), jnp.float32),
            pltpu.VMEM((2, steps, sims, tile), jnp.float32),
            pltpu.VMEM((2, sims, tile), jnp.float32),
            pltpu.VMEM((sims, tile), jnp.float32),
            pltpu.SemaphoreType.DMA((2, steps)),
            pltpu.SemaphoreType.DMA((2, steps)),
            pltpu.SemaphoreType.DMA((2,)),
        ],
        compiler_params=pltpu.CompilerParams(
            collective_id=0, has_side_effects=True, vmem_limit_bytes=48 * 1024 * 1024
        ),
    )(part)


def parts_kernel(n_lag, rows_ref, cols_ref, count_ref, lag_ref, hist_ref, tiles_ref, out_ref):
    lag = pl.program_id(0)
    slots = tiles_ref.shape[1]
    side = tiles_ref.shape[2]

    @pl.when(lag == 0)
    def _():
        out_ref[...] = jnp.zeros_like(out_ref)

    for k in range(slots):
        @pl.when(k < count_ref[lag])
        def _():
            col = cols_ref[lag * slots + k]
            row = rows_ref[lag * slots + k]
            history = hist_ref[0, col]
            contrib = lax.dot_general(
                history, tiles_ref[0, k], (((1,), (1,)), ((), ())),
                preferred_element_type=jnp.float32,
            )
            half = jnp.where(row % n_lag == lag_ref[0], 0, 1)
            out_ref[half, row // n_lag] += contrib


def stress_parts(history, tiles, rows, cols, count, n_col, n_lag):
    lags, n_blocks, sims, _ = history.shape
    _, slots, side, _ = tiles.shape
    lag = lax.axis_index("lag").astype(jnp.int32).reshape(1)
    grid_spec = pltpu.PrefetchScalarGridSpec(
        num_scalar_prefetch=4,
        grid=(lags,),
        in_specs=[
            pl.BlockSpec((1, n_blocks, sims, side), lambda l, *_: (l, 0, 0, 0)),
            pl.BlockSpec((1, slots, side, side), lambda l, *_: (l, 0, 0, 0)),
        ],
        out_specs=pl.BlockSpec((2, n_col, sims, side), lambda l, *_: (0, 0, 0, 0)),
    )
    return pl.pallas_call(
        functools.partial(parts_kernel, n_lag),
        out_shape=jax.ShapeDtypeStruct((2, n_col, sims, side), jnp.float32),
        grid_spec=grid_spec,
        compiler_params=pltpu.CompilerParams(vmem_limit_bytes=48 * 1024 * 1024),
    )(rows.reshape(-1), cols.reshape(-1), count, lag, history, tiles)


def local(
    n_col,
    n_lag,
    history,
    kernel_tiles,
    tile_rows,
    tile_cols,
    tile_count,
    base_stress,
    prev_rate,
    direct_effect,
    state_var,
):
    tile_side = kernel_tiles.shape[4]
    lag_local, _, sims_count, held = history.shape
    blocks = history.reshape(lag_local, sims_count, held // tile_side, tile_side)
    blocks = jnp.transpose(blocks, (0, 2, 1, 3))
    gathered = lax.all_gather(blocks, "row", axis=1, tiled=True)
    parts = stress_parts(gathered, kernel_tiles[0, 0], tile_rows[0, 0],
                         tile_cols[0, 0], tile_count[0, 0], n_col, n_lag)
    own, other = parts[0], parts[1]
    from_partner = lax.ppermute(other, "lag", perm=[(0, 1), (1, 0)])
    stress_change = reduce_scatter(own + from_partner, n_col)
    driving = base_stress + stress_change
    factor = jnp.exp(state_var) / 2.0
    velocity = prev_rate
    for step in range(NEWTON):
        scaled = velocity * factor
        misfit = direct_effect * inverse_sinh(scaled) + 0.5 * velocity - driving
        slope = direct_effect * factor / jnp.sqrt(1.0 + scaled * scaled) + 0.5
        velocity = velocity - misfit / slope
    return (stress_change, velocity)


def solution(mesh):
    return jax.shard_map(
        functools.partial(local, mesh.shape["col"], mesh.shape["lag"]),
        mesh=mesh,
        in_specs=(
            P("lag", "col", None, "row"),
            P("row", "col", "lag", None, None, None),
            P("row", "col", "lag", None),
            P("row", "col", "lag", None),
            P("row", "col", "lag"),
            P(None, ("row", "col", "lag")),
            P(None, ("row", "col", "lag")),
            P(None, ("row", "col", "lag")),
            P(None, ("row", "col", "lag")),
        ),
        out_specs=(P(None, ("row", "col", "lag")), P(None, ("row", "col", "lag"))),
        check_vma=False,
    )
```

```python
import functools

import jax
import jax.numpy as jnp
from jax import lax
from jax.experimental import pallas as pl
from jax.experimental.pallas import tpu as pltpu
from jax.sharding import PartitionSpec as P

NEWTON = 4
MESH = pl.DeviceIdType.MESH


def inverse_sinh(value):
    magnitude = jnp.abs(value)
    return jnp.sign(value) * jnp.log(magnitude + jnp.sqrt(1.0 + magnitude * magnitude))


def ring_kernel(n_z, n_pieces, part_ref, out_ref, recv, forward, final, cross,
                send_sem, recv_sem, cross_sem):
    row = lax.axis_index("row")
    col = lax.axis_index("col")
    lag = lax.axis_index("lag")
    z = col // 2
    y_hi = col % 2
    up = lax.rem(z + 1, n_z)
    down = lax.rem(z + n_z - 1, n_z)
    rows = part_ref.shape[1] // n_pieces

    def device(zz, yy):
        return (row, zz * 2 + yy, lag)

    barrier = pltpu.get_barrier_semaphore()
    for peer in (device(up, y_hi), device(down, y_hi), device(z, 1 - y_hi)):
        pl.semaphore_signal(barrier, inc=1, device_id=peer, device_id_type=MESH)
    pl.semaphore_wait(barrier, 3)

    steps = n_z - 1
    copies = {}
    for step in range(steps):
        for piece in range(n_pieces):
            span = pl.ds(piece * rows, rows)
            for way in range(2):
                if way == 0:
                    target = lax.rem(z + n_z - 1 - step, n_z)
                    dest = device(up, y_hi)
                else:
                    target = lax.rem(z + 1 + step, n_z)
                    dest = device(down, y_hi)
                block = target * 2 + way
                if step == 0:
                    source = part_ref.at[block, span]
                else:
                    copies[way, step - 1, piece].wait_recv()
                    forward[way, step, piece] = (
                        recv[way, step - 1, piece] + part_ref[block, span]
                    )
                    source = forward.at[way, step, piece]
                copy = pltpu.make_async_remote_copy(
                    src_ref=source,
                    dst_ref=recv.at[way, step, piece],
                    send_sem=send_sem.at[way, step, piece],
                    recv_sem=recv_sem.at[way, step, piece],
                    device_id=dest,
                    device_id_type=MESH,
                )
                copy.start()
                copies[way, step, piece] = copy

    handoffs = []
    for piece in range(n_pieces):
        span = pl.ds(piece * rows, rows)
        for way in range(2):
            copies[way, steps - 1, piece].wait_recv()
            final[way, piece] = recv[way, steps - 1, piece] + part_ref[z * 2 + way, span]
        handoff = pltpu.make_async_remote_copy(
            src_ref=final.at[1 - y_hi, piece],
            dst_ref=cross.at[piece],
            send_sem=cross_sem.at[0, piece],
            recv_sem=cross_sem.at[1, piece],
            device_id=device(z, 1 - y_hi),
            device_id_type=MESH,
        )
        handoff.start()
        handoffs.append(handoff)
    for piece in range(n_pieces):
        handoffs[piece].wait_recv()
        out_ref[pl.ds(piece * rows, rows), :] = final[y_hi, piece] + cross[piece]
    for handoff in handoffs:
        handoff.wait_send()
    for copy in copies.values():
        copy.wait_send()


def reduce_scatter(part, n_col, n_pieces=2):
    group, sims, tile = part.shape
    n_z = n_col // 2
    steps = n_z - 1
    rows = sims // n_pieces
    return pl.pallas_call(
        functools.partial(ring_kernel, n_z, n_pieces),
        out_shape=jax.ShapeDtypeStruct((sims, tile), jnp.float32),
        in_specs=[pl.BlockSpec(memory_space=pltpu.VMEM)],
        out_specs=pl.BlockSpec(memory_space=pltpu.VMEM),
        scratch_shapes=[
            pltpu.VMEM((2, steps, n_pieces, rows, tile), jnp.float32),
            pltpu.VMEM((2, steps, n_pieces, rows, tile), jnp.float32),
            pltpu.VMEM((2, n_pieces, rows, tile), jnp.float32),
            pltpu.VMEM((n_pieces, rows, tile), jnp.float32),
            pltpu.SemaphoreType.DMA((2, steps, n_pieces)),
            pltpu.SemaphoreType.DMA((2, steps, n_pieces)),
            pltpu.SemaphoreType.DMA((2, n_pieces)),
        ],
        compiler_params=pltpu.CompilerParams(
            collective_id=0, has_side_effects=True, vmem_limit_bytes=48 * 1024 * 1024
        ),
    )(part)


def parts_kernel(n_lag, rows_ref, cols_ref, count_ref, lag_ref, hist_ref, tiles_ref, out_ref):
    lag = pl.program_id(0)
    slots = tiles_ref.shape[1]
    side = tiles_ref.shape[2]

    @pl.when(lag == 0)
    def _():
        out_ref[...] = jnp.zeros_like(out_ref)

    for k in range(slots):
        @pl.when(k < count_ref[lag])
        def _():
            col = cols_ref[lag * slots + k]
            row = rows_ref[lag * slots + k]
            start = pl.multiple_of(col * side, side)
            history = hist_ref[0, :, pl.ds(start, side)]
            contrib = lax.dot_general(
                history, tiles_ref[0, k], (((1,), (1,)), ((), ())),
                preferred_element_type=jnp.float32,
            )
            half = jnp.where(row % n_lag == lag_ref[0], 0, 1)
            out_ref[half, row // n_lag] += contrib


def stress_parts(history, tiles, rows, cols, count, n_col, n_lag):
    lags, sims, sources = history.shape
    _, slots, side, _ = tiles.shape
    lag = lax.axis_index("lag").astype(jnp.int32).reshape(1)
    grid_spec = pltpu.PrefetchScalarGridSpec(
        num_scalar_prefetch=4,
        grid=(lags,),
        in_specs=[
            pl.BlockSpec((1, sims, sources), lambda l, *_: (l, 0, 0)),
            pl.BlockSpec((1, slots, side, side), lambda l, *_: (l, 0, 0, 0)),
        ],
        out_specs=pl.BlockSpec((2, n_col, sims, side), lambda l, *_: (0, 0, 0, 0)),
    )
    return pl.pallas_call(
        functools.partial(parts_kernel, n_lag),
        out_shape=jax.ShapeDtypeStruct((2, n_col, sims, side), jnp.float32),
        grid_spec=grid_spec,
        compiler_params=pltpu.CompilerParams(vmem_limit_bytes=48 * 1024 * 1024),
    )(rows.reshape(-1), cols.reshape(-1), count, lag, history, tiles)


def local(
    n_col,
    n_lag,
    history,
    kernel_tiles,
    tile_rows,
    tile_cols,
    tile_count,
    base_stress,
    prev_rate,
    direct_effect,
    state_var,
):
    gathered = lax.all_gather(history, "row", axis=3, tiled=True)
    tile_side = kernel_tiles.shape[4]
    parts = stress_parts(gathered[:, 0], kernel_tiles[0, 0], tile_rows[0, 0],
                         tile_cols[0, 0], tile_count[0, 0], n_col, n_lag)
    own, other = parts[0], parts[1]
    from_partner = lax.ppermute(other, "lag", perm=[(0, 1), (1, 0)])
    stress_change = reduce_scatter(own + from_partner, n_col)
    driving = base_stress + stress_change
    factor = jnp.exp(state_var) / 2.0
    velocity = prev_rate
    for step in range(NEWTON):
        scaled = velocity * factor
        misfit = direct_effect * inverse_sinh(scaled) + 0.5 * velocity - driving
        slope = direct_effect * factor / jnp.sqrt(1.0 + scaled * scaled) + 0.5
        velocity = velocity - misfit / slope
    return (stress_change, velocity)


def solution(mesh):
    return jax.shard_map(
        functools.partial(local, mesh.shape["col"], mesh.shape["lag"]),
        mesh=mesh,
        in_specs=(
            P("lag", "col", None, "row"),
            P("row", "col", "lag", None, None, None),
            P("row", "col", "lag", None),
            P("row", "col", "lag", None),
            P("row", "col", "lag"),
            P(None, ("row", "col", "lag")),
            P(None, ("row", "col", "lag")),
            P(None, ("row", "col", "lag")),
            P(None, ("row", "col", "lag")),
        ),
        out_specs=(P(None, ("row", "col", "lag")), P(None, ("row", "col", "lag"))),
        check_vma=False,
    )
```

```python
import functools

import jax
import jax.numpy as jnp
from jax import lax
from jax.experimental import pallas as pl
from jax.experimental.pallas import tpu as pltpu
from jax.sharding import PartitionSpec as P

NEWTON = 4
MESH = pl.DeviceIdType.MESH


def inverse_sinh(value):
    magnitude = jnp.abs(value)
    return jnp.sign(value) * jnp.log(magnitude + jnp.sqrt(1.0 + magnitude * magnitude))


def ring_kernel(n_z, n_pieces, part_ref, out_ref, recv, forward, final, cross,
                send_sem, recv_sem, cross_sem):
    row = lax.axis_index("row")
    col = lax.axis_index("col")
    lag = lax.axis_index("lag")
    z = col // 2
    y_hi = col % 2
    up = lax.rem(z + 1, n_z)
    down = lax.rem(z + n_z - 1, n_z)
    rows = part_ref.shape[1] // n_pieces

    def device(zz, yy):
        return (row, zz * 2 + yy, lag)

    barrier = pltpu.get_barrier_semaphore()
    for peer in (device(up, y_hi), device(down, y_hi), device(z, 1 - y_hi)):
        pl.semaphore_signal(barrier, inc=1, device_id=peer, device_id_type=MESH)
    pl.semaphore_wait(barrier, 3)

    steps = n_z - 1
    copies = {}
    for step in range(steps):
        for piece in range(n_pieces):
            span = pl.ds(piece * rows, rows)
            for way in range(2):
                if way == 0:
                    target = lax.rem(z + n_z - 1 - step, n_z)
                    dest = device(up, y_hi)
                else:
                    target = lax.rem(z + 1 + step, n_z)
                    dest = device(down, y_hi)
                block = target * 2 + way
                if step == 0:
                    source = part_ref.at[block, span]
                else:
                    copies[way, step - 1, piece].wait_recv()
                    forward[way, step, piece] = (
                        recv[way, step - 1, piece] + part_ref[block, span]
                    )
                    source = forward.at[way, step, piece]
                copy = pltpu.make_async_remote_copy(
                    src_ref=source,
                    dst_ref=recv.at[way, step, piece],
                    send_sem=send_sem.at[way, step, piece],
                    recv_sem=recv_sem.at[way, step, piece],
                    device_id=dest,
                    device_id_type=MESH,
                )
                copy.start()
                copies[way, step, piece] = copy

    handoffs = []
    for piece in range(n_pieces):
        span = pl.ds(piece * rows, rows)
        for way in range(2):
            copies[way, steps - 1, piece].wait_recv()
            final[way, piece] = recv[way, steps - 1, piece] + part_ref[z * 2 + way, span]
        handoff = pltpu.make_async_remote_copy(
            src_ref=final.at[1 - y_hi, piece],
            dst_ref=cross.at[piece],
            send_sem=cross_sem.at[0, piece],
            recv_sem=cross_sem.at[1, piece],
            device_id=device(z, 1 - y_hi),
            device_id_type=MESH,
        )
        handoff.start()
        handoffs.append(handoff)
    for piece in range(n_pieces):
        handoffs[piece].wait_recv()
        out_ref[pl.ds(piece * rows, rows), :] = final[y_hi, piece] + cross[piece]
    for handoff in handoffs:
        handoff.wait_send()
    for copy in copies.values():
        copy.wait_send()


def reduce_scatter(part, n_col, n_pieces=4):
    group, sims, tile = part.shape
    n_z = n_col // 2
    steps = n_z - 1
    rows = sims // n_pieces
    return pl.pallas_call(
        functools.partial(ring_kernel, n_z, n_pieces),
        out_shape=jax.ShapeDtypeStruct((sims, tile), jnp.float32),
        in_specs=[pl.BlockSpec(memory_space=pltpu.VMEM)],
        out_specs=pl.BlockSpec(memory_space=pltpu.VMEM),
        scratch_shapes=[
            pltpu.VMEM((2, steps, n_pieces, rows, tile), jnp.float32),
            pltpu.VMEM((2, steps, n_pieces, rows, tile), jnp.float32),
            pltpu.VMEM((2, n_pieces, rows, tile), jnp.float32),
            pltpu.VMEM((n_pieces, rows, tile), jnp.float32),
            pltpu.SemaphoreType.DMA((2, steps, n_pieces)),
            pltpu.SemaphoreType.DMA((2, steps, n_pieces)),
            pltpu.SemaphoreType.DMA((2, n_pieces)),
        ],
        compiler_params=pltpu.CompilerParams(
            collective_id=0, has_side_effects=True, vmem_limit_bytes=48 * 1024 * 1024
        ),
    )(part)


def parts_kernel(n_lag, rows_ref, cols_ref, count_ref, lag_ref, hist_ref, tiles_ref, out_ref):
    lag = pl.program_id(0)
    slots = tiles_ref.shape[1]
    side = tiles_ref.shape[2]

    @pl.when(lag == 0)
    def _():
        out_ref[...] = jnp.zeros_like(out_ref)

    for k in range(slots):
        @pl.when(k < count_ref[lag])
        def _():
            col = cols_ref[lag * slots + k]
            row = rows_ref[lag * slots + k]
            start = pl.multiple_of(col * side, side)
            history = hist_ref[0, :, pl.ds(start, side)]
            contrib = lax.dot_general(
                history, tiles_ref[0, k], (((1,), (1,)), ((), ())),
                preferred_element_type=jnp.float32,
            )
            half = jnp.where(row % n_lag == lag_ref[0], 0, 1)
            out_ref[half, row // n_lag] += contrib


def stress_parts(history, tiles, rows, cols, count, n_col, n_lag):
    lags, sims, sources = history.shape
    _, slots, side, _ = tiles.shape
    lag = lax.axis_index("lag").astype(jnp.int32).reshape(1)
    grid_spec = pltpu.PrefetchScalarGridSpec(
        num_scalar_prefetch=4,
        grid=(lags,),
        in_specs=[
            pl.BlockSpec((1, sims, sources), lambda l, *_: (l, 0, 0)),
            pl.BlockSpec((1, slots, side, side), lambda l, *_: (l, 0, 0, 0)),
        ],
        out_specs=pl.BlockSpec((2, n_col, sims, side), lambda l, *_: (0, 0, 0, 0)),
    )
    return pl.pallas_call(
        functools.partial(parts_kernel, n_lag),
        out_shape=jax.ShapeDtypeStruct((2, n_col, sims, side), jnp.float32),
        grid_spec=grid_spec,
        compiler_params=pltpu.CompilerParams(vmem_limit_bytes=48 * 1024 * 1024),
    )(rows.reshape(-1), cols.reshape(-1), count, lag, history, tiles)


def local(
    n_col,
    n_lag,
    history,
    kernel_tiles,
    tile_rows,
    tile_cols,
    tile_count,
    base_stress,
    prev_rate,
    direct_effect,
    state_var,
):
    gathered = lax.all_gather(history, "row", axis=3, tiled=True)
    tile_side = kernel_tiles.shape[4]
    parts = stress_parts(gathered[:, 0], kernel_tiles[0, 0], tile_rows[0, 0],
                         tile_cols[0, 0], tile_count[0, 0], n_col, n_lag)
    own, other = parts[0], parts[1]
    from_partner = lax.ppermute(other, "lag", perm=[(0, 1), (1, 0)])
    stress_change = reduce_scatter(own + from_partner, n_col)
    driving = base_stress + stress_change
    factor = jnp.exp(state_var) / 2.0
    velocity = prev_rate
    for step in range(NEWTON):
        scaled = velocity * factor
        misfit = direct_effect * inverse_sinh(scaled) + 0.5 * velocity - driving
        slope = direct_effect * factor / jnp.sqrt(1.0 + scaled * scaled) + 0.5
        velocity = velocity - misfit / slope
    return (stress_change, velocity)


def solution(mesh):
    return jax.shard_map(
        functools.partial(local, mesh.shape["col"], mesh.shape["lag"]),
        mesh=mesh,
        in_specs=(
            P("lag", "col", None, "row"),
            P("row", "col", "lag", None, None, None),
            P("row", "col", "lag", None),
            P("row", "col", "lag", None),
            P("row", "col", "lag"),
            P(None, ("row", "col", "lag")),
            P(None, ("row", "col", "lag")),
            P(None, ("row", "col", "lag")),
            P(None, ("row", "col", "lag")),
        ),
        out_specs=(P(None, ("row", "col", "lag")), P(None, ("row", "col", "lag"))),
        check_vma=False,
    )
```

```python
import functools

import jax
import jax.numpy as jnp
from jax import lax
from jax.experimental import pallas as pl
from jax.experimental.pallas import tpu as pltpu
from jax.sharding import PartitionSpec as P

NEWTON = 4
MESH = pl.DeviceIdType.MESH


def inverse_sinh(value):
    magnitude = jnp.abs(value)
    return jnp.sign(value) * jnp.log(magnitude + jnp.sqrt(1.0 + magnitude * magnitude))


def ring_kernel(n_z, n_pieces, part_ref, out_ref, recv, forward, final, cross,
                send_sem, recv_sem, cross_sem):
    row = lax.axis_index("row")
    col = lax.axis_index("col")
    lag = lax.axis_index("lag")
    z = col // 2
    y_hi = col % 2
    up = lax.rem(z + 1, n_z)
    down = lax.rem(z + n_z - 1, n_z)
    rows = part_ref.shape[1] // n_pieces

    def device(zz, yy):
        return (row, zz * 2 + yy, lag)

    barrier = pltpu.get_barrier_semaphore()
    for peer in (device(up, y_hi), device(down, y_hi), device(z, 1 - y_hi)):
        pl.semaphore_signal(barrier, inc=1, device_id=peer, device_id_type=MESH)
    pl.semaphore_wait(barrier, 3)

    steps = n_z - 1
    copies = {}
    for step in range(steps):
        for piece in range(n_pieces):
            span = pl.ds(piece * rows, rows)
            for way in range(2):
                if way == 0:
                    target = lax.rem(z + n_z - 1 - step, n_z)
                    dest = device(up, y_hi)
                else:
                    target = lax.rem(z + 1 + step, n_z)
                    dest = device(down, y_hi)
                block = target * 2 + way
                if step == 0:
                    source = part_ref.at[block, span]
                else:
                    copies[way, step - 1, piece].wait_recv()
                    forward[way, step, piece] = (
                        recv[way, step - 1, piece] + part_ref[block, span]
                    )
                    source = forward.at[way, step, piece]
                copy = pltpu.make_async_remote_copy(
                    src_ref=source,
                    dst_ref=recv.at[way, step, piece],
                    send_sem=send_sem.at[way, step, piece],
                    recv_sem=recv_sem.at[way, step, piece],
                    device_id=dest,
                    device_id_type=MESH,
                )
                copy.start()
                copies[way, step, piece] = copy

    handoffs = []
    for piece in range(n_pieces):
        span = pl.ds(piece * rows, rows)
        for way in range(2):
            copies[way, steps - 1, piece].wait_recv()
            final[way, piece] = recv[way, steps - 1, piece] + part_ref[z * 2 + way, span]
        handoff = pltpu.make_async_remote_copy(
            src_ref=final.at[1 - y_hi, piece],
            dst_ref=cross.at[piece],
            send_sem=cross_sem.at[0, piece],
            recv_sem=cross_sem.at[1, piece],
            device_id=device(z, 1 - y_hi),
            device_id_type=MESH,
        )
        handoff.start()
        handoffs.append(handoff)
    for piece in range(n_pieces):
        handoffs[piece].wait_recv()
        out_ref[pl.ds(piece * rows, rows), :] = final[y_hi, piece] + cross[piece]
    for handoff in handoffs:
        handoff.wait_send()
    for copy in copies.values():
        copy.wait_send()


def reduce_scatter(part, n_col, n_pieces=4):
    group, sims, tile = part.shape
    n_z = n_col // 2
    steps = n_z - 1
    rows = sims // n_pieces
    return pl.pallas_call(
        functools.partial(ring_kernel, n_z, n_pieces),
        out_shape=jax.ShapeDtypeStruct((sims, tile), jnp.float32),
        in_specs=[pl.BlockSpec(memory_space=pltpu.VMEM)],
        out_specs=pl.BlockSpec(memory_space=pltpu.VMEM),
        scratch_shapes=[
            pltpu.VMEM((2, steps, n_pieces, rows, tile), jnp.float32),
            pltpu.VMEM((2, steps, n_pieces, rows, tile), jnp.float32),
            pltpu.VMEM((2, n_pieces, rows, tile), jnp.float32),
            pltpu.VMEM((n_pieces, rows, tile), jnp.float32),
            pltpu.SemaphoreType.DMA((2, steps, n_pieces)),
            pltpu.SemaphoreType.DMA((2, steps, n_pieces)),
            pltpu.SemaphoreType.DMA((2, n_pieces)),
        ],
        compiler_params=pltpu.CompilerParams(
            collective_id=0, has_side_effects=True, vmem_limit_bytes=48 * 1024 * 1024
        ),
    )(part)


def gather_kernel(n_row, piece_ref, out_ref, local_sem, send_sem, recv_sem):
    me = lax.axis_index("row")
    col = lax.axis_index("col")
    lag = lax.axis_index("lag")

    def peer(t):
        return (t, col, lag)

    barrier = pltpu.get_barrier_semaphore()
    for d in range(1, n_row):
        t = lax.rem(me + d, n_row)
        pl.semaphore_signal(barrier, inc=1, device_id=peer(t), device_id_type=MESH)
    pl.semaphore_wait(barrier, n_row - 1)

    own = pltpu.make_async_copy(piece_ref, out_ref.at[me], local_sem)
    own.start()
    sends = []
    for d in range(1, n_row):
        t = lax.rem(me + d, n_row)
        copy = pltpu.make_async_remote_copy(
            src_ref=piece_ref,
            dst_ref=out_ref.at[me],
            send_sem=send_sem.at[t],
            recv_sem=recv_sem.at[me],
            device_id=peer(t),
            device_id_type=MESH,
        )
        copy.start()
        sends.append(copy)
    for d in range(1, n_row):
        s = lax.rem(me + n_row - d, n_row)
        incoming = pltpu.make_async_remote_copy(
            src_ref=piece_ref,
            dst_ref=out_ref.at[s],
            send_sem=send_sem.at[s],
            recv_sem=recv_sem.at[s],
            device_id=peer(s),
            device_id_type=MESH,
        )
        incoming.wait_recv()
    own.wait()
    for copy in sends:
        copy.wait_send()


def all_gather_rows(piece, n_row):
    return pl.pallas_call(
        functools.partial(gather_kernel, n_row),
        out_shape=jax.ShapeDtypeStruct((n_row,) + piece.shape, piece.dtype),
        in_specs=[pl.BlockSpec(memory_space=pltpu.VMEM)],
        out_specs=pl.BlockSpec(memory_space=pl.ANY),
        scratch_shapes=[
            pltpu.SemaphoreType.DMA(()),
            pltpu.SemaphoreType.DMA((n_row,)),
            pltpu.SemaphoreType.DMA((n_row,)),
        ],
        compiler_params=pltpu.CompilerParams(collective_id=1, has_side_effects=True),
    )(piece)


def parts_kernel(n_lag, rows_ref, cols_ref, count_ref, lag_ref, hist_ref, tiles_ref, out_ref):
    lag = pl.program_id(0)
    slots = tiles_ref.shape[1]
    side = tiles_ref.shape[2]
    halves = hist_ref.shape[3] // side

    @pl.when(lag == 0)
    def _():
        out_ref[...] = jnp.zeros_like(out_ref)

    for k in range(slots):
        @pl.when(k < count_ref[lag])
        def _():
            col = cols_ref[lag * slots + k]
            row = rows_ref[lag * slots + k]
            start = pl.multiple_of((col % halves) * side, side)
            history = hist_ref[col // halves, 0, :, pl.ds(start, side)]
            contrib = lax.dot_general(
                history, tiles_ref[0, k], (((1,), (1,)), ((), ())),
                preferred_element_type=jnp.float32,
            )
            half = jnp.where(row % n_lag == lag_ref[0], 0, 1)
            out_ref[half, row // n_lag] += contrib


def stress_parts(history, tiles, rows, cols, count, n_col, n_lag):
    n_row, lags, sims, held = history.shape
    _, slots, side, _ = tiles.shape
    lag = lax.axis_index("lag").astype(jnp.int32).reshape(1)
    grid_spec = pltpu.PrefetchScalarGridSpec(
        num_scalar_prefetch=4,
        grid=(lags,),
        in_specs=[
            pl.BlockSpec((n_row, 1, sims, held), lambda l, *_: (0, l, 0, 0)),
            pl.BlockSpec((1, slots, side, side), lambda l, *_: (l, 0, 0, 0)),
        ],
        out_specs=pl.BlockSpec((2, n_col, sims, side), lambda l, *_: (0, 0, 0, 0)),
    )
    return pl.pallas_call(
        functools.partial(parts_kernel, n_lag),
        out_shape=jax.ShapeDtypeStruct((2, n_col, sims, side), jnp.float32),
        grid_spec=grid_spec,
        compiler_params=pltpu.CompilerParams(vmem_limit_bytes=48 * 1024 * 1024),
    )(rows.reshape(-1), cols.reshape(-1), count, lag, history, tiles)


def local(
    n_row,
    n_col,
    n_lag,
    history,
    kernel_tiles,
    tile_rows,
    tile_cols,
    tile_count,
    base_stress,
    prev_rate,
    direct_effect,
    state_var,
):
    gathered = all_gather_rows(history[:, 0], n_row)
    tile_side = kernel_tiles.shape[4]
    parts = stress_parts(gathered, kernel_tiles[0, 0], tile_rows[0, 0],
                         tile_cols[0, 0], tile_count[0, 0], n_col, n_lag)
    own, other = parts[0], parts[1]
    from_partner = lax.ppermute(other, "lag", perm=[(0, 1), (1, 0)])
    stress_change = reduce_scatter(own + from_partner, n_col)
    driving = base_stress + stress_change
    factor = jnp.exp(state_var) / 2.0
    velocity = prev_rate
    for step in range(NEWTON):
        scaled = velocity * factor
        misfit = direct_effect * inverse_sinh(scaled) + 0.5 * velocity - driving
        slope = direct_effect * factor / jnp.sqrt(1.0 + scaled * scaled) + 0.5
        velocity = velocity - misfit / slope
    return (stress_change, velocity)


def solution(mesh):
    return jax.shard_map(
        functools.partial(local, mesh.shape["row"], mesh.shape["col"], mesh.shape["lag"]),
        mesh=mesh,
        in_specs=(
            P("lag", "col", None, "row"),
            P("row", "col", "lag", None, None, None),
            P("row", "col", "lag", None),
            P("row", "col", "lag", None),
            P("row", "col", "lag"),
            P(None, ("row", "col", "lag")),
            P(None, ("row", "col", "lag")),
            P(None, ("row", "col", "lag")),
            P(None, ("row", "col", "lag")),
        ),
        out_specs=(P(None, ("row", "col", "lag")), P(None, ("row", "col", "lag"))),
        check_vma=False,
    )
```

```python
import functools

import jax
import jax.numpy as jnp
from jax import lax
from jax.experimental import pallas as pl
from jax.experimental.pallas import tpu as pltpu
from jax.sharding import PartitionSpec as P

NEWTON = 4
MESH = pl.DeviceIdType.MESH


def inverse_sinh(value):
    magnitude = jnp.abs(value)
    return jnp.sign(value) * jnp.log(magnitude + jnp.sqrt(1.0 + magnitude * magnitude))


def ring_kernel(n_z, n_pieces, part_ref, out_ref, recv, forward, final, cross,
                send_sem, recv_sem, cross_sem):
    row = lax.axis_index("row")
    col = lax.axis_index("col")
    lag = lax.axis_index("lag")
    z = col // 2
    y_hi = col % 2
    up = lax.rem(z + 1, n_z)
    down = lax.rem(z + n_z - 1, n_z)
    rows = part_ref.shape[1] // n_pieces

    def device(zz, yy):
        return (row, zz * 2 + yy, lag)

    barrier = pltpu.get_barrier_semaphore()
    for peer in (device(up, y_hi), device(down, y_hi), device(z, 1 - y_hi)):
        pl.semaphore_signal(barrier, inc=1, device_id=peer, device_id_type=MESH)
    pl.semaphore_wait(barrier, 3)

    steps = n_z - 1
    copies = {}
    for step in range(steps):
        for piece in range(n_pieces):
            span = pl.ds(piece * rows, rows)
            for way in range(2):
                if way == 0:
                    target = lax.rem(z + n_z - 1 - step, n_z)
                    dest = device(up, y_hi)
                else:
                    target = lax.rem(z + 1 + step, n_z)
                    dest = device(down, y_hi)
                block = target * 2 + way
                if step == 0:
                    source = part_ref.at[block, span]
                else:
                    copies[way, step - 1, piece].wait_recv()
                    forward[way, step, piece] = (
                        recv[way, step - 1, piece] + part_ref[block, span]
                    )
                    source = forward.at[way, step, piece]
                copy = pltpu.make_async_remote_copy(
                    src_ref=source,
                    dst_ref=recv.at[way, step, piece],
                    send_sem=send_sem.at[way, step, piece],
                    recv_sem=recv_sem.at[way, step, piece],
                    device_id=dest,
                    device_id_type=MESH,
                )
                copy.start()
                copies[way, step, piece] = copy

    handoffs = []
    for piece in range(n_pieces):
        span = pl.ds(piece * rows, rows)
        for way in range(2):
            copies[way, steps - 1, piece].wait_recv()
            final[way, piece] = recv[way, steps - 1, piece] + part_ref[z * 2 + way, span]
        handoff = pltpu.make_async_remote_copy(
            src_ref=final.at[1 - y_hi, piece],
            dst_ref=cross.at[piece],
            send_sem=cross_sem.at[0, piece],
            recv_sem=cross_sem.at[1, piece],
            device_id=device(z, 1 - y_hi),
            device_id_type=MESH,
        )
        handoff.start()
        handoffs.append(handoff)
    for piece in range(n_pieces):
        handoffs[piece].wait_recv()
        out_ref[pl.ds(piece * rows, rows), :] = final[y_hi, piece] + cross[piece]
    for handoff in handoffs:
        handoff.wait_send()
    for copy in copies.values():
        copy.wait_send()


def reduce_scatter(part, n_col, n_pieces=4):
    group, sims, tile = part.shape
    n_z = n_col // 2
    steps = n_z - 1
    rows = sims // n_pieces
    return pl.pallas_call(
        functools.partial(ring_kernel, n_z, n_pieces),
        out_shape=jax.ShapeDtypeStruct((sims, tile), jnp.float32),
        in_specs=[pl.BlockSpec(memory_space=pltpu.VMEM)],
        out_specs=pl.BlockSpec(memory_space=pltpu.VMEM),
        scratch_shapes=[
            pltpu.VMEM((2, steps, n_pieces, rows, tile), jnp.float32),
            pltpu.VMEM((2, steps, n_pieces, rows, tile), jnp.float32),
            pltpu.VMEM((2, n_pieces, rows, tile), jnp.float32),
            pltpu.VMEM((n_pieces, rows, tile), jnp.float32),
            pltpu.SemaphoreType.DMA((2, steps, n_pieces)),
            pltpu.SemaphoreType.DMA((2, steps, n_pieces)),
            pltpu.SemaphoreType.DMA((2, n_pieces)),
        ],
        compiler_params=pltpu.CompilerParams(
            collective_id=0, has_side_effects=True, vmem_limit_bytes=48 * 1024 * 1024
        ),
    )(part)


def gather_kernel(n_x, piece_ref, out_ref, local_sem, send_sem, recv_sem):
    me = lax.axis_index("row")
    col = lax.axis_index("col")
    lag = lax.axis_index("lag")
    y = me // n_x
    x = me % n_x
    right = x + 1
    left = x + n_x - 1
    across = 1 - y
    half = piece_ref.shape[0] // 2

    def slot(yy, xx):
        return yy * n_x + lax.rem(xx, n_x)

    def device(yy, xx):
        return (slot(yy, xx), col, lag)

    def region(index, part):
        if part is None:
            return out_ref.at[index], recv_sem.at[index, 0]
        return out_ref.at[index, pl.ds(part * half, half)], recv_sem.at[index, part]

    barrier = pltpu.get_barrier_semaphore()
    for peer in (device(y, right), device(y, left), device(across, x)):
        pl.semaphore_signal(barrier, inc=1, device_id=peer, device_id_type=MESH)
    pl.semaphore_wait(barrier, 3)

    mine = slot(y, x)
    own = pltpu.make_async_copy(piece_ref, out_ref.at[mine], local_sem)
    own.start()
    sends = []

    def send(index, part, dest, from_input=False):
        target, sem = region(index, part)
        if from_input:
            source = piece_ref
        else:
            source = region(index, part)[0]
        copy = pltpu.make_async_remote_copy(
            src_ref=source,
            dst_ref=target,
            send_sem=send_sem.at[len(sends)],
            recv_sem=sem,
            device_id=dest,
            device_id_type=MESH,
        )
        copy.start()
        sends.append(copy)

    def arrive(index, part):
        target, sem = region(index, part)
        source = piece_ref if part is None else piece_ref.at[pl.ds(part * half, half)]
        pltpu.make_async_remote_copy(
            src_ref=source,
            dst_ref=target,
            send_sem=send_sem.at[0],
            recv_sem=sem,
            device_id=device(y, right),
            device_id_type=MESH,
        ).wait_recv()

    send(mine, None, device(y, right), from_input=True)
    send(mine, None, device(y, left), from_input=True)
    send(mine, None, device(across, x), from_input=True)
    arrive(slot(y, left), None)
    send(slot(y, left), 0, device(y, right))
    arrive(slot(y, right), None)
    send(slot(y, right), 1, device(y, left))
    arrive(slot(across, x), None)
    send(slot(across, x), None, device(y, right))
    send(slot(across, x), None, device(y, left))
    arrive(slot(across, left), None)
    send(slot(across, left), 0, device(y, right))
    arrive(slot(across, right), None)
    send(slot(across, right), 1, device(y, left))
    for yy in (y, across):
        arrive(slot(yy, x + 2), 0)
        arrive(slot(yy, x + 2), 1)
    own.wait()
    for copy in sends:
        copy.wait_send()


def all_gather_rows(piece, n_row):
    n_x = n_row // 2
    assert n_x == 4
    return pl.pallas_call(
        functools.partial(gather_kernel, n_x),
        out_shape=jax.ShapeDtypeStruct((n_row,) + piece.shape, piece.dtype),
        in_specs=[pl.BlockSpec(memory_space=pltpu.VMEM)],
        out_specs=pl.BlockSpec(memory_space=pl.ANY),
        scratch_shapes=[
            pltpu.SemaphoreType.DMA(()),
            pltpu.SemaphoreType.DMA((9,)),
            pltpu.SemaphoreType.DMA((n_row, 2)),
        ],
        compiler_params=pltpu.CompilerParams(collective_id=1, has_side_effects=True),
    )(piece)


def parts_kernel(n_lag, rows_ref, cols_ref, count_ref, lag_ref, hist_ref, tiles_ref, out_ref):
    lag = pl.program_id(0)
    slots = tiles_ref.shape[1]
    side = tiles_ref.shape[2]
    halves = hist_ref.shape[3] // side

    @pl.when(lag == 0)
    def _():
        out_ref[...] = jnp.zeros_like(out_ref)

    for k in range(slots):
        @pl.when(k < count_ref[lag])
        def _():
            col = cols_ref[lag * slots + k]
            row = rows_ref[lag * slots + k]
            start = pl.multiple_of((col % halves) * side, side)
            history = hist_ref[col // halves, 0, :, pl.ds(start, side)]
            contrib = lax.dot_general(
                history, tiles_ref[0, k], (((1,), (1,)), ((), ())),
                preferred_element_type=jnp.float32,
            )
            half = jnp.where(row % n_lag == lag_ref[0], 0, 1)
            out_ref[half, row // n_lag] += contrib


def stress_parts(history, tiles, rows, cols, count, n_col, n_lag):
    n_row, lags, sims, held = history.shape
    _, slots, side, _ = tiles.shape
    lag = lax.axis_index("lag").astype(jnp.int32).reshape(1)
    grid_spec = pltpu.PrefetchScalarGridSpec(
        num_scalar_prefetch=4,
        grid=(lags,),
        in_specs=[
            pl.BlockSpec((n_row, 1, sims, held), lambda l, *_: (0, l, 0, 0)),
            pl.BlockSpec((1, slots, side, side), lambda l, *_: (l, 0, 0, 0)),
        ],
        out_specs=pl.BlockSpec((2, n_col, sims, side), lambda l, *_: (0, 0, 0, 0)),
    )
    return pl.pallas_call(
        functools.partial(parts_kernel, n_lag),
        out_shape=jax.ShapeDtypeStruct((2, n_col, sims, side), jnp.float32),
        grid_spec=grid_spec,
        compiler_params=pltpu.CompilerParams(vmem_limit_bytes=48 * 1024 * 1024),
    )(rows.reshape(-1), cols.reshape(-1), count, lag, history, tiles)


def local(
    n_row,
    n_col,
    n_lag,
    history,
    kernel_tiles,
    tile_rows,
    tile_cols,
    tile_count,
    base_stress,
    prev_rate,
    direct_effect,
    state_var,
):
    gathered = all_gather_rows(history[:, 0], n_row)
    tile_side = kernel_tiles.shape[4]
    parts = stress_parts(gathered, kernel_tiles[0, 0], tile_rows[0, 0],
                         tile_cols[0, 0], tile_count[0, 0], n_col, n_lag)
    own, other = parts[0], parts[1]
    from_partner = lax.ppermute(other, "lag", perm=[(0, 1), (1, 0)])
    stress_change = reduce_scatter(own + from_partner, n_col)
    driving = base_stress + stress_change
    factor = jnp.exp(state_var) / 2.0
    velocity = prev_rate
    for step in range(NEWTON):
        scaled = velocity * factor
        misfit = direct_effect * inverse_sinh(scaled) + 0.5 * velocity - driving
        slope = direct_effect * factor / jnp.sqrt(1.0 + scaled * scaled) + 0.5
        velocity = velocity - misfit / slope
    return (stress_change, velocity)


def solution(mesh):
    return jax.shard_map(
        functools.partial(local, mesh.shape["row"], mesh.shape["col"], mesh.shape["lag"]),
        mesh=mesh,
        in_specs=(
            P("lag", "col", None, "row"),
            P("row", "col", "lag", None, None, None),
            P("row", "col", "lag", None),
            P("row", "col", "lag", None),
            P("row", "col", "lag"),
            P(None, ("row", "col", "lag")),
            P(None, ("row", "col", "lag")),
            P(None, ("row", "col", "lag")),
            P(None, ("row", "col", "lag")),
        ),
        out_specs=(P(None, ("row", "col", "lag")), P(None, ("row", "col", "lag"))),
        check_vma=False,
    )
```

```python
import functools

import jax
import jax.numpy as jnp
from jax import lax
from jax.experimental import pallas as pl
from jax.experimental.pallas import tpu as pltpu
from jax.sharding import PartitionSpec as P

NEWTON = 4
MESH = pl.DeviceIdType.MESH


def inverse_sinh(value):
    magnitude = jnp.abs(value)
    return jnp.sign(value) * jnp.log(magnitude + jnp.sqrt(1.0 + magnitude * magnitude))


def ring_kernel(n_z, n_pieces, part_ref, out_ref, recv, forward, final, cross,
                send_sem, recv_sem, cross_sem):
    row = lax.axis_index("row")
    col = lax.axis_index("col")
    lag = lax.axis_index("lag")
    z = col // 2
    y_hi = col % 2
    up = lax.rem(z + 1, n_z)
    down = lax.rem(z + n_z - 1, n_z)
    rows = part_ref.shape[1] // n_pieces

    def device(zz, yy):
        return (row, zz * 2 + yy, lag)

    barrier = pltpu.get_barrier_semaphore()
    for peer in (device(up, y_hi), device(down, y_hi), device(z, 1 - y_hi)):
        pl.semaphore_signal(barrier, inc=1, device_id=peer, device_id_type=MESH)
    pl.semaphore_wait(barrier, 3)

    steps = n_z - 1
    copies = {}
    for step in range(steps):
        for piece in range(n_pieces):
            span = pl.ds(piece * rows, rows)
            for way in range(2):
                if way == 0:
                    target = lax.rem(z + n_z - 1 - step, n_z)
                    dest = device(up, y_hi)
                else:
                    target = lax.rem(z + 1 + step, n_z)
                    dest = device(down, y_hi)
                block = target * 2 + way
                if step == 0:
                    source = part_ref.at[block, span]
                else:
                    copies[way, step - 1, piece].wait_recv()
                    forward[way, step, piece] = (
                        recv[way, step - 1, piece] + part_ref[block, span]
                    )
                    source = forward.at[way, step, piece]
                copy = pltpu.make_async_remote_copy(
                    src_ref=source,
                    dst_ref=recv.at[way, step, piece],
                    send_sem=send_sem.at[way, step, piece],
                    recv_sem=recv_sem.at[way, step, piece],
                    device_id=dest,
                    device_id_type=MESH,
                )
                copy.start()
                copies[way, step, piece] = copy

    handoffs = []
    for piece in range(n_pieces):
        span = pl.ds(piece * rows, rows)
        for way in range(2):
            copies[way, steps - 1, piece].wait_recv()
            final[way, piece] = recv[way, steps - 1, piece] + part_ref[z * 2 + way, span]
        handoff = pltpu.make_async_remote_copy(
            src_ref=final.at[1 - y_hi, piece],
            dst_ref=cross.at[piece],
            send_sem=cross_sem.at[0, piece],
            recv_sem=cross_sem.at[1, piece],
            device_id=device(z, 1 - y_hi),
            device_id_type=MESH,
        )
        handoff.start()
        handoffs.append(handoff)
    for piece in range(n_pieces):
        handoffs[piece].wait_recv()
        out_ref[pl.ds(piece * rows, rows), :] = final[y_hi, piece] + cross[piece]
    for handoff in handoffs:
        handoff.wait_send()
    for copy in copies.values():
        copy.wait_send()


def reduce_scatter(part, n_col, n_pieces=4):
    group, sims, tile = part.shape
    n_z = n_col // 2
    steps = n_z - 1
    rows = sims // n_pieces
    return pl.pallas_call(
        functools.partial(ring_kernel, n_z, n_pieces),
        out_shape=jax.ShapeDtypeStruct((sims, tile), jnp.float32),
        in_specs=[pl.BlockSpec(memory_space=pltpu.VMEM)],
        out_specs=pl.BlockSpec(memory_space=pltpu.VMEM),
        scratch_shapes=[
            pltpu.VMEM((2, steps, n_pieces, rows, tile), jnp.float32),
            pltpu.VMEM((2, steps, n_pieces, rows, tile), jnp.float32),
            pltpu.VMEM((2, n_pieces, rows, tile), jnp.float32),
            pltpu.VMEM((n_pieces, rows, tile), jnp.float32),
            pltpu.SemaphoreType.DMA((2, steps, n_pieces)),
            pltpu.SemaphoreType.DMA((2, steps, n_pieces)),
            pltpu.SemaphoreType.DMA((2, n_pieces)),
        ],
        compiler_params=pltpu.CompilerParams(
            collective_id=0, has_side_effects=True, vmem_limit_bytes=48 * 1024 * 1024
        ),
    )(part)


def gather_kernel(n_x, n_pieces, piece_ref, out_ref, local_sem, send_sem, recv_sem):
    me = lax.axis_index("row")
    col = lax.axis_index("col")
    lag = lax.axis_index("lag")
    y = me // n_x
    x = me % n_x
    right = x + 1
    left = x + n_x - 1
    across = 1 - y
    half = piece_ref.shape[0] // 2
    rows = piece_ref.shape[1] // n_pieces

    def slot(yy, xx):
        return yy * n_x + lax.rem(xx, n_x)

    def device(yy, xx):
        return (slot(yy, xx), col, lag)

    def span(part):
        return slice(None) if part is None else pl.ds(part * half, half)

    def region(ref, part, piece):
        return ref.at[span(part), pl.ds(piece * rows, rows)]

    def semaphore(index, part, piece):
        return recv_sem.at[index, 0 if part is None else part, piece]

    barrier = pltpu.get_barrier_semaphore()
    for peer in (device(y, right), device(y, left), device(across, x)):
        pl.semaphore_signal(barrier, inc=1, device_id=peer, device_id_type=MESH)
    pl.semaphore_wait(barrier, 3)

    mine = slot(y, x)
    own = pltpu.make_async_copy(piece_ref, out_ref.at[mine], local_sem)
    own.start()
    sends = []

    def send(index, part, dest, from_input=False):
        for piece in range(n_pieces):
            source = piece_ref if from_input else out_ref.at[index]
            copy = pltpu.make_async_remote_copy(
                src_ref=region(source, part, piece),
                dst_ref=region(out_ref.at[index], part, piece),
                send_sem=send_sem.at[len(sends)],
                recv_sem=semaphore(index, part, piece),
                device_id=dest,
                device_id_type=MESH,
            )
            copy.start()
            sends.append(copy)

    def arrive(index, part, piece):
        pltpu.make_async_remote_copy(
            src_ref=region(piece_ref, part, piece),
            dst_ref=region(out_ref.at[index], part, piece),
            send_sem=send_sem.at[0],
            recv_sem=semaphore(index, part, piece),
            device_id=device(y, right),
            device_id_type=MESH,
        ).wait_recv()

    def relay(index, part, dests):
        for piece in range(n_pieces):
            arrive(index, None, piece)
            for dest in dests:
                for_piece = pltpu.make_async_remote_copy(
                    src_ref=region(out_ref.at[index], part, piece),
                    dst_ref=region(out_ref.at[index], part, piece),
                    send_sem=send_sem.at[len(sends)],
                    recv_sem=semaphore(index, part, piece),
                    device_id=dest,
                    device_id_type=MESH,
                )
                for_piece.start()
                sends.append(for_piece)

    send(mine, None, device(y, right), from_input=True)
    send(mine, None, device(y, left), from_input=True)
    send(mine, None, device(across, x), from_input=True)
    relay(slot(y, left), 0, [device(y, right)])
    relay(slot(y, right), 1, [device(y, left)])
    relay(slot(across, x), None, [device(y, right), device(y, left)])
    relay(slot(across, left), 0, [device(y, right)])
    relay(slot(across, right), 1, [device(y, left)])
    for yy in (y, across):
        for piece in range(n_pieces):
            arrive(slot(yy, x + 2), 0, piece)
            arrive(slot(yy, x + 2), 1, piece)
    own.wait()
    for copy in sends:
        copy.wait_send()


def all_gather_rows(piece, n_row, n_pieces=2):
    n_x = n_row // 2
    assert n_x == 4
    return pl.pallas_call(
        functools.partial(gather_kernel, n_x, n_pieces),
        out_shape=jax.ShapeDtypeStruct((n_row,) + piece.shape, piece.dtype),
        in_specs=[pl.BlockSpec(memory_space=pltpu.VMEM)],
        out_specs=pl.BlockSpec(memory_space=pl.ANY),
        scratch_shapes=[
            pltpu.SemaphoreType.DMA(()),
            pltpu.SemaphoreType.DMA((9 * n_pieces,)),
            pltpu.SemaphoreType.DMA((n_row, 2, n_pieces)),
        ],
        compiler_params=pltpu.CompilerParams(collective_id=1, has_side_effects=True),
    )(piece)


def parts_kernel(n_lag, rows_ref, cols_ref, count_ref, lag_ref, hist_ref, tiles_ref, out_ref):
    lag = pl.program_id(0)
    slots = tiles_ref.shape[1]
    side = tiles_ref.shape[2]
    halves = hist_ref.shape[3] // side

    @pl.when(lag == 0)
    def _():
        out_ref[...] = jnp.zeros_like(out_ref)

    for k in range(slots):
        @pl.when(k < count_ref[lag])
        def _():
            col = cols_ref[lag * slots + k]
            row = rows_ref[lag * slots + k]
            start = pl.multiple_of((col % halves) * side, side)
            history = hist_ref[col // halves, 0, :, pl.ds(start, side)]
            contrib = lax.dot_general(
                history, tiles_ref[0, k], (((1,), (1,)), ((), ())),
                preferred_element_type=jnp.float32,
            )
            half = jnp.where(row % n_lag == lag_ref[0], 0, 1)
            out_ref[half, row // n_lag] += contrib


def stress_parts(history, tiles, rows, cols, count, n_col, n_lag):
    n_row, lags, sims, held = history.shape
    _, slots, side, _ = tiles.shape
    lag = lax.axis_index("lag").astype(jnp.int32).reshape(1)
    grid_spec = pltpu.PrefetchScalarGridSpec(
        num_scalar_prefetch=4,
        grid=(lags,),
        in_specs=[
            pl.BlockSpec((n_row, 1, sims, held), lambda l, *_: (0, l, 0, 0)),
            pl.BlockSpec((1, slots, side, side), lambda l, *_: (l, 0, 0, 0)),
        ],
        out_specs=pl.BlockSpec((2, n_col, sims, side), lambda l, *_: (0, 0, 0, 0)),
    )
    return pl.pallas_call(
        functools.partial(parts_kernel, n_lag),
        out_shape=jax.ShapeDtypeStruct((2, n_col, sims, side), jnp.float32),
        grid_spec=grid_spec,
        compiler_params=pltpu.CompilerParams(vmem_limit_bytes=48 * 1024 * 1024),
    )(rows.reshape(-1), cols.reshape(-1), count, lag, history, tiles)


def local(
    n_row,
    n_col,
    n_lag,
    history,
    kernel_tiles,
    tile_rows,
    tile_cols,
    tile_count,
    base_stress,
    prev_rate,
    direct_effect,
    state_var,
):
    gathered = all_gather_rows(history[:, 0], n_row)
    tile_side = kernel_tiles.shape[4]
    parts = stress_parts(gathered, kernel_tiles[0, 0], tile_rows[0, 0],
                         tile_cols[0, 0], tile_count[0, 0], n_col, n_lag)
    own, other = parts[0], parts[1]
    from_partner = lax.ppermute(other, "lag", perm=[(0, 1), (1, 0)])
    stress_change = reduce_scatter(own + from_partner, n_col)
    driving = base_stress + stress_change
    factor = jnp.exp(state_var) / 2.0
    velocity = prev_rate
    for step in range(NEWTON):
        scaled = velocity * factor
        misfit = direct_effect * inverse_sinh(scaled) + 0.5 * velocity - driving
        slope = direct_effect * factor / jnp.sqrt(1.0 + scaled * scaled) + 0.5
        velocity = velocity - misfit / slope
    return (stress_change, velocity)


def solution(mesh):
    return jax.shard_map(
        functools.partial(local, mesh.shape["row"], mesh.shape["col"], mesh.shape["lag"]),
        mesh=mesh,
        in_specs=(
            P("lag", "col", None, "row"),
            P("row", "col", "lag", None, None, None),
            P("row", "col", "lag", None),
            P("row", "col", "lag", None),
            P("row", "col", "lag"),
            P(None, ("row", "col", "lag")),
            P(None, ("row", "col", "lag")),
            P(None, ("row", "col", "lag")),
            P(None, ("row", "col", "lag")),
        ),
        out_specs=(P(None, ("row", "col", "lag")), P(None, ("row", "col", "lag"))),
        check_vma=False,
    )
```

```python
import functools

import jax
import jax.numpy as jnp
from jax import lax
from jax.experimental import pallas as pl
from jax.experimental.pallas import tpu as pltpu
from jax.sharding import PartitionSpec as P

NEWTON = 4
MESH = pl.DeviceIdType.MESH


def inverse_sinh(value):
    magnitude = jnp.abs(value)
    return jnp.sign(value) * jnp.log(magnitude + jnp.sqrt(1.0 + magnitude * magnitude))


def ring_kernel(n_z, n_pieces, part_ref, out_ref, recv, forward, final, cross,
                send_sem, recv_sem, cross_sem):
    row = lax.axis_index("row")
    col = lax.axis_index("col")
    lag = lax.axis_index("lag")
    z = col // 2
    y_hi = col % 2
    up = lax.rem(z + 1, n_z)
    down = lax.rem(z + n_z - 1, n_z)
    rows = part_ref.shape[1] // n_pieces

    def device(zz, yy):
        return (row, zz * 2 + yy, lag)

    barrier = pltpu.get_barrier_semaphore()
    for peer in (device(up, y_hi), device(down, y_hi), device(z, 1 - y_hi)):
        pl.semaphore_signal(barrier, inc=1, device_id=peer, device_id_type=MESH)
    pl.semaphore_wait(barrier, 3)

    steps = n_z - 1
    copies = {}
    for step in range(steps):
        for piece in range(n_pieces):
            span = pl.ds(piece * rows, rows)
            for way in range(2):
                if way == 0:
                    target = lax.rem(z + n_z - 1 - step, n_z)
                    dest = device(up, y_hi)
                else:
                    target = lax.rem(z + 1 + step, n_z)
                    dest = device(down, y_hi)
                block = target * 2 + way
                if step == 0:
                    source = part_ref.at[block, span]
                else:
                    copies[way, step - 1, piece].wait_recv()
                    forward[way, step, piece] = (
                        recv[way, step - 1, piece] + part_ref[block, span]
                    )
                    source = forward.at[way, step, piece]
                copy = pltpu.make_async_remote_copy(
                    src_ref=source,
                    dst_ref=recv.at[way, step, piece],
                    send_sem=send_sem.at[way, step, piece],
                    recv_sem=recv_sem.at[way, step, piece],
                    device_id=dest,
                    device_id_type=MESH,
                )
                copy.start()
                copies[way, step, piece] = copy

    handoffs = []
    for piece in range(n_pieces):
        span = pl.ds(piece * rows, rows)
        for way in range(2):
            copies[way, steps - 1, piece].wait_recv()
            final[way, piece] = recv[way, steps - 1, piece] + part_ref[z * 2 + way, span]
        handoff = pltpu.make_async_remote_copy(
            src_ref=final.at[1 - y_hi, piece],
            dst_ref=cross.at[piece],
            send_sem=cross_sem.at[0, piece],
            recv_sem=cross_sem.at[1, piece],
            device_id=device(z, 1 - y_hi),
            device_id_type=MESH,
        )
        handoff.start()
        handoffs.append(handoff)
    for piece in range(n_pieces):
        handoffs[piece].wait_recv()
        out_ref[pl.ds(piece * rows, rows), :] = final[y_hi, piece] + cross[piece]
    for handoff in handoffs:
        handoff.wait_send()
    for copy in copies.values():
        copy.wait_send()


def reduce_scatter(part, n_col, n_pieces=4):
    group, sims, tile = part.shape
    n_z = n_col // 2
    steps = n_z - 1
    rows = sims // n_pieces
    return pl.pallas_call(
        functools.partial(ring_kernel, n_z, n_pieces),
        out_shape=jax.ShapeDtypeStruct((sims, tile), jnp.float32),
        in_specs=[pl.BlockSpec(memory_space=pltpu.VMEM)],
        out_specs=pl.BlockSpec(memory_space=pltpu.VMEM),
        scratch_shapes=[
            pltpu.VMEM((2, steps, n_pieces, rows, tile), jnp.float32),
            pltpu.VMEM((2, steps, n_pieces, rows, tile), jnp.float32),
            pltpu.VMEM((2, n_pieces, rows, tile), jnp.float32),
            pltpu.VMEM((n_pieces, rows, tile), jnp.float32),
            pltpu.SemaphoreType.DMA((2, steps, n_pieces)),
            pltpu.SemaphoreType.DMA((2, steps, n_pieces)),
            pltpu.SemaphoreType.DMA((2, n_pieces)),
        ],
        compiler_params=pltpu.CompilerParams(
            collective_id=0, has_side_effects=True, vmem_limit_bytes=48 * 1024 * 1024
        ),
    )(part)


def gather_kernel(n_x, piece_ref, out_ref, local_sem, send_sem, recv_sem):
    me = lax.axis_index("row")
    col = lax.axis_index("col")
    lag = lax.axis_index("lag")
    y = me // n_x
    x = me % n_x
    right = x + 1
    left = x + n_x - 1
    across = 1 - y
    half = piece_ref.shape[0] // 2

    def slot(yy, xx):
        return yy * n_x + lax.rem(xx, n_x)

    def device(yy, xx):
        return (slot(yy, xx), col, lag)

    def region(index, part):
        if part is None:
            return out_ref.at[index], recv_sem.at[index, 0]
        return out_ref.at[index, pl.ds(part * half, half)], recv_sem.at[index, part]

    barrier = pltpu.get_barrier_semaphore()
    for peer in (device(y, right), device(y, left), device(across, x)):
        pl.semaphore_signal(barrier, inc=1, device_id=peer, device_id_type=MESH)
    pl.semaphore_wait(barrier, 3)

    mine = slot(y, x)
    own = pltpu.make_async_copy(piece_ref, out_ref.at[mine], local_sem)
    own.start()
    sends = []

    def send(index, part, dest, from_input=False):
        target, sem = region(index, part)
        if from_input:
            source = piece_ref
        else:
            source = region(index, part)[0]
        copy = pltpu.make_async_remote_copy(
            src_ref=source,
            dst_ref=target,
            send_sem=send_sem.at[len(sends)],
            recv_sem=sem,
            device_id=dest,
            device_id_type=MESH,
        )
        copy.start()
        sends.append(copy)

    def arrive(index, part):
        target, sem = region(index, part)
        source = piece_ref if part is None else piece_ref.at[pl.ds(part * half, half)]
        pltpu.make_async_remote_copy(
            src_ref=source,
            dst_ref=target,
            send_sem=send_sem.at[0],
            recv_sem=sem,
            device_id=device(y, right),
            device_id_type=MESH,
        ).wait_recv()

    send(mine, None, device(y, right), from_input=True)
    send(mine, None, device(y, left), from_input=True)
    send(mine, None, device(across, x), from_input=True)
    arrive(slot(y, left), None)
    send(slot(y, left), 0, device(y, right))
    arrive(slot(y, right), None)
    send(slot(y, right), 1, device(y, left))
    arrive(slot(across, x), None)
    send(slot(across, x), None, device(y, right))
    send(slot(across, x), None, device(y, left))
    arrive(slot(across, left), None)
    send(slot(across, left), 0, device(y, right))
    arrive(slot(across, right), None)
    send(slot(across, right), 1, device(y, left))
    for yy in (y, across):
        arrive(slot(yy, x + 2), 0)
        arrive(slot(yy, x + 2), 1)
    own.wait()
    for copy in sends:
        copy.wait_send()


def all_gather_rows(piece, n_row):
    n_x = n_row // 2
    assert n_x == 4
    return pl.pallas_call(
        functools.partial(gather_kernel, n_x),
        out_shape=jax.ShapeDtypeStruct((n_row,) + piece.shape, piece.dtype),
        in_specs=[pl.BlockSpec(memory_space=pltpu.VMEM)],
        out_specs=pl.BlockSpec(memory_space=pl.ANY),
        scratch_shapes=[
            pltpu.SemaphoreType.DMA(()),
            pltpu.SemaphoreType.DMA((9,)),
            pltpu.SemaphoreType.DMA((n_row, 2)),
        ],
        compiler_params=pltpu.CompilerParams(collective_id=1, has_side_effects=True),
    )(piece)


def parts_kernel(n_lag, rows_ref, cols_ref, count_ref, lag_ref, hist_ref, tiles_ref, out_ref):
    lag = pl.program_id(0)
    slots = tiles_ref.shape[1]
    side = tiles_ref.shape[2]
    halves = hist_ref.shape[3] // side

    @pl.when(lag == 0)
    def _():
        out_ref[...] = jnp.zeros_like(out_ref)

    for k in range(slots):
        @pl.when(k < count_ref[lag])
        def _():
            col = cols_ref[lag, k]
            row = rows_ref[lag, k]
            both = hist_ref[col // halves, 0]
            history = jnp.where(col % halves == 0, both[:, :side], both[:, side:])
            contrib = lax.dot_general(
                history, tiles_ref[0, k], (((1,), (1,)), ((), ())),
                preferred_element_type=jnp.float32,
            )
            half = jnp.where(row % n_lag == lag_ref[0], 0, 1)
            out_ref[half, row // n_lag] += contrib


def stress_parts(history, tiles, rows, cols, count, n_col, n_lag):
    n_row, lags, sims, held = history.shape
    _, slots, side, _ = tiles.shape
    lag = lax.axis_index("lag").astype(jnp.int32).reshape(1)
    grid_spec = pltpu.PrefetchScalarGridSpec(
        num_scalar_prefetch=4,
        grid=(lags,),
        in_specs=[
            pl.BlockSpec((n_row, 1, sims, held), lambda l, *_: (0, l, 0, 0)),
            pl.BlockSpec((1, slots, side, side), lambda l, *_: (l, 0, 0, 0)),
        ],
        out_specs=pl.BlockSpec((2, n_col, sims, side), lambda l, *_: (0, 0, 0, 0)),
    )
    return pl.pallas_call(
        functools.partial(parts_kernel, n_lag),
        out_shape=jax.ShapeDtypeStruct((2, n_col, sims, side), jnp.float32),
        grid_spec=grid_spec,
        compiler_params=pltpu.CompilerParams(vmem_limit_bytes=48 * 1024 * 1024),
    )(rows, cols, count, lag, history, tiles)


def local(
    n_row,
    n_col,
    n_lag,
    history,
    kernel_tiles,
    tile_rows,
    tile_cols,
    tile_count,
    base_stress,
    prev_rate,
    direct_effect,
    state_var,
):
    gathered = all_gather_rows(history[:, 0], n_row)
    tile_side = kernel_tiles.shape[4]
    parts = stress_parts(gathered, kernel_tiles[0, 0], tile_rows[0, 0],
                         tile_cols[0, 0], tile_count[0, 0], n_col, n_lag)
    own, other = parts[0], parts[1]
    from_partner = lax.ppermute(other, "lag", perm=[(0, 1), (1, 0)])
    stress_change = reduce_scatter(own + from_partner, n_col)
    driving = base_stress + stress_change
    factor = jnp.exp(state_var) / 2.0
    velocity = prev_rate
    for step in range(NEWTON):
        scaled = velocity * factor
        misfit = direct_effect * inverse_sinh(scaled) + 0.5 * velocity - driving
        slope = direct_effect * factor / jnp.sqrt(1.0 + scaled * scaled) + 0.5
        velocity = velocity - misfit / slope
    return (stress_change, velocity)


def solution(mesh):
    return jax.shard_map(
        functools.partial(local, mesh.shape["row"], mesh.shape["col"], mesh.shape["lag"]),
        mesh=mesh,
        in_specs=(
            P("lag", "col", None, "row"),
            P("row", "col", "lag", None, None, None),
            P("row", "col", "lag", None),
            P("row", "col", "lag", None),
            P("row", "col", "lag"),
            P(None, ("row", "col", "lag")),
            P(None, ("row", "col", "lag")),
            P(None, ("row", "col", "lag")),
            P(None, ("row", "col", "lag")),
        ),
        out_specs=(P(None, ("row", "col", "lag")), P(None, ("row", "col", "lag"))),
        check_vma=False,
    )
```

```python
import functools

import jax
import jax.numpy as jnp
from jax import lax
from jax.experimental import pallas as pl
from jax.experimental.pallas import tpu as pltpu
from jax.sharding import PartitionSpec as P

NEWTON = 4
MESH = pl.DeviceIdType.MESH


def inverse_sinh(value):
    magnitude = jnp.abs(value)
    return jnp.sign(value) * jnp.log(magnitude + jnp.sqrt(1.0 + magnitude * magnitude))


def ring_kernel(n_z, n_pieces, part_ref, out_ref, recv, forward, final, cross,
                send_sem, recv_sem, cross_sem):
    row = lax.axis_index("row")
    col = lax.axis_index("col")
    lag = lax.axis_index("lag")
    z = col // 2
    y_hi = col % 2
    up = lax.rem(z + 1, n_z)
    down = lax.rem(z + n_z - 1, n_z)
    rows = part_ref.shape[1] // n_pieces
    longer = n_z // 2
    shorter = n_z - 1 - longer

    def device(zz, yy):
        return (row, zz * 2 + yy, lag)

    def length(way, side):
        return longer if way == side else shorter

    barrier = pltpu.get_barrier_semaphore()
    for peer in (device(up, y_hi), device(down, y_hi), device(z, 1 - y_hi)):
        pl.semaphore_signal(barrier, inc=1, device_id=peer, device_id_type=MESH)
    pl.semaphore_wait(barrier, 3)

    copies = {}
    for step in range(longer):
        for piece in range(n_pieces):
            span = pl.ds(piece * rows, rows)
            for side in range(2):
                for way in range(2):
                    chain = length(way, side)
                    if step >= chain:
                        continue
                    if side == 0:
                        target = lax.rem(z + chain - step, n_z)
                        dest = device(up, y_hi)
                    else:
                        target = lax.rem(z + n_z - chain + step, n_z)
                        dest = device(down, y_hi)
                    block = target * 2 + way
                    if step == 0:
                        source = part_ref.at[block, span]
                    else:
                        copies[side, way, step - 1, piece].wait_recv()
                        forward[side, way, step, piece] = (
                            recv[side, way, step - 1, piece] + part_ref[block, span]
                        )
                        source = forward.at[side, way, step, piece]
                    copy = pltpu.make_async_remote_copy(
                        src_ref=source,
                        dst_ref=recv.at[side, way, step, piece],
                        send_sem=send_sem.at[side, way, step, piece],
                        recv_sem=recv_sem.at[side, way, step, piece],
                        device_id=dest,
                        device_id_type=MESH,
                    )
                    copy.start()
                    copies[side, way, step, piece] = copy

    handoffs = []
    for piece in range(n_pieces):
        span = pl.ds(piece * rows, rows)
        for way in range(2):
            total = part_ref[z * 2 + way, span]
            for side in range(2):
                last = length(way, side) - 1
                copies[side, way, last, piece].wait_recv()
                total = total + recv[side, way, last, piece]
            final[way, piece] = total
        handoff = pltpu.make_async_remote_copy(
            src_ref=final.at[1 - y_hi, piece],
            dst_ref=cross.at[piece],
            send_sem=cross_sem.at[0, piece],
            recv_sem=cross_sem.at[1, piece],
            device_id=device(z, 1 - y_hi),
            device_id_type=MESH,
        )
        handoff.start()
        handoffs.append(handoff)
    for piece in range(n_pieces):
        handoffs[piece].wait_recv()
        out_ref[pl.ds(piece * rows, rows), :] = final[y_hi, piece] + cross[piece]
    for handoff in handoffs:
        handoff.wait_send()
    for copy in copies.values():
        copy.wait_send()


def reduce_scatter(part, n_col, n_pieces=4):
    group, sims, tile = part.shape
    n_z = n_col // 2
    longer = n_z // 2
    rows = sims // n_pieces
    return pl.pallas_call(
        functools.partial(ring_kernel, n_z, n_pieces),
        out_shape=jax.ShapeDtypeStruct((sims, tile), jnp.float32),
        in_specs=[pl.BlockSpec(memory_space=pltpu.VMEM)],
        out_specs=pl.BlockSpec(memory_space=pltpu.VMEM),
        scratch_shapes=[
            pltpu.VMEM((2, 2, longer, n_pieces, rows, tile), jnp.float32),
            pltpu.VMEM((2, 2, longer, n_pieces, rows, tile), jnp.float32),
            pltpu.VMEM((2, n_pieces, rows, tile), jnp.float32),
            pltpu.VMEM((n_pieces, rows, tile), jnp.float32),
            pltpu.SemaphoreType.DMA((2, 2, longer, n_pieces)),
            pltpu.SemaphoreType.DMA((2, 2, longer, n_pieces)),
            pltpu.SemaphoreType.DMA((2, n_pieces)),
        ],
        compiler_params=pltpu.CompilerParams(
            collective_id=0, has_side_effects=True, vmem_limit_bytes=48 * 1024 * 1024
        ),
    )(part)


def gather_kernel(n_x, piece_ref, out_ref, local_sem, send_sem, recv_sem):
    me = lax.axis_index("row")
    col = lax.axis_index("col")
    lag = lax.axis_index("lag")
    y = me // n_x
    x = me % n_x
    right = x + 1
    left = x + n_x - 1
    across = 1 - y
    half = piece_ref.shape[0] // 2

    def slot(yy, xx):
        return yy * n_x + lax.rem(xx, n_x)

    def device(yy, xx):
        return (slot(yy, xx), col, lag)

    def region(index, part):
        if part is None:
            return out_ref.at[index], recv_sem.at[index, 0]
        return out_ref.at[index, pl.ds(part * half, half)], recv_sem.at[index, part]

    barrier = pltpu.get_barrier_semaphore()
    for peer in (device(y, right), device(y, left), device(across, x)):
        pl.semaphore_signal(barrier, inc=1, device_id=peer, device_id_type=MESH)
    pl.semaphore_wait(barrier, 3)

    mine = slot(y, x)
    own = pltpu.make_async_copy(piece_ref, out_ref.at[mine], local_sem)
    own.start()
    sends = []

    def send(index, part, dest, from_input=False):
        target, sem = region(index, part)
        if from_input:
            source = piece_ref
        else:
            source = region(index, part)[0]
        copy = pltpu.make_async_remote_copy(
            src_ref=source,
            dst_ref=target,
            send_sem=send_sem.at[len(sends)],
            recv_sem=sem,
            device_id=dest,
            device_id_type=MESH,
        )
        copy.start()
        sends.append(copy)

    def arrive(index, part):
        target, sem = region(index, part)
        source = piece_ref if part is None else piece_ref.at[pl.ds(part * half, half)]
        pltpu.make_async_remote_copy(
            src_ref=source,
            dst_ref=target,
            send_sem=send_sem.at[0],
            recv_sem=sem,
            device_id=device(y, right),
            device_id_type=MESH,
        ).wait_recv()

    send(mine, None, device(y, right), from_input=True)
    send(mine, None, device(y, left), from_input=True)
    send(mine, None, device(across, x), from_input=True)
    arrive(slot(y, left), None)
    send(slot(y, left), 0, device(y, right))
    arrive(slot(y, right), None)
    send(slot(y, right), 1, device(y, left))
    arrive(slot(across, x), None)
    send(slot(across, x), None, device(y, right))
    send(slot(across, x), None, device(y, left))
    arrive(slot(across, left), None)
    send(slot(across, left), 0, device(y, right))
    arrive(slot(across, right), None)
    send(slot(across, right), 1, device(y, left))
    for yy in (y, across):
        arrive(slot(yy, x + 2), 0)
        arrive(slot(yy, x + 2), 1)
    own.wait()
    for copy in sends:
        copy.wait_send()


def all_gather_rows(piece, n_row):
    n_x = n_row // 2
    assert n_x == 4
    return pl.pallas_call(
        functools.partial(gather_kernel, n_x),
        out_shape=jax.ShapeDtypeStruct((n_row,) + piece.shape, piece.dtype),
        in_specs=[pl.BlockSpec(memory_space=pltpu.VMEM)],
        out_specs=pl.BlockSpec(memory_space=pl.ANY),
        scratch_shapes=[
            pltpu.SemaphoreType.DMA(()),
            pltpu.SemaphoreType.DMA((9,)),
            pltpu.SemaphoreType.DMA((n_row, 2)),
        ],
        compiler_params=pltpu.CompilerParams(collective_id=1, has_side_effects=True),
    )(piece)


def parts_kernel(n_lag, rows_ref, cols_ref, count_ref, lag_ref, hist_ref, tiles_ref, out_ref):
    lag = pl.program_id(0)
    slots = tiles_ref.shape[1]
    side = tiles_ref.shape[2]
    halves = hist_ref.shape[3] // side

    @pl.when(lag == 0)
    def _():
        out_ref[...] = jnp.zeros_like(out_ref)

    for k in range(slots):
        @pl.when(k < count_ref[lag])
        def _():
            col = cols_ref[lag, k]
            row = rows_ref[lag, k]
            both = hist_ref[col // halves, 0]
            history = jnp.where(col % halves == 0, both[:, :side], both[:, side:])
            contrib = lax.dot_general(
                history, tiles_ref[0, k], (((1,), (1,)), ((), ())),
                preferred_element_type=jnp.float32,
            )
            half = jnp.where(row % n_lag == lag_ref[0], 0, 1)
            out_ref[half, row // n_lag] += contrib


def stress_parts(history, tiles, rows, cols, count, n_col, n_lag):
    n_row, lags, sims, held = history.shape
    _, slots, side, _ = tiles.shape
    lag = lax.axis_index("lag").astype(jnp.int32).reshape(1)
    grid_spec = pltpu.PrefetchScalarGridSpec(
        num_scalar_prefetch=4,
        grid=(lags,),
        in_specs=[
            pl.BlockSpec((n_row, 1, sims, held), lambda l, *_: (0, l, 0, 0)),
            pl.BlockSpec((1, slots, side, side), lambda l, *_: (l, 0, 0, 0)),
        ],
        out_specs=pl.BlockSpec((2, n_col, sims, side), lambda l, *_: (0, 0, 0, 0)),
    )
    return pl.pallas_call(
        functools.partial(parts_kernel, n_lag),
        out_shape=jax.ShapeDtypeStruct((2, n_col, sims, side), jnp.float32),
        grid_spec=grid_spec,
        compiler_params=pltpu.CompilerParams(vmem_limit_bytes=48 * 1024 * 1024),
    )(rows, cols, count, lag, history, tiles)


def local(
    n_row,
    n_col,
    n_lag,
    history,
    kernel_tiles,
    tile_rows,
    tile_cols,
    tile_count,
    base_stress,
    prev_rate,
    direct_effect,
    state_var,
):
    gathered = all_gather_rows(history[:, 0], n_row)
    tile_side = kernel_tiles.shape[4]
    parts = stress_parts(gathered, kernel_tiles[0, 0], tile_rows[0, 0],
                         tile_cols[0, 0], tile_count[0, 0], n_col, n_lag)
    own, other = parts[0], parts[1]
    from_partner = lax.ppermute(other, "lag", perm=[(0, 1), (1, 0)])
    stress_change = reduce_scatter(own + from_partner, n_col)
    driving = base_stress + stress_change
    factor = jnp.exp(state_var) / 2.0
    velocity = prev_rate
    for step in range(NEWTON):
        scaled = velocity * factor
        misfit = direct_effect * inverse_sinh(scaled) + 0.5 * velocity - driving
        slope = direct_effect * factor / jnp.sqrt(1.0 + scaled * scaled) + 0.5
        velocity = velocity - misfit / slope
    return (stress_change, velocity)


def solution(mesh):
    return jax.shard_map(
        functools.partial(local, mesh.shape["row"], mesh.shape["col"], mesh.shape["lag"]),
        mesh=mesh,
        in_specs=(
            P("lag", "col", None, "row"),
            P("row", "col", "lag", None, None, None),
            P("row", "col", "lag", None),
            P("row", "col", "lag", None),
            P("row", "col", "lag"),
            P(None, ("row", "col", "lag")),
            P(None, ("row", "col", "lag")),
            P(None, ("row", "col", "lag")),
            P(None, ("row", "col", "lag")),
        ),
        out_specs=(P(None, ("row", "col", "lag")), P(None, ("row", "col", "lag"))),
        check_vma=False,
    )
```

```python
import functools

import jax
import jax.numpy as jnp
from jax import lax
from jax.experimental import pallas as pl
from jax.experimental.pallas import tpu as pltpu
from jax.sharding import PartitionSpec as P

NEWTON = 4
MESH = pl.DeviceIdType.MESH


def inverse_sinh(value):
    magnitude = jnp.abs(value)
    return jnp.sign(value) * jnp.log(magnitude + jnp.sqrt(1.0 + magnitude * magnitude))


def ring_kernel(n_z, n_pieces, part_ref, out_ref, recv, forward, final, cross, mate,
                send_sem, recv_sem, cross_sem, mate_sem):
    row = lax.axis_index("row")
    col = lax.axis_index("col")
    lag = lax.axis_index("lag")
    z = col // 2
    y_hi = col % 2
    up = lax.rem(z + 1, n_z)
    down = lax.rem(z + n_z - 1, n_z)
    rows = part_ref.shape[2] // n_pieces
    longer = n_z // 2
    shorter = n_z - 1 - longer

    def device(zz, yy):
        return (row, zz * 2 + yy, lag)

    def length(way, side):
        return longer if way == side else shorter

    partner = (row, col, 1 - lag)
    barrier = pltpu.get_barrier_semaphore()
    for peer in (device(up, y_hi), device(down, y_hi), device(z, 1 - y_hi), partner):
        pl.semaphore_signal(barrier, inc=1, device_id=peer, device_id_type=MESH)
    pl.semaphore_wait(barrier, 4)

    def chain_block(step, side, way):
        chain = length(way, side)
        if side == 0:
            target = lax.rem(z + chain - step, n_z)
        else:
            target = lax.rem(z + n_z - chain + step, n_z)
        return target * 2 + way

    order = []
    for step in range(longer):
        for side in range(2):
            for way in range(2):
                if step < length(way, side):
                    order.append(chain_block(step, side, way))
    order += [z * 2 + way for way in range(2)]
    handed = {}
    for index, block in enumerate(order):
        copy = pltpu.make_async_remote_copy(
            src_ref=part_ref.at[1, block],
            dst_ref=mate.at[block],
            send_sem=mate_sem.at[0, index],
            recv_sem=mate_sem.at[1, index],
            device_id=partner,
            device_id_type=MESH,
        )
        copy.start()
        handed[index] = copy
    ready = set()

    def own(index, span):
        if index not in ready:
            handed[index].wait_recv()
            ready.add(index)
        block = order[index]
        return part_ref[0, block, span] + mate[block, span]

    copies = {}
    for step in range(longer):
        for piece in range(n_pieces):
            span = pl.ds(piece * rows, rows)
            for side in range(2):
                for way in range(2):
                    if step >= length(way, side):
                        continue
                    dest = device(up, y_hi) if side == 0 else device(down, y_hi)
                    index = len([1 for st in range(step) for sd in range(2) for w in range(2)
                                 if st < length(w, sd)])
                    index += len([1 for sd in range(side) for w in range(2)
                                  if step < length(w, sd)])
                    index += len([1 for w in range(way) if step < length(w, side)])
                    if step == 0:
                        forward[side, way, step, piece] = own(index, span)
                    else:
                        copies[side, way, step - 1, piece].wait_recv()
                        forward[side, way, step, piece] = (
                            recv[side, way, step - 1, piece] + own(index, span)
                        )
                    source = forward.at[side, way, step, piece]
                    copy = pltpu.make_async_remote_copy(
                        src_ref=source,
                        dst_ref=recv.at[side, way, step, piece],
                        send_sem=send_sem.at[side, way, step, piece],
                        recv_sem=recv_sem.at[side, way, step, piece],
                        device_id=dest,
                        device_id_type=MESH,
                    )
                    copy.start()
                    copies[side, way, step, piece] = copy

    handoffs = []
    for piece in range(n_pieces):
        span = pl.ds(piece * rows, rows)
        for way in range(2):
            total = own(len(order) - 2 + way, span)
            for side in range(2):
                last = length(way, side) - 1
                copies[side, way, last, piece].wait_recv()
                total = total + recv[side, way, last, piece]
            final[way, piece] = total
        handoff = pltpu.make_async_remote_copy(
            src_ref=final.at[1 - y_hi, piece],
            dst_ref=cross.at[piece],
            send_sem=cross_sem.at[0, piece],
            recv_sem=cross_sem.at[1, piece],
            device_id=device(z, 1 - y_hi),
            device_id_type=MESH,
        )
        handoff.start()
        handoffs.append(handoff)
    for piece in range(n_pieces):
        handoffs[piece].wait_recv()
        out_ref[pl.ds(piece * rows, rows), :] = final[y_hi, piece] + cross[piece]
    for handoff in handoffs:
        handoff.wait_send()
    for copy in copies.values():
        copy.wait_send()
    for copy in handed.values():
        copy.wait_send()


def reduce_scatter(part, n_col, n_pieces=4):
    _, group, sims, tile = part.shape
    n_z = n_col // 2
    longer = n_z // 2
    rows = sims // n_pieces
    return pl.pallas_call(
        functools.partial(ring_kernel, n_z, n_pieces),
        out_shape=jax.ShapeDtypeStruct((sims, tile), jnp.float32),
        in_specs=[pl.BlockSpec(memory_space=pltpu.VMEM)],
        out_specs=pl.BlockSpec(memory_space=pltpu.VMEM),
        scratch_shapes=[
            pltpu.VMEM((2, 2, longer, n_pieces, rows, tile), jnp.float32),
            pltpu.VMEM((2, 2, longer, n_pieces, rows, tile), jnp.float32),
            pltpu.VMEM((2, n_pieces, rows, tile), jnp.float32),
            pltpu.VMEM((n_pieces, rows, tile), jnp.float32),
            pltpu.VMEM((group, sims, tile), jnp.float32),
            pltpu.SemaphoreType.DMA((2, 2, longer, n_pieces)),
            pltpu.SemaphoreType.DMA((2, 2, longer, n_pieces)),
            pltpu.SemaphoreType.DMA((2, n_pieces)),
            pltpu.SemaphoreType.DMA((2, group)),
        ],
        compiler_params=pltpu.CompilerParams(
            collective_id=0, has_side_effects=True, vmem_limit_bytes=48 * 1024 * 1024
        ),
    )(part)


def gather_kernel(n_x, piece_ref, out_ref, local_sem, send_sem, recv_sem):
    me = lax.axis_index("row")
    col = lax.axis_index("col")
    lag = lax.axis_index("lag")
    y = me // n_x
    x = me % n_x
    right = x + 1
    left = x + n_x - 1
    across = 1 - y
    half = piece_ref.shape[0] // 2

    def slot(yy, xx):
        return yy * n_x + lax.rem(xx, n_x)

    def device(yy, xx):
        return (slot(yy, xx), col, lag)

    def region(index, part):
        if part is None:
            return out_ref.at[index], recv_sem.at[index, 0]
        return out_ref.at[index, pl.ds(part * half, half)], recv_sem.at[index, part]

    barrier = pltpu.get_barrier_semaphore()
    for peer in (device(y, right), device(y, left), device(across, x)):
        pl.semaphore_signal(barrier, inc=1, device_id=peer, device_id_type=MESH)
    pl.semaphore_wait(barrier, 3)

    mine = slot(y, x)
    own = pltpu.make_async_copy(piece_ref, out_ref.at[mine], local_sem)
    own.start()
    sends = []

    def send(index, part, dest, from_input=False):
        target, sem = region(index, part)
        if from_input:
            source = piece_ref
        else:
            source = region(index, part)[0]
        copy = pltpu.make_async_remote_copy(
            src_ref=source,
            dst_ref=target,
            send_sem=send_sem.at[len(sends)],
            recv_sem=sem,
            device_id=dest,
            device_id_type=MESH,
        )
        copy.start()
        sends.append(copy)

    def arrive(index, part):
        target, sem = region(index, part)
        source = piece_ref if part is None else piece_ref.at[pl.ds(part * half, half)]
        pltpu.make_async_remote_copy(
            src_ref=source,
            dst_ref=target,
            send_sem=send_sem.at[0],
            recv_sem=sem,
            device_id=device(y, right),
            device_id_type=MESH,
        ).wait_recv()

    send(mine, None, device(y, right), from_input=True)
    send(mine, None, device(y, left), from_input=True)
    send(mine, None, device(across, x), from_input=True)
    arrive(slot(y, left), None)
    send(slot(y, left), 0, device(y, right))
    arrive(slot(y, right), None)
    send(slot(y, right), 1, device(y, left))
    arrive(slot(across, x), None)
    send(slot(across, x), None, device(y, right))
    send(slot(across, x), None, device(y, left))
    arrive(slot(across, left), None)
    send(slot(across, left), 0, device(y, right))
    arrive(slot(across, right), None)
    send(slot(across, right), 1, device(y, left))
    for yy in (y, across):
        arrive(slot(yy, x + 2), 0)
        arrive(slot(yy, x + 2), 1)
    own.wait()
    for copy in sends:
        copy.wait_send()


def all_gather_rows(piece, n_row):
    n_x = n_row // 2
    assert n_x == 4
    return pl.pallas_call(
        functools.partial(gather_kernel, n_x),
        out_shape=jax.ShapeDtypeStruct((n_row,) + piece.shape, piece.dtype),
        in_specs=[pl.BlockSpec(memory_space=pltpu.VMEM)],
        out_specs=pl.BlockSpec(memory_space=pl.ANY),
        scratch_shapes=[
            pltpu.SemaphoreType.DMA(()),
            pltpu.SemaphoreType.DMA((9,)),
            pltpu.SemaphoreType.DMA((n_row, 2)),
        ],
        compiler_params=pltpu.CompilerParams(collective_id=1, has_side_effects=True),
    )(piece)


def parts_kernel(n_lag, rows_ref, cols_ref, count_ref, lag_ref, hist_ref, tiles_ref, out_ref):
    lag = pl.program_id(0)
    slots = tiles_ref.shape[1]
    side = tiles_ref.shape[2]
    halves = hist_ref.shape[3] // side

    @pl.when(lag == 0)
    def _():
        out_ref[...] = jnp.zeros_like(out_ref)

    for k in range(slots):
        @pl.when(k < count_ref[lag])
        def _():
            col = cols_ref[lag, k]
            row = rows_ref[lag, k]
            both = hist_ref[col // halves, 0]
            history = jnp.where(col % halves == 0, both[:, :side], both[:, side:])
            contrib = lax.dot_general(
                history, tiles_ref[0, k], (((1,), (1,)), ((), ())),
                preferred_element_type=jnp.float32,
            )
            half = jnp.where(row % n_lag == lag_ref[0], 0, 1)
            out_ref[half, row // n_lag] += contrib


def stress_parts(history, tiles, rows, cols, count, n_col, n_lag):
    n_row, lags, sims, held = history.shape
    _, slots, side, _ = tiles.shape
    lag = lax.axis_index("lag").astype(jnp.int32).reshape(1)
    grid_spec = pltpu.PrefetchScalarGridSpec(
        num_scalar_prefetch=4,
        grid=(lags,),
        in_specs=[
            pl.BlockSpec((n_row, 1, sims, held), lambda l, *_: (0, l, 0, 0)),
            pl.BlockSpec((1, slots, side, side), lambda l, *_: (l, 0, 0, 0)),
        ],
        out_specs=pl.BlockSpec((2, n_col, sims, side), lambda l, *_: (0, 0, 0, 0)),
    )
    return pl.pallas_call(
        functools.partial(parts_kernel, n_lag),
        out_shape=jax.ShapeDtypeStruct((2, n_col, sims, side), jnp.float32),
        grid_spec=grid_spec,
        compiler_params=pltpu.CompilerParams(vmem_limit_bytes=48 * 1024 * 1024),
    )(rows, cols, count, lag, history, tiles)


def local(
    n_row,
    n_col,
    n_lag,
    history,
    kernel_tiles,
    tile_rows,
    tile_cols,
    tile_count,
    base_stress,
    prev_rate,
    direct_effect,
    state_var,
):
    gathered = all_gather_rows(history[:, 0], n_row)
    tile_side = kernel_tiles.shape[4]
    parts = stress_parts(gathered, kernel_tiles[0, 0], tile_rows[0, 0],
                         tile_cols[0, 0], tile_count[0, 0], n_col, n_lag)
    stress_change = reduce_scatter(parts, n_col)
    driving = base_stress + stress_change
    factor = jnp.exp(state_var) / 2.0
    velocity = prev_rate
    for step in range(NEWTON):
        scaled = velocity * factor
        misfit = direct_effect * inverse_sinh(scaled) + 0.5 * velocity - driving
        slope = direct_effect * factor / jnp.sqrt(1.0 + scaled * scaled) + 0.5
        velocity = velocity - misfit / slope
    return (stress_change, velocity)


def solution(mesh):
    return jax.shard_map(
        functools.partial(local, mesh.shape["row"], mesh.shape["col"], mesh.shape["lag"]),
        mesh=mesh,
        in_specs=(
            P("lag", "col", None, "row"),
            P("row", "col", "lag", None, None, None),
            P("row", "col", "lag", None),
            P("row", "col", "lag", None),
            P("row", "col", "lag"),
            P(None, ("row", "col", "lag")),
            P(None, ("row", "col", "lag")),
            P(None, ("row", "col", "lag")),
            P(None, ("row", "col", "lag")),
        ),
        out_specs=(P(None, ("row", "col", "lag")), P(None, ("row", "col", "lag"))),
        check_vma=False,
    )
```

```python
import functools

import jax
import jax.numpy as jnp
from jax import lax
from jax.experimental import pallas as pl
from jax.experimental.pallas import tpu as pltpu
from jax.sharding import PartitionSpec as P

NEWTON = 4
MESH = pl.DeviceIdType.MESH


def inverse_sinh(value):
    magnitude = jnp.abs(value)
    return jnp.sign(value) * jnp.log(magnitude + jnp.sqrt(1.0 + magnitude * magnitude))


def ring_kernel(n_z, n_pieces, part_ref, out_ref, recv, forward, final, cross, mate,
                send_sem, recv_sem, cross_sem, mate_sem):
    row = lax.axis_index("row")
    col = lax.axis_index("col")
    lag = lax.axis_index("lag")
    z = col // 2
    y_hi = col % 2
    up = lax.rem(z + 1, n_z)
    down = lax.rem(z + n_z - 1, n_z)
    rows = part_ref.shape[2] // n_pieces
    longer = n_z // 2
    shorter = n_z - 1 - longer

    def device(zz, yy):
        return (row, zz * 2 + yy, lag)

    def length(way, side):
        return longer if way == side else shorter

    partner = (row, col, 1 - lag)
    barrier = pltpu.get_barrier_semaphore()
    for peer in (device(up, y_hi), device(down, y_hi), device(z, 1 - y_hi), partner):
        pl.semaphore_signal(barrier, inc=1, device_id=peer, device_id_type=MESH)
    pl.semaphore_wait(barrier, 4)

    def chain_block(step, side, way):
        chain = length(way, side)
        if side == 0:
            target = lax.rem(z + chain - step, n_z)
        else:
            target = lax.rem(z + n_z - chain + step, n_z)
        return target * 2 + way

    order = []
    for step in range(longer):
        for side in range(2):
            for way in range(2):
                if step < length(way, side):
                    order.append(chain_block(step, side, way))
    order += [z * 2 + way for way in range(2)]
    handed = {}
    for index, block in enumerate(order):
        copy = pltpu.make_async_remote_copy(
            src_ref=part_ref.at[1, block],
            dst_ref=mate.at[block],
            send_sem=mate_sem.at[0, index],
            recv_sem=mate_sem.at[1, index],
            device_id=partner,
            device_id_type=MESH,
        )
        copy.start()
        handed[index] = copy
    ready = set()

    def own(index, span):
        if index not in ready:
            handed[index].wait_recv()
            ready.add(index)
        block = order[index]
        return part_ref[0, block, span] + mate[block, span]

    copies = {}
    for step in range(longer):
        for piece in range(n_pieces):
            span = pl.ds(piece * rows, rows)
            for side in range(2):
                for way in range(2):
                    if step >= length(way, side):
                        continue
                    dest = device(up, y_hi) if side == 0 else device(down, y_hi)
                    index = len([1 for st in range(step) for sd in range(2) for w in range(2)
                                 if st < length(w, sd)])
                    index += len([1 for sd in range(side) for w in range(2)
                                  if step < length(w, sd)])
                    index += len([1 for w in range(way) if step < length(w, side)])
                    if step == 0:
                        forward[side, way, step, piece] = own(index, span)
                    else:
                        copies[side, way, step - 1, piece].wait_recv()
                        forward[side, way, step, piece] = (
                            recv[side, way, step - 1, piece] + own(index, span)
                        )
                    source = forward.at[side, way, step, piece]
                    copy = pltpu.make_async_remote_copy(
                        src_ref=source,
                        dst_ref=recv.at[side, way, step, piece],
                        send_sem=send_sem.at[side, way, step, piece],
                        recv_sem=recv_sem.at[side, way, step, piece],
                        device_id=dest,
                        device_id_type=MESH,
                    )
                    copy.start()
                    copies[side, way, step, piece] = copy

    handoffs = []
    for piece in range(n_pieces):
        span = pl.ds(piece * rows, rows)
        for way in range(2):
            total = own(len(order) - 2 + way, span)
            for side in range(2):
                last = length(way, side) - 1
                copies[side, way, last, piece].wait_recv()
                total = total + recv[side, way, last, piece]
            final[way, piece] = total
        handoff = pltpu.make_async_remote_copy(
            src_ref=final.at[1 - y_hi, piece],
            dst_ref=cross.at[piece],
            send_sem=cross_sem.at[0, piece],
            recv_sem=cross_sem.at[1, piece],
            device_id=device(z, 1 - y_hi),
            device_id_type=MESH,
        )
        handoff.start()
        handoffs.append(handoff)
    for piece in range(n_pieces):
        handoffs[piece].wait_recv()
        out_ref[pl.ds(piece * rows, rows), :] = final[y_hi, piece] + cross[piece]
    for handoff in handoffs:
        handoff.wait_send()
    for copy in copies.values():
        copy.wait_send()
    for copy in handed.values():
        copy.wait_send()


def reduce_scatter(part, n_col, n_pieces=8):
    _, group, sims, tile = part.shape
    n_z = n_col // 2
    longer = n_z // 2
    rows = sims // n_pieces
    return pl.pallas_call(
        functools.partial(ring_kernel, n_z, n_pieces),
        out_shape=jax.ShapeDtypeStruct((sims, tile), jnp.float32),
        in_specs=[pl.BlockSpec(memory_space=pltpu.VMEM)],
        out_specs=pl.BlockSpec(memory_space=pltpu.VMEM),
        scratch_shapes=[
            pltpu.VMEM((2, 2, longer, n_pieces, rows, tile), jnp.float32),
            pltpu.VMEM((2, 2, longer, n_pieces, rows, tile), jnp.float32),
            pltpu.VMEM((2, n_pieces, rows, tile), jnp.float32),
            pltpu.VMEM((n_pieces, rows, tile), jnp.float32),
            pltpu.VMEM((group, sims, tile), jnp.float32),
            pltpu.SemaphoreType.DMA((2, 2, longer, n_pieces)),
            pltpu.SemaphoreType.DMA((2, 2, longer, n_pieces)),
            pltpu.SemaphoreType.DMA((2, n_pieces)),
            pltpu.SemaphoreType.DMA((2, group)),
        ],
        compiler_params=pltpu.CompilerParams(
            collective_id=0, has_side_effects=True, vmem_limit_bytes=48 * 1024 * 1024
        ),
    )(part)


def gather_kernel(n_x, piece_ref, out_ref, local_sem, send_sem, recv_sem):
    me = lax.axis_index("row")
    col = lax.axis_index("col")
    lag = lax.axis_index("lag")
    y = me // n_x
    x = me % n_x
    right = x + 1
    left = x + n_x - 1
    across = 1 - y
    half = piece_ref.shape[0] // 2

    def slot(yy, xx):
        return yy * n_x + lax.rem(xx, n_x)

    def device(yy, xx):
        return (slot(yy, xx), col, lag)

    def region(index, part):
        if part is None:
            return out_ref.at[index], recv_sem.at[index, 0]
        return out_ref.at[index, pl.ds(part * half, half)], recv_sem.at[index, part]

    barrier = pltpu.get_barrier_semaphore()
    for peer in (device(y, right), device(y, left), device(across, x)):
        pl.semaphore_signal(barrier, inc=1, device_id=peer, device_id_type=MESH)
    pl.semaphore_wait(barrier, 3)

    mine = slot(y, x)
    own = pltpu.make_async_copy(piece_ref, out_ref.at[mine], local_sem)
    own.start()
    sends = []

    def send(index, part, dest, from_input=False):
        target, sem = region(index, part)
        if from_input:
            source = piece_ref
        else:
            source = region(index, part)[0]
        copy = pltpu.make_async_remote_copy(
            src_ref=source,
            dst_ref=target,
            send_sem=send_sem.at[len(sends)],
            recv_sem=sem,
            device_id=dest,
            device_id_type=MESH,
        )
        copy.start()
        sends.append(copy)

    def arrive(index, part):
        target, sem = region(index, part)
        source = piece_ref if part is None else piece_ref.at[pl.ds(part * half, half)]
        pltpu.make_async_remote_copy(
            src_ref=source,
            dst_ref=target,
            send_sem=send_sem.at[0],
            recv_sem=sem,
            device_id=device(y, right),
            device_id_type=MESH,
        ).wait_recv()

    send(mine, None, device(y, right), from_input=True)
    send(mine, None, device(y, left), from_input=True)
    send(mine, None, device(across, x), from_input=True)
    arrive(slot(y, left), None)
    send(slot(y, left), 0, device(y, right))
    arrive(slot(y, right), None)
    send(slot(y, right), 1, device(y, left))
    arrive(slot(across, x), None)
    send(slot(across, x), None, device(y, right))
    send(slot(across, x), None, device(y, left))
    arrive(slot(across, left), None)
    send(slot(across, left), 0, device(y, right))
    arrive(slot(across, right), None)
    send(slot(across, right), 1, device(y, left))
    for yy in (y, across):
        arrive(slot(yy, x + 2), 0)
        arrive(slot(yy, x + 2), 1)
    own.wait()
    for copy in sends:
        copy.wait_send()


def all_gather_rows(piece, n_row):
    n_x = n_row // 2
    assert n_x == 4
    return pl.pallas_call(
        functools.partial(gather_kernel, n_x),
        out_shape=jax.ShapeDtypeStruct((n_row,) + piece.shape, piece.dtype),
        in_specs=[pl.BlockSpec(memory_space=pltpu.VMEM)],
        out_specs=pl.BlockSpec(memory_space=pl.ANY),
        scratch_shapes=[
            pltpu.SemaphoreType.DMA(()),
            pltpu.SemaphoreType.DMA((9,)),
            pltpu.SemaphoreType.DMA((n_row, 2)),
        ],
        compiler_params=pltpu.CompilerParams(collective_id=1, has_side_effects=True),
    )(piece)


def parts_kernel(n_lag, rows_ref, cols_ref, count_ref, lag_ref, hist_ref, tiles_ref, out_ref):
    lag = pl.program_id(0)
    slots = tiles_ref.shape[1]
    side = tiles_ref.shape[2]
    halves = hist_ref.shape[3] // side

    @pl.when(lag == 0)
    def _():
        out_ref[...] = jnp.zeros_like(out_ref)

    for k in range(slots):
        @pl.when(k < count_ref[lag])
        def _():
            col = cols_ref[lag, k]
            row = rows_ref[lag, k]
            both = hist_ref[col // halves, 0]
            history = jnp.where(col % halves == 0, both[:, :side], both[:, side:])
            contrib = lax.dot_general(
                history, tiles_ref[0, k], (((1,), (1,)), ((), ())),
                preferred_element_type=jnp.float32,
            )
            half = jnp.where(row % n_lag == lag_ref[0], 0, 1)
            out_ref[half, row // n_lag] += contrib


def stress_parts(history, tiles, rows, cols, count, n_col, n_lag):
    n_row, lags, sims, held = history.shape
    _, slots, side, _ = tiles.shape
    lag = lax.axis_index("lag").astype(jnp.int32).reshape(1)
    grid_spec = pltpu.PrefetchScalarGridSpec(
        num_scalar_prefetch=4,
        grid=(lags,),
        in_specs=[
            pl.BlockSpec((n_row, 1, sims, held), lambda l, *_: (0, l, 0, 0)),
            pl.BlockSpec((1, slots, side, side), lambda l, *_: (l, 0, 0, 0)),
        ],
        out_specs=pl.BlockSpec((2, n_col, sims, side), lambda l, *_: (0, 0, 0, 0)),
    )
    return pl.pallas_call(
        functools.partial(parts_kernel, n_lag),
        out_shape=jax.ShapeDtypeStruct((2, n_col, sims, side), jnp.float32),
        grid_spec=grid_spec,
        compiler_params=pltpu.CompilerParams(vmem_limit_bytes=48 * 1024 * 1024),
    )(rows, cols, count, lag, history, tiles)


def local(
    n_row,
    n_col,
    n_lag,
    history,
    kernel_tiles,
    tile_rows,
    tile_cols,
    tile_count,
    base_stress,
    prev_rate,
    direct_effect,
    state_var,
):
    gathered = all_gather_rows(history[:, 0], n_row)
    tile_side = kernel_tiles.shape[4]
    parts = stress_parts(gathered, kernel_tiles[0, 0], tile_rows[0, 0],
                         tile_cols[0, 0], tile_count[0, 0], n_col, n_lag)
    stress_change = reduce_scatter(parts, n_col)
    driving = base_stress + stress_change
    factor = jnp.exp(state_var) / 2.0
    velocity = prev_rate
    for step in range(NEWTON):
        scaled = velocity * factor
        misfit = direct_effect * inverse_sinh(scaled) + 0.5 * velocity - driving
        slope = direct_effect * factor / jnp.sqrt(1.0 + scaled * scaled) + 0.5
        velocity = velocity - misfit / slope
    return (stress_change, velocity)


def solution(mesh):
    return jax.shard_map(
        functools.partial(local, mesh.shape["row"], mesh.shape["col"], mesh.shape["lag"]),
        mesh=mesh,
        in_specs=(
            P("lag", "col", None, "row"),
            P("row", "col", "lag", None, None, None),
            P("row", "col", "lag", None),
            P("row", "col", "lag", None),
            P("row", "col", "lag"),
            P(None, ("row", "col", "lag")),
            P(None, ("row", "col", "lag")),
            P(None, ("row", "col", "lag")),
            P(None, ("row", "col", "lag")),
        ),
        out_specs=(P(None, ("row", "col", "lag")), P(None, ("row", "col", "lag"))),
        check_vma=False,
    )
```

```python
import functools

import jax
import jax.numpy as jnp
from jax import lax
from jax.experimental import pallas as pl
from jax.experimental.pallas import tpu as pltpu
from jax.sharding import PartitionSpec as P

NEWTON = 4
MESH = pl.DeviceIdType.MESH


def inverse_sinh(value):
    magnitude = jnp.abs(value)
    return jnp.sign(value) * jnp.log(magnitude + jnp.sqrt(1.0 + magnitude * magnitude))


def ring_kernel(n_z, n_pieces, part_ref, out_ref, recv, forward, final, cross, mate,
                send_sem, recv_sem, cross_sem, mate_sem):
    row = lax.axis_index("row")
    col = lax.axis_index("col")
    lag = lax.axis_index("lag")
    z = col // 2
    y_hi = col % 2
    up = lax.rem(z + 1, n_z)
    down = lax.rem(z + n_z - 1, n_z)
    rows = part_ref.shape[2] // n_pieces
    longer = n_z // 2
    shorter = n_z - 1 - longer

    def device(zz, yy):
        return (row, zz * 2 + yy, lag)

    def length(way, side):
        return longer if way == side else shorter

    partner = (row, col, 1 - lag)
    barrier = pltpu.get_barrier_semaphore()
    for peer in (device(up, y_hi), device(down, y_hi), device(z, 1 - y_hi), partner):
        pl.semaphore_signal(barrier, inc=1, device_id=peer, device_id_type=MESH)
    pl.semaphore_wait(barrier, 4)

    def chain_block(step, side, way):
        chain = length(way, side)
        if side == 0:
            target = lax.rem(z + chain - step, n_z)
        else:
            target = lax.rem(z + n_z - chain + step, n_z)
        return target * 2 + way

    order = []
    for step in range(longer):
        for side in range(2):
            for way in range(2):
                if step < length(way, side):
                    order.append(chain_block(step, side, way))
    order += [z * 2 + way for way in range(2)]
    handed = {}
    for index, block in enumerate(order):
        copy = pltpu.make_async_remote_copy(
            src_ref=part_ref.at[1, block],
            dst_ref=mate.at[block],
            send_sem=mate_sem.at[0, index],
            recv_sem=mate_sem.at[1, index],
            device_id=partner,
            device_id_type=MESH,
        )
        copy.start()
        handed[index] = copy
    ready = set()

    def own(index, span):
        if index not in ready:
            handed[index].wait_recv()
            ready.add(index)
        block = order[index]
        return part_ref[0, block, span] + mate[block, span]

    copies = {}
    for step in range(longer):
        for piece in range(n_pieces):
            span = pl.ds(piece * rows, rows)
            for side in range(2):
                for way in range(2):
                    if step >= length(way, side):
                        continue
                    dest = device(up, y_hi) if side == 0 else device(down, y_hi)
                    index = len([1 for st in range(step) for sd in range(2) for w in range(2)
                                 if st < length(w, sd)])
                    index += len([1 for sd in range(side) for w in range(2)
                                  if step < length(w, sd)])
                    index += len([1 for w in range(way) if step < length(w, side)])
                    if step == 0:
                        forward[side, way, step, piece] = own(index, span)
                    else:
                        copies[side, way, step - 1, piece].wait_recv()
                        forward[side, way, step, piece] = (
                            recv[side, way, step - 1, piece] + own(index, span)
                        )
                    source = forward.at[side, way, step, piece]
                    copy = pltpu.make_async_remote_copy(
                        src_ref=source,
                        dst_ref=recv.at[side, way, step, piece],
                        send_sem=send_sem.at[side, way, step, piece],
                        recv_sem=recv_sem.at[side, way, step, piece],
                        device_id=dest,
                        device_id_type=MESH,
                    )
                    copy.start()
                    copies[side, way, step, piece] = copy

    handoffs = []
    for piece in range(n_pieces):
        span = pl.ds(piece * rows, rows)
        for way in range(2):
            total = own(len(order) - 2 + way, span)
            for side in range(2):
                last = length(way, side) - 1
                copies[side, way, last, piece].wait_recv()
                total = total + recv[side, way, last, piece]
            final[way, piece] = total
        handoff = pltpu.make_async_remote_copy(
            src_ref=final.at[1 - y_hi, piece],
            dst_ref=cross.at[piece],
            send_sem=cross_sem.at[0, piece],
            recv_sem=cross_sem.at[1, piece],
            device_id=device(z, 1 - y_hi),
            device_id_type=MESH,
        )
        handoff.start()
        handoffs.append(handoff)
    for piece in range(n_pieces):
        handoffs[piece].wait_recv()
        out_ref[pl.ds(piece * rows, rows), :] = final[y_hi, piece] + cross[piece]
    for handoff in handoffs:
        handoff.wait_send()
    for copy in copies.values():
        copy.wait_send()
    for copy in handed.values():
        copy.wait_send()


def reduce_scatter(part, n_col, n_pieces=4):
    _, group, sims, tile = part.shape
    n_z = n_col // 2
    longer = n_z // 2
    rows = sims // n_pieces
    return pl.pallas_call(
        functools.partial(ring_kernel, n_z, n_pieces),
        out_shape=jax.ShapeDtypeStruct((sims, tile), jnp.float32),
        in_specs=[pl.BlockSpec(memory_space=pltpu.VMEM)],
        out_specs=pl.BlockSpec(memory_space=pltpu.VMEM),
        scratch_shapes=[
            pltpu.VMEM((2, 2, longer, n_pieces, rows, tile), jnp.float32),
            pltpu.VMEM((2, 2, longer, n_pieces, rows, tile), jnp.float32),
            pltpu.VMEM((2, n_pieces, rows, tile), jnp.float32),
            pltpu.VMEM((n_pieces, rows, tile), jnp.float32),
            pltpu.VMEM((group, sims, tile), jnp.float32),
            pltpu.SemaphoreType.DMA((2, 2, longer, n_pieces)),
            pltpu.SemaphoreType.DMA((2, 2, longer, n_pieces)),
            pltpu.SemaphoreType.DMA((2, n_pieces)),
            pltpu.SemaphoreType.DMA((2, group)),
        ],
        compiler_params=pltpu.CompilerParams(
            collective_id=0, has_side_effects=True, vmem_limit_bytes=48 * 1024 * 1024
        ),
    )(part)


def gather_kernel(n_x, piece_ref, out_ref, local_sem, send_sem, recv_sem):
    me = lax.axis_index("row")
    col = lax.axis_index("col")
    lag = lax.axis_index("lag")
    y = me // n_x
    x = me % n_x
    right = x + 1
    left = x + n_x - 1
    across = 1 - y
    half = piece_ref.shape[0] // 2

    def slot(yy, xx):
        return yy * n_x + lax.rem(xx, n_x)

    def device(yy, xx):
        return (slot(yy, xx), col, lag)

    def region(index, part):
        if part is None:
            return out_ref.at[index], recv_sem.at[index, 0]
        return out_ref.at[index, pl.ds(part * half, half)], recv_sem.at[index, part]

    barrier = pltpu.get_barrier_semaphore()
    for peer in (device(y, right), device(y, left), device(across, x)):
        pl.semaphore_signal(barrier, inc=1, device_id=peer, device_id_type=MESH)
    pl.semaphore_wait(barrier, 3)

    mine = slot(y, x)
    own = pltpu.make_async_copy(piece_ref, out_ref.at[mine], local_sem)
    own.start()
    sends = []

    def send(index, part, dest, from_input=False):
        target, sem = region(index, part)
        if from_input:
            source = piece_ref
        else:
            source = region(index, part)[0]
        copy = pltpu.make_async_remote_copy(
            src_ref=source,
            dst_ref=target,
            send_sem=send_sem.at[len(sends)],
            recv_sem=sem,
            device_id=dest,
            device_id_type=MESH,
        )
        copy.start()
        sends.append(copy)

    def arrive(index, part):
        target, sem = region(index, part)
        source = piece_ref if part is None else piece_ref.at[pl.ds(part * half, half)]
        pltpu.make_async_remote_copy(
            src_ref=source,
            dst_ref=target,
            send_sem=send_sem.at[0],
            recv_sem=sem,
            device_id=device(y, right),
            device_id_type=MESH,
        ).wait_recv()

    send(mine, None, device(y, right), from_input=True)
    send(mine, None, device(y, left), from_input=True)
    send(mine, None, device(across, x), from_input=True)
    arrive(slot(y, left), None)
    send(slot(y, left), 0, device(y, right))
    arrive(slot(y, right), None)
    send(slot(y, right), 1, device(y, left))
    arrive(slot(across, x), None)
    send(slot(across, x), None, device(y, right))
    send(slot(across, x), None, device(y, left))
    for part in range(2):
        arrive(slot(y, x + 2), part)
        send(slot(y, x + 2), part, device(across, x))
    arrive(slot(across, left), None)
    arrive(slot(across, right), None)
    for part in range(2):
        arrive(slot(across, x + 2), part)
    own.wait()
    for copy in sends:
        copy.wait_send()


def all_gather_rows(piece, n_row):
    n_x = n_row // 2
    assert n_x == 4
    return pl.pallas_call(
        functools.partial(gather_kernel, n_x),
        out_shape=jax.ShapeDtypeStruct((n_row,) + piece.shape, piece.dtype),
        in_specs=[pl.BlockSpec(memory_space=pltpu.VMEM)],
        out_specs=pl.BlockSpec(memory_space=pl.ANY),
        scratch_shapes=[
            pltpu.SemaphoreType.DMA(()),
            pltpu.SemaphoreType.DMA((9,)),
            pltpu.SemaphoreType.DMA((n_row, 2)),
        ],
        compiler_params=pltpu.CompilerParams(collective_id=1, has_side_effects=True),
    )(piece)


def parts_kernel(n_lag, rows_ref, cols_ref, count_ref, lag_ref, hist_ref, tiles_ref, out_ref):
    lag = pl.program_id(0)
    slots = tiles_ref.shape[1]
    side = tiles_ref.shape[2]
    halves = hist_ref.shape[3] // side

    @pl.when(lag == 0)
    def _():
        out_ref[...] = jnp.zeros_like(out_ref)

    for k in range(slots):
        @pl.when(k < count_ref[lag])
        def _():
            col = cols_ref[lag, k]
            row = rows_ref[lag, k]
            both = hist_ref[col // halves, 0]
            history = jnp.where(col % halves == 0, both[:, :side], both[:, side:])
            contrib = lax.dot_general(
                history, tiles_ref[0, k], (((1,), (1,)), ((), ())),
                preferred_element_type=jnp.float32,
            )
            half = jnp.where(row % n_lag == lag_ref[0], 0, 1)
            out_ref[half, row // n_lag] += contrib


def stress_parts(history, tiles, rows, cols, count, n_col, n_lag):
    n_row, lags, sims, held = history.shape
    _, slots, side, _ = tiles.shape
    lag = lax.axis_index("lag").astype(jnp.int32).reshape(1)
    grid_spec = pltpu.PrefetchScalarGridSpec(
        num_scalar_prefetch=4,
        grid=(lags,),
        in_specs=[
            pl.BlockSpec((n_row, 1, sims, held), lambda l, *_: (0, l, 0, 0)),
            pl.BlockSpec((1, slots, side, side), lambda l, *_: (l, 0, 0, 0)),
        ],
        out_specs=pl.BlockSpec((2, n_col, sims, side), lambda l, *_: (0, 0, 0, 0)),
    )
    return pl.pallas_call(
        functools.partial(parts_kernel, n_lag),
        out_shape=jax.ShapeDtypeStruct((2, n_col, sims, side), jnp.float32),
        grid_spec=grid_spec,
        compiler_params=pltpu.CompilerParams(vmem_limit_bytes=48 * 1024 * 1024),
    )(rows, cols, count, lag, history, tiles)


def local(
    n_row,
    n_col,
    n_lag,
    history,
    kernel_tiles,
    tile_rows,
    tile_cols,
    tile_count,
    base_stress,
    prev_rate,
    direct_effect,
    state_var,
):
    gathered = all_gather_rows(history[:, 0], n_row)
    tile_side = kernel_tiles.shape[4]
    parts = stress_parts(gathered, kernel_tiles[0, 0], tile_rows[0, 0],
                         tile_cols[0, 0], tile_count[0, 0], n_col, n_lag)
    stress_change = reduce_scatter(parts, n_col)
    driving = base_stress + stress_change
    factor = jnp.exp(state_var) / 2.0
    velocity = prev_rate
    for step in range(NEWTON):
        scaled = velocity * factor
        misfit = direct_effect * inverse_sinh(scaled) + 0.5 * velocity - driving
        slope = direct_effect * factor / jnp.sqrt(1.0 + scaled * scaled) + 0.5
        velocity = velocity - misfit / slope
    return (stress_change, velocity)


def solution(mesh):
    return jax.shard_map(
        functools.partial(local, mesh.shape["row"], mesh.shape["col"], mesh.shape["lag"]),
        mesh=mesh,
        in_specs=(
            P("lag", "col", None, "row"),
            P("row", "col", "lag", None, None, None),
            P("row", "col", "lag", None),
            P("row", "col", "lag", None),
            P("row", "col", "lag"),
            P(None, ("row", "col", "lag")),
            P(None, ("row", "col", "lag")),
            P(None, ("row", "col", "lag")),
            P(None, ("row", "col", "lag")),
        ),
        out_specs=(P(None, ("row", "col", "lag")), P(None, ("row", "col", "lag"))),
        check_vma=False,
    )
```

```python
import functools

import jax
import jax.numpy as jnp
from jax import lax
from jax.experimental import pallas as pl
from jax.experimental.pallas import tpu as pltpu
from jax.sharding import PartitionSpec as P

NEWTON = 4
MESH = pl.DeviceIdType.MESH


def inverse_sinh(value):
    magnitude = jnp.abs(value)
    return jnp.sign(value) * jnp.log(magnitude + jnp.sqrt(1.0 + magnitude * magnitude))


def ring_kernel(n_z, n_pieces, part_ref, out_ref, recv, forward, final, cross, mate,
                send_sem, recv_sem, cross_sem, mate_sem):
    row = lax.axis_index("row")
    col = lax.axis_index("col")
    lag = lax.axis_index("lag")
    z = col // 2
    y_hi = col % 2
    up = lax.rem(z + 1, n_z)
    down = lax.rem(z + n_z - 1, n_z)
    rows = part_ref.shape[2] // n_pieces
    longer = n_z // 2
    shorter = n_z - 1 - longer

    def device(zz, yy):
        return (row, zz * 2 + yy, lag)

    def length(way, side):
        return longer if way == side else shorter

    partner = (row, col, 1 - lag)
    barrier = pltpu.get_barrier_semaphore()
    for peer in (device(up, y_hi), device(down, y_hi), device(z, 1 - y_hi), partner):
        pl.semaphore_signal(barrier, inc=1, device_id=peer, device_id_type=MESH)
    pl.semaphore_wait(barrier, 4)

    def chain_block(step, side, way):
        chain = length(way, side)
        if side == 0:
            target = lax.rem(z + chain - step, n_z)
        else:
            target = lax.rem(z + n_z - chain + step, n_z)
        return target * 2 + way

    order = []
    for step in range(longer):
        for side in range(2):
            for way in range(2):
                if step < length(way, side):
                    order.append(chain_block(step, side, way))
    order += [z * 2 + way for way in range(2)]
    handed = {}
    for index, block in enumerate(order):
        copy = pltpu.make_async_remote_copy(
            src_ref=part_ref.at[1, block],
            dst_ref=mate.at[block],
            send_sem=mate_sem.at[0, index],
            recv_sem=mate_sem.at[1, index],
            device_id=partner,
            device_id_type=MESH,
        )
        copy.start()
        handed[index] = copy
    ready = set()

    def own(index, span):
        if index not in ready:
            handed[index].wait_recv()
            ready.add(index)
        block = order[index]
        return part_ref[0, block, span] + mate[block, span]

    copies = {}
    for step in range(longer):
        for piece in range(n_pieces):
            span = pl.ds(piece * rows, rows)
            for side in range(2):
                for way in range(2):
                    if step >= length(way, side):
                        continue
                    dest = device(up, y_hi) if side == 0 else device(down, y_hi)
                    index = len([1 for st in range(step) for sd in range(2) for w in range(2)
                                 if st < length(w, sd)])
                    index += len([1 for sd in range(side) for w in range(2)
                                  if step < length(w, sd)])
                    index += len([1 for w in range(way) if step < length(w, side)])
                    if step == 0:
                        forward[side, way, step, piece] = own(index, span)
                    else:
                        copies[side, way, step - 1, piece].wait_recv()
                        forward[side, way, step, piece] = (
                            recv[side, way, step - 1, piece] + own(index, span)
                        )
                    source = forward.at[side, way, step, piece]
                    copy = pltpu.make_async_remote_copy(
                        src_ref=source,
                        dst_ref=recv.at[side, way, step, piece],
                        send_sem=send_sem.at[side, way, step, piece],
                        recv_sem=recv_sem.at[side, way, step, piece],
                        device_id=dest,
                        device_id_type=MESH,
                    )
                    copy.start()
                    copies[side, way, step, piece] = copy

    handoffs = []
    for piece in range(n_pieces):
        span = pl.ds(piece * rows, rows)
        for way in range(2):
            total = own(len(order) - 2 + way, span)
            for side in range(2):
                last = length(way, side) - 1
                copies[side, way, last, piece].wait_recv()
                total = total + recv[side, way, last, piece]
            final[way, piece] = total
        handoff = pltpu.make_async_remote_copy(
            src_ref=final.at[1 - y_hi, piece],
            dst_ref=cross.at[piece],
            send_sem=cross_sem.at[0, piece],
            recv_sem=cross_sem.at[1, piece],
            device_id=device(z, 1 - y_hi),
            device_id_type=MESH,
        )
        handoff.start()
        handoffs.append(handoff)
    for piece in range(n_pieces):
        handoffs[piece].wait_recv()
        out_ref[pl.ds(piece * rows, rows), :] = final[y_hi, piece] + cross[piece]
    for handoff in handoffs:
        handoff.wait_send()
    for copy in copies.values():
        copy.wait_send()
    for copy in handed.values():
        copy.wait_send()


def reduce_scatter(part, n_col, n_pieces=4):
    _, group, sims, tile = part.shape
    n_z = n_col // 2
    longer = n_z // 2
    rows = sims // n_pieces
    return pl.pallas_call(
        functools.partial(ring_kernel, n_z, n_pieces),
        out_shape=jax.ShapeDtypeStruct((sims, tile), jnp.float32),
        in_specs=[pl.BlockSpec(memory_space=pltpu.VMEM)],
        out_specs=pl.BlockSpec(memory_space=pltpu.VMEM),
        scratch_shapes=[
            pltpu.VMEM((2, 2, longer, n_pieces, rows, tile), jnp.float32),
            pltpu.VMEM((2, 2, longer, n_pieces, rows, tile), jnp.float32),
            pltpu.VMEM((2, n_pieces, rows, tile), jnp.float32),
            pltpu.VMEM((n_pieces, rows, tile), jnp.float32),
            pltpu.VMEM((group, sims, tile), jnp.float32),
            pltpu.SemaphoreType.DMA((2, 2, longer, n_pieces)),
            pltpu.SemaphoreType.DMA((2, 2, longer, n_pieces)),
            pltpu.SemaphoreType.DMA((2, n_pieces)),
            pltpu.SemaphoreType.DMA((2, group)),
        ],
        compiler_params=pltpu.CompilerParams(
            collective_id=0, has_side_effects=True, vmem_limit_bytes=48 * 1024 * 1024
        ),
    )(part)


def gather_kernel(n_x, piece_ref, out_ref, local_sem, send_sem, recv_sem):
    me = lax.axis_index("row")
    col = lax.axis_index("col")
    lag = lax.axis_index("lag")
    y = me // n_x
    x = me % n_x
    right = x + 1
    left = x + n_x - 1
    across = 1 - y
    half = piece_ref.shape[0] // 2

    def slot(yy, xx):
        return yy * n_x + lax.rem(xx, n_x)

    def device(yy, xx):
        return (slot(yy, xx), col, lag)

    def region(index, part):
        if part is None:
            return out_ref.at[index], recv_sem.at[index, 0]
        return out_ref.at[index, pl.ds(part * half, half)], recv_sem.at[index, part]

    barrier = pltpu.get_barrier_semaphore()
    for peer in (device(y, right), device(y, left), device(across, x)):
        pl.semaphore_signal(barrier, inc=1, device_id=peer, device_id_type=MESH)
    pl.semaphore_wait(barrier, 3)

    mine = slot(y, x)
    own = pltpu.make_async_copy(piece_ref, out_ref.at[mine], local_sem)
    own.start()
    sends = []

    def send(index, part, dest, from_input=False):
        target, sem = region(index, part)
        if from_input:
            source = piece_ref
        else:
            source = region(index, part)[0]
        copy = pltpu.make_async_remote_copy(
            src_ref=source,
            dst_ref=target,
            send_sem=send_sem.at[len(sends)],
            recv_sem=sem,
            device_id=dest,
            device_id_type=MESH,
        )
        copy.start()
        sends.append(copy)

    def arrive(index, part):
        target, sem = region(index, part)
        source = piece_ref if part is None else piece_ref.at[pl.ds(part * half, half)]
        pltpu.make_async_remote_copy(
            src_ref=source,
            dst_ref=target,
            send_sem=send_sem.at[0],
            recv_sem=sem,
            device_id=device(y, right),
            device_id_type=MESH,
        ).wait_recv()

    send(mine, None, device(across, x), from_input=True)
    send(mine, None, device(y, right), from_input=True)
    send(mine, None, device(y, left), from_input=True)
    arrive(slot(y, left), None)
    send(slot(y, left), 0, device(y, right))
    arrive(slot(y, right), None)
    send(slot(y, right), 1, device(y, left))
    arrive(slot(across, x), None)
    send(slot(across, x), None, device(y, right))
    send(slot(across, x), None, device(y, left))
    for part in range(2):
        arrive(slot(y, x + 2), part)
        send(slot(y, x + 2), part, device(across, x))
    arrive(slot(across, left), None)
    arrive(slot(across, right), None)
    for part in range(2):
        arrive(slot(across, x + 2), part)
    own.wait()
    for copy in sends:
        copy.wait_send()


def all_gather_rows(piece, n_row):
    n_x = n_row // 2
    assert n_x == 4
    return pl.pallas_call(
        functools.partial(gather_kernel, n_x),
        out_shape=jax.ShapeDtypeStruct((n_row,) + piece.shape, piece.dtype),
        in_specs=[pl.BlockSpec(memory_space=pltpu.VMEM)],
        out_specs=pl.BlockSpec(memory_space=pl.ANY),
        scratch_shapes=[
            pltpu.SemaphoreType.DMA(()),
            pltpu.SemaphoreType.DMA((9,)),
            pltpu.SemaphoreType.DMA((n_row, 2)),
        ],
        compiler_params=pltpu.CompilerParams(collective_id=1, has_side_effects=True),
    )(piece)


def parts_kernel(n_lag, rows_ref, cols_ref, count_ref, lag_ref, hist_ref, tiles_ref, out_ref):
    lag = pl.program_id(0)
    slots = tiles_ref.shape[1]
    side = tiles_ref.shape[2]
    halves = hist_ref.shape[3] // side

    @pl.when(lag == 0)
    def _():
        out_ref[...] = jnp.zeros_like(out_ref)

    for k in range(slots):
        @pl.when(k < count_ref[lag])
        def _():
            col = cols_ref[lag, k]
            row = rows_ref[lag, k]
            both = hist_ref[col // halves, 0]
            history = jnp.where(col % halves == 0, both[:, :side], both[:, side:])
            contrib = lax.dot_general(
                history, tiles_ref[0, k], (((1,), (1,)), ((), ())),
                preferred_element_type=jnp.float32,
            )
            half = jnp.where(row % n_lag == lag_ref[0], 0, 1)
            out_ref[half, row // n_lag] += contrib


def stress_parts(history, tiles, rows, cols, count, n_col, n_lag):
    n_row, lags, sims, held = history.shape
    _, slots, side, _ = tiles.shape
    lag = lax.axis_index("lag").astype(jnp.int32).reshape(1)
    grid_spec = pltpu.PrefetchScalarGridSpec(
        num_scalar_prefetch=4,
        grid=(lags,),
        in_specs=[
            pl.BlockSpec((n_row, 1, sims, held), lambda l, *_: (0, l, 0, 0)),
            pl.BlockSpec((1, slots, side, side), lambda l, *_: (l, 0, 0, 0)),
        ],
        out_specs=pl.BlockSpec((2, n_col, sims, side), lambda l, *_: (0, 0, 0, 0)),
    )
    return pl.pallas_call(
        functools.partial(parts_kernel, n_lag),
        out_shape=jax.ShapeDtypeStruct((2, n_col, sims, side), jnp.float32),
        grid_spec=grid_spec,
        compiler_params=pltpu.CompilerParams(vmem_limit_bytes=48 * 1024 * 1024),
    )(rows, cols, count, lag, history, tiles)


def local(
    n_row,
    n_col,
    n_lag,
    history,
    kernel_tiles,
    tile_rows,
    tile_cols,
    tile_count,
    base_stress,
    prev_rate,
    direct_effect,
    state_var,
):
    gathered = all_gather_rows(history[:, 0], n_row)
    tile_side = kernel_tiles.shape[4]
    parts = stress_parts(gathered, kernel_tiles[0, 0], tile_rows[0, 0],
                         tile_cols[0, 0], tile_count[0, 0], n_col, n_lag)
    stress_change = reduce_scatter(parts, n_col)
    driving = base_stress + stress_change
    factor = jnp.exp(state_var) / 2.0
    velocity = prev_rate
    for step in range(NEWTON):
        scaled = velocity * factor
        misfit = direct_effect * inverse_sinh(scaled) + 0.5 * velocity - driving
        slope = direct_effect * factor / jnp.sqrt(1.0 + scaled * scaled) + 0.5
        velocity = velocity - misfit / slope
    return (stress_change, velocity)


def solution(mesh):
    return jax.shard_map(
        functools.partial(local, mesh.shape["row"], mesh.shape["col"], mesh.shape["lag"]),
        mesh=mesh,
        in_specs=(
            P("lag", "col", None, "row"),
            P("row", "col", "lag", None, None, None),
            P("row", "col", "lag", None),
            P("row", "col", "lag", None),
            P("row", "col", "lag"),
            P(None, ("row", "col", "lag")),
            P(None, ("row", "col", "lag")),
            P(None, ("row", "col", "lag")),
            P(None, ("row", "col", "lag")),
        ),
        out_specs=(P(None, ("row", "col", "lag")), P(None, ("row", "col", "lag"))),
        check_vma=False,
    )
```

```python
import functools

import jax
import jax.numpy as jnp
from jax import lax
from jax.experimental import pallas as pl
from jax.experimental.pallas import tpu as pltpu
from jax.sharding import PartitionSpec as P

NEWTON = 4
MESH = pl.DeviceIdType.MESH


def inverse_sinh(value):
    magnitude = jnp.abs(value)
    return jnp.sign(value) * jnp.log(magnitude + jnp.sqrt(1.0 + magnitude * magnitude))


def ring_kernel(n_z, n_pieces, part_ref, out_ref, recv, forward, final, cross, mate,
                own_buf, send_sem, recv_sem, cross_sem, mate_sem, own_sem):
    row = lax.axis_index("row")
    col = lax.axis_index("col")
    lag = lax.axis_index("lag")
    z = col // 2
    y_hi = col % 2
    up = lax.rem(z + 1, n_z)
    down = lax.rem(z + n_z - 1, n_z)
    rows = part_ref.shape[2] // n_pieces
    longer = n_z // 2
    shorter = n_z - 1 - longer

    def device(zz, yy):
        return (row, zz * 2 + yy, lag)

    def length(way, side):
        return longer if way == side else shorter

    partner = (row, col, 1 - lag)
    own_copy = pltpu.make_async_copy(part_ref.at[0], own_buf, own_sem)
    own_copy.start()
    barrier = pltpu.get_barrier_semaphore()
    for peer in (device(up, y_hi), device(down, y_hi), device(z, 1 - y_hi), partner):
        pl.semaphore_signal(barrier, inc=1, device_id=peer, device_id_type=MESH)
    pl.semaphore_wait(barrier, 4)

    def chain_block(step, side, way):
        chain = length(way, side)
        if side == 0:
            target = lax.rem(z + chain - step, n_z)
        else:
            target = lax.rem(z + n_z - chain + step, n_z)
        return target * 2 + way

    order = []
    for step in range(longer):
        for side in range(2):
            for way in range(2):
                if step < length(way, side):
                    order.append(chain_block(step, side, way))
    order += [z * 2 + way for way in range(2)]
    handed = {}
    for index, block in enumerate(order):
        copy = pltpu.make_async_remote_copy(
            src_ref=part_ref.at[1, block],
            dst_ref=mate.at[block],
            send_sem=mate_sem.at[0, index],
            recv_sem=mate_sem.at[1, index],
            device_id=partner,
            device_id_type=MESH,
        )
        copy.start()
        handed[index] = copy
    ready = set()

    def own(index, span):
        if not ready:
            own_copy.wait()
        if index not in ready:
            handed[index].wait_recv()
            ready.add(index)
        block = order[index]
        return own_buf[block, span] + mate[block, span]

    copies = {}
    for step in range(longer):
        for piece in range(n_pieces):
            span = pl.ds(piece * rows, rows)
            for side in range(2):
                for way in range(2):
                    if step >= length(way, side):
                        continue
                    dest = device(up, y_hi) if side == 0 else device(down, y_hi)
                    index = len([1 for st in range(step) for sd in range(2) for w in range(2)
                                 if st < length(w, sd)])
                    index += len([1 for sd in range(side) for w in range(2)
                                  if step < length(w, sd)])
                    index += len([1 for w in range(way) if step < length(w, side)])
                    if step == 0:
                        forward[side, way, step, piece] = own(index, span)
                    else:
                        copies[side, way, step - 1, piece].wait_recv()
                        forward[side, way, step, piece] = (
                            recv[side, way, step - 1, piece] + own(index, span)
                        )
                    source = forward.at[side, way, step, piece]
                    copy = pltpu.make_async_remote_copy(
                        src_ref=source,
                        dst_ref=recv.at[side, way, step, piece],
                        send_sem=send_sem.at[side, way, step, piece],
                        recv_sem=recv_sem.at[side, way, step, piece],
                        device_id=dest,
                        device_id_type=MESH,
                    )
                    copy.start()
                    copies[side, way, step, piece] = copy

    handoffs = []
    for piece in range(n_pieces):
        span = pl.ds(piece * rows, rows)
        for way in range(2):
            total = own(len(order) - 2 + way, span)
            for side in range(2):
                last = length(way, side) - 1
                copies[side, way, last, piece].wait_recv()
                total = total + recv[side, way, last, piece]
            final[way, piece] = total
        handoff = pltpu.make_async_remote_copy(
            src_ref=final.at[1 - y_hi, piece],
            dst_ref=cross.at[piece],
            send_sem=cross_sem.at[0, piece],
            recv_sem=cross_sem.at[1, piece],
            device_id=device(z, 1 - y_hi),
            device_id_type=MESH,
        )
        handoff.start()
        handoffs.append(handoff)
    for piece in range(n_pieces):
        handoffs[piece].wait_recv()
        out_ref[pl.ds(piece * rows, rows), :] = final[y_hi, piece] + cross[piece]
    for handoff in handoffs:
        handoff.wait_send()
    for copy in copies.values():
        copy.wait_send()
    for copy in handed.values():
        copy.wait_send()


def reduce_scatter(part, n_col, n_pieces=4):
    _, group, sims, tile = part.shape
    n_z = n_col // 2
    longer = n_z // 2
    rows = sims // n_pieces
    return pl.pallas_call(
        functools.partial(ring_kernel, n_z, n_pieces),
        out_shape=jax.ShapeDtypeStruct((sims, tile), jnp.float32),
        in_specs=[pl.BlockSpec(memory_space=pl.ANY)],
        out_specs=pl.BlockSpec(memory_space=pltpu.VMEM),
        scratch_shapes=[
            pltpu.VMEM((2, 2, longer, n_pieces, rows, tile), jnp.float32),
            pltpu.VMEM((2, 2, longer, n_pieces, rows, tile), jnp.float32),
            pltpu.VMEM((2, n_pieces, rows, tile), jnp.float32),
            pltpu.VMEM((n_pieces, rows, tile), jnp.float32),
            pltpu.VMEM((group, sims, tile), jnp.float32),
            pltpu.VMEM((group, sims, tile), jnp.float32),
            pltpu.SemaphoreType.DMA((2, 2, longer, n_pieces)),
            pltpu.SemaphoreType.DMA((2, 2, longer, n_pieces)),
            pltpu.SemaphoreType.DMA((2, n_pieces)),
            pltpu.SemaphoreType.DMA((2, group)),
            pltpu.SemaphoreType.DMA(()),
        ],
        compiler_params=pltpu.CompilerParams(
            collective_id=0, has_side_effects=True, vmem_limit_bytes=48 * 1024 * 1024
        ),
    )(part)


def gather_kernel(n_x, piece_ref, out_ref, local_sem, send_sem, recv_sem):
    me = lax.axis_index("row")
    col = lax.axis_index("col")
    lag = lax.axis_index("lag")
    y = me // n_x
    x = me % n_x
    right = x + 1
    left = x + n_x - 1
    across = 1 - y
    half = piece_ref.shape[0] // 2

    def slot(yy, xx):
        return yy * n_x + lax.rem(xx, n_x)

    def device(yy, xx):
        return (slot(yy, xx), col, lag)

    def region(index, part):
        if part is None:
            return out_ref.at[index], recv_sem.at[index, 0]
        return out_ref.at[index, pl.ds(part * half, half)], recv_sem.at[index, part]

    barrier = pltpu.get_barrier_semaphore()
    for peer in (device(y, right), device(y, left), device(across, x)):
        pl.semaphore_signal(barrier, inc=1, device_id=peer, device_id_type=MESH)
    pl.semaphore_wait(barrier, 3)

    mine = slot(y, x)
    own = pltpu.make_async_copy(piece_ref, out_ref.at[mine], local_sem)
    own.start()
    sends = []

    def send(index, part, dest, from_input=False):
        target, sem = region(index, part)
        if from_input:
            source = piece_ref
        else:
            source = region(index, part)[0]
        copy = pltpu.make_async_remote_copy(
            src_ref=source,
            dst_ref=target,
            send_sem=send_sem.at[len(sends)],
            recv_sem=sem,
            device_id=dest,
            device_id_type=MESH,
        )
        copy.start()
        sends.append(copy)

    def arrive(index, part):
        target, sem = region(index, part)
        source = piece_ref if part is None else piece_ref.at[pl.ds(part * half, half)]
        pltpu.make_async_remote_copy(
            src_ref=source,
            dst_ref=target,
            send_sem=send_sem.at[0],
            recv_sem=sem,
            device_id=device(y, right),
            device_id_type=MESH,
        ).wait_recv()

    send(mine, None, device(across, x), from_input=True)
    send(mine, None, device(y, right), from_input=True)
    send(mine, None, device(y, left), from_input=True)
    arrive(slot(y, left), None)
    send(slot(y, left), 0, device(y, right))
    arrive(slot(y, right), None)
    send(slot(y, right), 1, device(y, left))
    arrive(slot(across, x), None)
    send(slot(across, x), None, device(y, right))
    send(slot(across, x), None, device(y, left))
    for part in range(2):
        arrive(slot(y, x + 2), part)
        send(slot(y, x + 2), part, device(across, x))
    arrive(slot(across, left), None)
    arrive(slot(across, right), None)
    for part in range(2):
        arrive(slot(across, x + 2), part)
    own.wait()
    for copy in sends:
        copy.wait_send()


def all_gather_rows(piece, n_row):
    n_x = n_row // 2
    assert n_x == 4
    return pl.pallas_call(
        functools.partial(gather_kernel, n_x),
        out_shape=jax.ShapeDtypeStruct((n_row,) + piece.shape, piece.dtype),
        in_specs=[pl.BlockSpec(memory_space=pltpu.VMEM)],
        out_specs=pl.BlockSpec(memory_space=pl.ANY),
        scratch_shapes=[
            pltpu.SemaphoreType.DMA(()),
            pltpu.SemaphoreType.DMA((9,)),
            pltpu.SemaphoreType.DMA((n_row, 2)),
        ],
        compiler_params=pltpu.CompilerParams(collective_id=1, has_side_effects=True),
    )(piece)


def parts_kernel(n_lag, rows_ref, cols_ref, count_ref, lag_ref, hist_ref, tiles_ref, out_ref):
    lag = pl.program_id(0)
    slots = tiles_ref.shape[1]
    side = tiles_ref.shape[2]
    halves = hist_ref.shape[3] // side

    @pl.when(lag == 0)
    def _():
        out_ref[...] = jnp.zeros_like(out_ref)

    for k in range(slots):
        @pl.when(k < count_ref[lag])
        def _():
            col = cols_ref[lag, k]
            row = rows_ref[lag, k]
            both = hist_ref[col // halves, 0]
            history = jnp.where(col % halves == 0, both[:, :side], both[:, side:])
            contrib = lax.dot_general(
                history, tiles_ref[0, k], (((1,), (1,)), ((), ())),
                preferred_element_type=jnp.float32,
            )
            half = jnp.where(row % n_lag == lag_ref[0], 0, 1)
            out_ref[half, row // n_lag] += contrib


def stress_parts(history, tiles, rows, cols, count, n_col, n_lag):
    n_row, lags, sims, held = history.shape
    _, slots, side, _ = tiles.shape
    lag = lax.axis_index("lag").astype(jnp.int32).reshape(1)
    grid_spec = pltpu.PrefetchScalarGridSpec(
        num_scalar_prefetch=4,
        grid=(lags,),
        in_specs=[
            pl.BlockSpec((n_row, 1, sims, held), lambda l, *_: (0, l, 0, 0)),
            pl.BlockSpec((1, slots, side, side), lambda l, *_: (l, 0, 0, 0)),
        ],
        out_specs=pl.BlockSpec((2, n_col, sims, side), lambda l, *_: (0, 0, 0, 0)),
    )
    return pl.pallas_call(
        functools.partial(parts_kernel, n_lag),
        out_shape=jax.ShapeDtypeStruct((2, n_col, sims, side), jnp.float32),
        grid_spec=grid_spec,
        compiler_params=pltpu.CompilerParams(vmem_limit_bytes=48 * 1024 * 1024),
    )(rows, cols, count, lag, history, tiles)


def local(
    n_row,
    n_col,
    n_lag,
    history,
    kernel_tiles,
    tile_rows,
    tile_cols,
    tile_count,
    base_stress,
    prev_rate,
    direct_effect,
    state_var,
):
    gathered = all_gather_rows(history[:, 0], n_row)
    tile_side = kernel_tiles.shape[4]
    parts = stress_parts(gathered, kernel_tiles[0, 0], tile_rows[0, 0],
                         tile_cols[0, 0], tile_count[0, 0], n_col, n_lag)
    stress_change = reduce_scatter(parts, n_col)
    driving = base_stress + stress_change
    factor = jnp.exp(state_var) / 2.0
    velocity = prev_rate
    for step in range(NEWTON):
        scaled = velocity * factor
        misfit = direct_effect * inverse_sinh(scaled) + 0.5 * velocity - driving
        slope = direct_effect * factor / jnp.sqrt(1.0 + scaled * scaled) + 0.5
        velocity = velocity - misfit / slope
    return (stress_change, velocity)


def solution(mesh):
    return jax.shard_map(
        functools.partial(local, mesh.shape["row"], mesh.shape["col"], mesh.shape["lag"]),
        mesh=mesh,
        in_specs=(
            P("lag", "col", None, "row"),
            P("row", "col", "lag", None, None, None),
            P("row", "col", "lag", None),
            P("row", "col", "lag", None),
            P("row", "col", "lag"),
            P(None, ("row", "col", "lag")),
            P(None, ("row", "col", "lag")),
            P(None, ("row", "col", "lag")),
            P(None, ("row", "col", "lag")),
        ),
        out_specs=(P(None, ("row", "col", "lag")), P(None, ("row", "col", "lag"))),
        check_vma=False,
    )
```

```python
import functools

import jax
import jax.numpy as jnp
from jax import lax
from jax.experimental import pallas as pl
from jax.experimental.pallas import tpu as pltpu
from jax.sharding import PartitionSpec as P

NEWTON = 4
MESH = pl.DeviceIdType.MESH


def inverse_sinh(value):
    magnitude = jnp.abs(value)
    return jnp.sign(value) * jnp.log(magnitude + jnp.sqrt(1.0 + magnitude * magnitude))


def ring_kernel(n_z, n_pieces, part_ref, out_ref, cross_ref, recv, forward, final, cross, mate,
                send_sem, recv_sem, cross_sem, mate_sem):
    row = lax.axis_index("row")
    col = lax.axis_index("col")
    lag = lax.axis_index("lag")
    z = col // 2
    y_hi = col % 2
    up = lax.rem(z + 1, n_z)
    down = lax.rem(z + n_z - 1, n_z)
    rows = part_ref.shape[2] // n_pieces
    longer = n_z // 2
    shorter = n_z - 1 - longer

    def device(zz, yy):
        return (row, zz * 2 + yy, lag)

    def length(way, side):
        return longer if way == side else shorter

    partner = (row, col, 1 - lag)
    barrier = pltpu.get_barrier_semaphore()
    for peer in (device(up, y_hi), device(down, y_hi), device(z, 1 - y_hi), partner):
        pl.semaphore_signal(barrier, inc=1, device_id=peer, device_id_type=MESH)
    pl.semaphore_wait(barrier, 4)

    def chain_block(step, side, way):
        chain = length(way, side)
        if side == 0:
            target = lax.rem(z + chain - step, n_z)
        else:
            target = lax.rem(z + n_z - chain + step, n_z)
        return target * 2 + way

    order = []
    for step in range(longer):
        for side in range(2):
            for way in range(2):
                if step < length(way, side):
                    order.append(chain_block(step, side, way))
    order += [z * 2 + way for way in range(2)]
    handed = {}
    for index, block in enumerate(order):
        copy = pltpu.make_async_remote_copy(
            src_ref=part_ref.at[1, block],
            dst_ref=mate.at[block],
            send_sem=mate_sem.at[0, index],
            recv_sem=mate_sem.at[1, index],
            device_id=partner,
            device_id_type=MESH,
        )
        copy.start()
        handed[index] = copy
    ready = set()

    def own(index, span):
        if index not in ready:
            handed[index].wait_recv()
            ready.add(index)
        block = order[index]
        return part_ref[0, block, span] + mate[block, span]

    copies = {}
    for step in range(longer):
        for piece in range(n_pieces):
            span = pl.ds(piece * rows, rows)
            for side in range(2):
                for way in range(2):
                    if step >= length(way, side):
                        continue
                    dest = device(up, y_hi) if side == 0 else device(down, y_hi)
                    index = len([1 for st in range(step) for sd in range(2) for w in range(2)
                                 if st < length(w, sd)])
                    index += len([1 for sd in range(side) for w in range(2)
                                  if step < length(w, sd)])
                    index += len([1 for w in range(way) if step < length(w, side)])
                    if step == 0:
                        forward[side, way, step, piece] = own(index, span)
                    else:
                        copies[side, way, step - 1, piece].wait_recv()
                        forward[side, way, step, piece] = (
                            recv[side, way, step - 1, piece] + own(index, span)
                        )
                    source = forward.at[side, way, step, piece]
                    copy = pltpu.make_async_remote_copy(
                        src_ref=source,
                        dst_ref=recv.at[side, way, step, piece],
                        send_sem=send_sem.at[side, way, step, piece],
                        recv_sem=recv_sem.at[side, way, step, piece],
                        device_id=dest,
                        device_id_type=MESH,
                    )
                    copy.start()
                    copies[side, way, step, piece] = copy

    handoffs = []
    for piece in range(n_pieces):
        span = pl.ds(piece * rows, rows)
        for way in range(2):
            total = own(len(order) - 2 + way, span)
            for side in range(2):
                last = length(way, side) - 1
                copies[side, way, last, piece].wait_recv()
                total = total + recv[side, way, last, piece]
            final[way, piece] = total
        handoff = pltpu.make_async_remote_copy(
            src_ref=final.at[1 - y_hi, piece],
            dst_ref=cross.at[piece],
            send_sem=cross_sem.at[0, piece],
            recv_sem=cross_sem.at[1, piece],
            device_id=device(z, 1 - y_hi),
            device_id_type=MESH,
        )
        handoff.start()
        handoffs.append(handoff)
    for piece in range(n_pieces):
        handoffs[piece].wait_recv()
        out_ref[pl.ds(piece * rows, rows), :] = final[y_hi, piece]
        cross_ref[pl.ds(piece * rows, rows), :] = cross[piece]
    for handoff in handoffs:
        handoff.wait_send()
    for copy in copies.values():
        copy.wait_send()
    for copy in handed.values():
        copy.wait_send()


def reduce_scatter(part, n_col, n_pieces=4):
    _, group, sims, tile = part.shape
    n_z = n_col // 2
    longer = n_z // 2
    rows = sims // n_pieces
    return pl.pallas_call(
        functools.partial(ring_kernel, n_z, n_pieces),
        out_shape=[jax.ShapeDtypeStruct((sims, tile), jnp.float32)] * 2,
        in_specs=[pl.BlockSpec(memory_space=pltpu.VMEM)],
        out_specs=[pl.BlockSpec(memory_space=pltpu.VMEM)] * 2,
        scratch_shapes=[
            pltpu.VMEM((2, 2, longer, n_pieces, rows, tile), jnp.float32),
            pltpu.VMEM((2, 2, longer, n_pieces, rows, tile), jnp.float32),
            pltpu.VMEM((2, n_pieces, rows, tile), jnp.float32),
            pltpu.VMEM((n_pieces, rows, tile), jnp.float32),
            pltpu.VMEM((group, sims, tile), jnp.float32),
            pltpu.SemaphoreType.DMA((2, 2, longer, n_pieces)),
            pltpu.SemaphoreType.DMA((2, 2, longer, n_pieces)),
            pltpu.SemaphoreType.DMA((2, n_pieces)),
            pltpu.SemaphoreType.DMA((2, group)),
        ],
        compiler_params=pltpu.CompilerParams(
            collective_id=0, has_side_effects=True, vmem_limit_bytes=48 * 1024 * 1024
        ),
    )(part)


def gather_kernel(n_x, piece_ref, out_ref, local_sem, send_sem, recv_sem):
    me = lax.axis_index("row")
    col = lax.axis_index("col")
    lag = lax.axis_index("lag")
    y = me // n_x
    x = me % n_x
    right = x + 1
    left = x + n_x - 1
    across = 1 - y
    half = piece_ref.shape[0] // 2

    def slot(yy, xx):
        return yy * n_x + lax.rem(xx, n_x)

    def device(yy, xx):
        return (slot(yy, xx), col, lag)

    def region(index, part):
        if part is None:
            return out_ref.at[index], recv_sem.at[index, 0]
        return out_ref.at[index, pl.ds(part * half, half)], recv_sem.at[index, part]

    barrier = pltpu.get_barrier_semaphore()
    for peer in (device(y, right), device(y, left), device(across, x)):
        pl.semaphore_signal(barrier, inc=1, device_id=peer, device_id_type=MESH)
    pl.semaphore_wait(barrier, 3)

    mine = slot(y, x)
    own = pltpu.make_async_copy(piece_ref, out_ref.at[mine], local_sem)
    own.start()
    sends = []

    def send(index, part, dest, from_input=False):
        target, sem = region(index, part)
        if from_input:
            source = piece_ref
        else:
            source = region(index, part)[0]
        copy = pltpu.make_async_remote_copy(
            src_ref=source,
            dst_ref=target,
            send_sem=send_sem.at[len(sends)],
            recv_sem=sem,
            device_id=dest,
            device_id_type=MESH,
        )
        copy.start()
        sends.append(copy)

    def arrive(index, part):
        target, sem = region(index, part)
        source = piece_ref if part is None else piece_ref.at[pl.ds(part * half, half)]
        pltpu.make_async_remote_copy(
            src_ref=source,
            dst_ref=target,
            send_sem=send_sem.at[0],
            recv_sem=sem,
            device_id=device(y, right),
            device_id_type=MESH,
        ).wait_recv()

    send(mine, None, device(across, x), from_input=True)
    send(mine, None, device(y, right), from_input=True)
    send(mine, None, device(y, left), from_input=True)
    arrive(slot(y, left), None)
    send(slot(y, left), 0, device(y, right))
    arrive(slot(y, right), None)
    send(slot(y, right), 1, device(y, left))
    arrive(slot(across, x), None)
    send(slot(across, x), None, device(y, right))
    send(slot(across, x), None, device(y, left))
    for part in range(2):
        arrive(slot(y, x + 2), part)
        send(slot(y, x + 2), part, device(across, x))
    arrive(slot(across, left), None)
    arrive(slot(across, right), None)
    for part in range(2):
        arrive(slot(across, x + 2), part)
    own.wait()
    for copy in sends:
        copy.wait_send()


def all_gather_rows(piece, n_row):
    n_x = n_row // 2
    assert n_x == 4
    return pl.pallas_call(
        functools.partial(gather_kernel, n_x),
        out_shape=jax.ShapeDtypeStruct((n_row,) + piece.shape, piece.dtype),
        in_specs=[pl.BlockSpec(memory_space=pltpu.VMEM)],
        out_specs=pl.BlockSpec(memory_space=pl.ANY),
        scratch_shapes=[
            pltpu.SemaphoreType.DMA(()),
            pltpu.SemaphoreType.DMA((9,)),
            pltpu.SemaphoreType.DMA((n_row, 2)),
        ],
        compiler_params=pltpu.CompilerParams(collective_id=1, has_side_effects=True),
    )(piece)


def parts_kernel(n_lag, rows_ref, cols_ref, count_ref, lag_ref, hist_ref, tiles_ref, out_ref):
    lag = pl.program_id(0)
    slots = tiles_ref.shape[1]
    side = tiles_ref.shape[2]
    halves = hist_ref.shape[3] // side

    @pl.when(lag == 0)
    def _():
        out_ref[...] = jnp.zeros_like(out_ref)

    for k in range(slots):
        @pl.when(k < count_ref[lag])
        def _():
            col = cols_ref[lag, k]
            row = rows_ref[lag, k]
            both = hist_ref[col // halves, 0]
            history = jnp.where(col % halves == 0, both[:, :side], both[:, side:])
            contrib = lax.dot_general(
                history, tiles_ref[0, k], (((1,), (1,)), ((), ())),
                preferred_element_type=jnp.float32,
            )
            half = jnp.where(row % n_lag == lag_ref[0], 0, 1)
            out_ref[half, row // n_lag] += contrib


def stress_parts(history, tiles, rows, cols, count, n_col, n_lag):
    n_row, lags, sims, held = history.shape
    _, slots, side, _ = tiles.shape
    lag = lax.axis_index("lag").astype(jnp.int32).reshape(1)
    grid_spec = pltpu.PrefetchScalarGridSpec(
        num_scalar_prefetch=4,
        grid=(lags,),
        in_specs=[
            pl.BlockSpec((n_row, 1, sims, held), lambda l, *_: (0, l, 0, 0)),
            pl.BlockSpec((1, slots, side, side), lambda l, *_: (l, 0, 0, 0)),
        ],
        out_specs=pl.BlockSpec((2, n_col, sims, side), lambda l, *_: (0, 0, 0, 0)),
    )
    return pl.pallas_call(
        functools.partial(parts_kernel, n_lag),
        out_shape=jax.ShapeDtypeStruct((2, n_col, sims, side), jnp.float32),
        grid_spec=grid_spec,
        compiler_params=pltpu.CompilerParams(vmem_limit_bytes=48 * 1024 * 1024),
    )(rows, cols, count, lag, history, tiles)


def local(
    n_row,
    n_col,
    n_lag,
    history,
    kernel_tiles,
    tile_rows,
    tile_cols,
    tile_count,
    base_stress,
    prev_rate,
    direct_effect,
    state_var,
):
    gathered = all_gather_rows(history[:, 0], n_row)
    tile_side = kernel_tiles.shape[4]
    parts = stress_parts(gathered, kernel_tiles[0, 0], tile_rows[0, 0],
                         tile_cols[0, 0], tile_count[0, 0], n_col, n_lag)
    held, handed_over = reduce_scatter(parts, n_col)
    stress_change = held + handed_over
    driving = base_stress + stress_change
    factor = jnp.exp(state_var) / 2.0
    velocity = prev_rate
    for step in range(NEWTON):
        scaled = velocity * factor
        misfit = direct_effect * inverse_sinh(scaled) + 0.5 * velocity - driving
        slope = direct_effect * factor / jnp.sqrt(1.0 + scaled * scaled) + 0.5
        velocity = velocity - misfit / slope
    return (stress_change, velocity)


def solution(mesh):
    return jax.shard_map(
        functools.partial(local, mesh.shape["row"], mesh.shape["col"], mesh.shape["lag"]),
        mesh=mesh,
        in_specs=(
            P("lag", "col", None, "row"),
            P("row", "col", "lag", None, None, None),
            P("row", "col", "lag", None),
            P("row", "col", "lag", None),
            P("row", "col", "lag"),
            P(None, ("row", "col", "lag")),
            P(None, ("row", "col", "lag")),
            P(None, ("row", "col", "lag")),
            P(None, ("row", "col", "lag")),
        ),
        out_specs=(P(None, ("row", "col", "lag")), P(None, ("row", "col", "lag"))),
        check_vma=False,
    )
```

```python
import functools

import jax
import jax.numpy as jnp
from jax import lax
from jax.experimental import pallas as pl
from jax.experimental.pallas import tpu as pltpu
from jax.sharding import PartitionSpec as P

NEWTON = 4
MESH = pl.DeviceIdType.MESH


def inverse_sinh(value):
    magnitude = jnp.abs(value)
    return jnp.sign(value) * jnp.log(magnitude + jnp.sqrt(1.0 + magnitude * magnitude))


def ring_kernel(n_z, n_pieces, part_ref, out_ref, recv, forward, final, cross, mate,
                send_sem, recv_sem, cross_sem, mate_sem):
    row = lax.axis_index("row")
    col = lax.axis_index("col")
    lag = lax.axis_index("lag")
    z = col // 2
    y_hi = col % 2
    up = lax.rem(z + 1, n_z)
    down = lax.rem(z + n_z - 1, n_z)
    rows = part_ref.shape[2] // n_pieces
    longer = n_z // 2
    shorter = n_z - 1 - longer

    def device(zz, yy):
        return (row, zz * 2 + yy, lag)

    def length(way, side):
        return longer if way == side else shorter

    partner = (row, col, 1 - lag)
    barrier = pltpu.get_barrier_semaphore()
    for peer in (device(up, y_hi), device(down, y_hi), device(z, 1 - y_hi), partner):
        pl.semaphore_signal(barrier, inc=1, device_id=peer, device_id_type=MESH)
    pl.semaphore_wait(barrier, 4)

    def chain_block(step, side, way):
        chain = length(way, side)
        if side == 0:
            target = lax.rem(z + chain - step, n_z)
        else:
            target = lax.rem(z + n_z - chain + step, n_z)
        return target * 2 + way

    order = []
    for step in range(longer):
        for side in range(2):
            for way in range(2):
                if step < length(way, side):
                    order.append(chain_block(step, side, way))
    order += [z * 2 + way for way in range(2)]
    handed = {}
    for index, block in enumerate(order):
        copy = pltpu.make_async_remote_copy(
            src_ref=part_ref.at[1, block],
            dst_ref=mate.at[block],
            send_sem=mate_sem.at[0, index],
            recv_sem=mate_sem.at[1, index],
            device_id=partner,
            device_id_type=MESH,
        )
        copy.start()
        handed[index] = copy
    ready = set()

    def own(index, span):
        if index not in ready:
            handed[index].wait_recv()
            ready.add(index)
        block = order[index]
        return part_ref[0, block, span] + mate[block, span]

    copies = {}
    for step in range(longer):
        for piece in range(n_pieces):
            span = pl.ds(piece * rows, rows)
            for side in range(2):
                for way in range(2):
                    if step >= length(way, side):
                        continue
                    dest = device(up, y_hi) if side == 0 else device(down, y_hi)
                    index = len([1 for st in range(step) for sd in range(2) for w in range(2)
                                 if st < length(w, sd)])
                    index += len([1 for sd in range(side) for w in range(2)
                                  if step < length(w, sd)])
                    index += len([1 for w in range(way) if step < length(w, side)])
                    if step == 0:
                        forward[side, way, step, piece] = own(index, span)
                    else:
                        copies[side, way, step - 1, piece].wait_recv()
                        forward[side, way, step, piece] = (
                            recv[side, way, step - 1, piece] + own(index, span)
                        )
                    source = forward.at[side, way, step, piece]
                    copy = pltpu.make_async_remote_copy(
                        src_ref=source,
                        dst_ref=recv.at[side, way, step, piece],
                        send_sem=send_sem.at[side, way, step, piece],
                        recv_sem=recv_sem.at[side, way, step, piece],
                        device_id=dest,
                        device_id_type=MESH,
                    )
                    copy.start()
                    copies[side, way, step, piece] = copy

    handoffs = []
    for piece in range(n_pieces):
        span = pl.ds(piece * rows, rows)
        for way in range(2):
            total = own(len(order) - 2 + way, span)
            for side in range(2):
                last = length(way, side) - 1
                copies[side, way, last, piece].wait_recv()
                total = total + recv[side, way, last, piece]
            final[way, piece] = total
        handoff = pltpu.make_async_remote_copy(
            src_ref=final.at[1 - y_hi, piece],
            dst_ref=cross.at[piece],
            send_sem=cross_sem.at[0, piece],
            recv_sem=cross_sem.at[1, piece],
            device_id=device(z, 1 - y_hi),
            device_id_type=MESH,
        )
        handoff.start()
        handoffs.append(handoff)
    for piece in range(n_pieces):
        handoffs[piece].wait_recv()
        out_ref[pl.ds(piece * rows, rows), :] = final[y_hi, piece] + cross[piece]
    for handoff in handoffs:
        handoff.wait_send()
    for copy in copies.values():
        copy.wait_send()
    for copy in handed.values():
        copy.wait_send()


def reduce_scatter(part, n_col, n_pieces=4):
    _, group, sims, tile = part.shape
    n_z = n_col // 2
    longer = n_z // 2
    rows = sims // n_pieces
    return pl.pallas_call(
        functools.partial(ring_kernel, n_z, n_pieces),
        out_shape=jax.ShapeDtypeStruct((sims, tile), jnp.float32),
        in_specs=[pl.BlockSpec(memory_space=pltpu.VMEM)],
        out_specs=pl.BlockSpec(memory_space=pltpu.VMEM),
        scratch_shapes=[
            pltpu.VMEM((2, 2, longer, n_pieces, rows, tile), jnp.float32),
            pltpu.VMEM((2, 2, longer, n_pieces, rows, tile), jnp.float32),
            pltpu.VMEM((2, n_pieces, rows, tile), jnp.float32),
            pltpu.VMEM((n_pieces, rows, tile), jnp.float32),
            pltpu.VMEM((group, sims, tile), jnp.float32),
            pltpu.SemaphoreType.DMA((2, 2, longer, n_pieces)),
            pltpu.SemaphoreType.DMA((2, 2, longer, n_pieces)),
            pltpu.SemaphoreType.DMA((2, n_pieces)),
            pltpu.SemaphoreType.DMA((2, group)),
        ],
        compiler_params=pltpu.CompilerParams(
            collective_id=0, has_side_effects=True, vmem_limit_bytes=48 * 1024 * 1024
        ),
    )(part)


def gather_kernel(n_x, piece_ref, out_ref, local_sem, send_sem, recv_sem):
    me = lax.axis_index("row")
    col = lax.axis_index("col")
    lag = lax.axis_index("lag")
    y = me // n_x
    x = me % n_x
    right = x + 1
    left = x + n_x - 1
    across = 1 - y
    half = piece_ref.shape[0] // 2

    def slot(yy, xx):
        return yy * n_x + lax.rem(xx, n_x)

    def device(yy, xx):
        return (slot(yy, xx), col, lag)

    few = 16
    sims = piece_ref.shape[1]

    def span(part):
        if part is None:
            return (slice(None),)
        if part < 2:
            return (pl.ds(part * half, half),)
        if part == 2:
            return (slice(None), pl.ds(0, few))
        return (slice(None), pl.ds(few, sims - few))

    def region(index, part):
        sem = recv_sem.at[index, 0 if part is None else part]
        return out_ref.at[(index,) + span(part)], sem

    barrier = pltpu.get_barrier_semaphore()
    for peer in (device(y, right), device(y, left), device(across, x)):
        pl.semaphore_signal(barrier, inc=1, device_id=peer, device_id_type=MESH)
    pl.semaphore_wait(barrier, 3)

    mine = slot(y, x)
    own = pltpu.make_async_copy(piece_ref, out_ref.at[mine], local_sem)
    own.start()
    sends = []

    def send(index, part, dest, from_input=False):
        target, sem = region(index, part)
        if from_input:
            source = piece_ref
        else:
            source = region(index, part)[0]
        copy = pltpu.make_async_remote_copy(
            src_ref=source,
            dst_ref=target,
            send_sem=send_sem.at[len(sends)],
            recv_sem=sem,
            device_id=dest,
            device_id_type=MESH,
        )
        copy.start()
        sends.append(copy)

    def arrive(index, part):
        target, sem = region(index, part)
        source = piece_ref.at[span(part)]
        pltpu.make_async_remote_copy(
            src_ref=source,
            dst_ref=target,
            send_sem=send_sem.at[0],
            recv_sem=sem,
            device_id=device(y, right),
            device_id_type=MESH,
        ).wait_recv()

    send(mine, None, device(across, x), from_input=True)
    send(mine, None, device(y, right), from_input=True)
    send(mine, None, device(y, left), from_input=True)
    arrive(slot(y, left), None)
    send(slot(y, left), 0, device(y, right))
    send(slot(y, left), 2, device(across, x))
    arrive(slot(y, right), None)
    send(slot(y, right), 1, device(y, left))
    send(slot(y, right), 2, device(across, x))
    arrive(slot(across, x), None)
    send(slot(across, x), 3, device(y, right))
    send(slot(across, x), 3, device(y, left))
    for part in range(2):
        arrive(slot(y, x + 2), part)
        send(slot(y, x + 2), part, device(across, x))
    for part in (2, 3):
        arrive(slot(across, left), part)
        arrive(slot(across, right), part)
    for part in range(2):
        arrive(slot(across, x + 2), part)
    own.wait()
    for copy in sends:
        copy.wait_send()


def all_gather_rows(piece, n_row):
    n_x = n_row // 2
    assert n_x == 4
    return pl.pallas_call(
        functools.partial(gather_kernel, n_x),
        out_shape=jax.ShapeDtypeStruct((n_row,) + piece.shape, piece.dtype),
        in_specs=[pl.BlockSpec(memory_space=pltpu.VMEM)],
        out_specs=pl.BlockSpec(memory_space=pl.ANY),
        scratch_shapes=[
            pltpu.SemaphoreType.DMA(()),
            pltpu.SemaphoreType.DMA((11,)),
            pltpu.SemaphoreType.DMA((n_row, 4)),
        ],
        compiler_params=pltpu.CompilerParams(collective_id=1, has_side_effects=True),
    )(piece)


def parts_kernel(n_lag, rows_ref, cols_ref, count_ref, lag_ref, hist_ref, tiles_ref, out_ref):
    lag = pl.program_id(0)
    slots = tiles_ref.shape[1]
    side = tiles_ref.shape[2]
    halves = hist_ref.shape[3] // side

    @pl.when(lag == 0)
    def _():
        out_ref[...] = jnp.zeros_like(out_ref)

    for k in range(slots):
        @pl.when(k < count_ref[lag])
        def _():
            col = cols_ref[lag, k]
            row = rows_ref[lag, k]
            both = hist_ref[col // halves, 0]
            history = jnp.where(col % halves == 0, both[:, :side], both[:, side:])
            contrib = lax.dot_general(
                history, tiles_ref[0, k], (((1,), (1,)), ((), ())),
                preferred_element_type=jnp.float32,
            )
            half = jnp.where(row % n_lag == lag_ref[0], 0, 1)
            out_ref[half, row // n_lag] += contrib


def stress_parts(history, tiles, rows, cols, count, n_col, n_lag):
    n_row, lags, sims, held = history.shape
    _, slots, side, _ = tiles.shape
    lag = lax.axis_index("lag").astype(jnp.int32).reshape(1)
    grid_spec = pltpu.PrefetchScalarGridSpec(
        num_scalar_prefetch=4,
        grid=(lags,),
        in_specs=[
            pl.BlockSpec((n_row, 1, sims, held), lambda l, *_: (0, l, 0, 0)),
            pl.BlockSpec((1, slots, side, side), lambda l, *_: (l, 0, 0, 0)),
        ],
        out_specs=pl.BlockSpec((2, n_col, sims, side), lambda l, *_: (0, 0, 0, 0)),
    )
    return pl.pallas_call(
        functools.partial(parts_kernel, n_lag),
        out_shape=jax.ShapeDtypeStruct((2, n_col, sims, side), jnp.float32),
        grid_spec=grid_spec,
        compiler_params=pltpu.CompilerParams(vmem_limit_bytes=48 * 1024 * 1024),
    )(rows, cols, count, lag, history, tiles)


def local(
    n_row,
    n_col,
    n_lag,
    history,
    kernel_tiles,
    tile_rows,
    tile_cols,
    tile_count,
    base_stress,
    prev_rate,
    direct_effect,
    state_var,
):
    gathered = all_gather_rows(history[:, 0], n_row)
    tile_side = kernel_tiles.shape[4]
    parts = stress_parts(gathered, kernel_tiles[0, 0], tile_rows[0, 0],
                         tile_cols[0, 0], tile_count[0, 0], n_col, n_lag)
    stress_change = reduce_scatter(parts, n_col)
    driving = base_stress + stress_change
    factor = jnp.exp(state_var) / 2.0
    velocity = prev_rate
    for step in range(NEWTON):
        scaled = velocity * factor
        misfit = direct_effect * inverse_sinh(scaled) + 0.5 * velocity - driving
        slope = direct_effect * factor / jnp.sqrt(1.0 + scaled * scaled) + 0.5
        velocity = velocity - misfit / slope
    return (stress_change, velocity)


def solution(mesh):
    return jax.shard_map(
        functools.partial(local, mesh.shape["row"], mesh.shape["col"], mesh.shape["lag"]),
        mesh=mesh,
        in_specs=(
            P("lag", "col", None, "row"),
            P("row", "col", "lag", None, None, None),
            P("row", "col", "lag", None),
            P("row", "col", "lag", None),
            P("row", "col", "lag"),
            P(None, ("row", "col", "lag")),
            P(None, ("row", "col", "lag")),
            P(None, ("row", "col", "lag")),
            P(None, ("row", "col", "lag")),
        ),
        out_specs=(P(None, ("row", "col", "lag")), P(None, ("row", "col", "lag"))),
        check_vma=False,
    )
```

```python
import functools

import jax
import jax.numpy as jnp
from jax import lax
from jax.experimental import pallas as pl
from jax.experimental.pallas import tpu as pltpu
from jax.sharding import PartitionSpec as P

NEWTON = 4
MESH = pl.DeviceIdType.MESH


def inverse_sinh(value):
    magnitude = jnp.abs(value)
    return jnp.sign(value) * jnp.log(magnitude + jnp.sqrt(1.0 + magnitude * magnitude))


def ring_kernel(n_z, n_pieces, part_ref, out_ref, recv, forward, final, cross, mate,
                send_sem, recv_sem, cross_sem, mate_sem):
    row = lax.axis_index("row")
    col = lax.axis_index("col")
    lag = lax.axis_index("lag")
    z = col // 2
    y_hi = col % 2
    up = lax.rem(z + 1, n_z)
    down = lax.rem(z + n_z - 1, n_z)
    rows = part_ref.shape[2] // n_pieces
    longer = n_z // 2
    shorter = n_z - 1 - longer

    def device(zz, yy):
        return (row, zz * 2 + yy, lag)

    def length(way, side):
        return longer if way == side else shorter

    partner = (row, col, 1 - lag)
    barrier = pltpu.get_barrier_semaphore()
    for peer in (device(up, y_hi), device(down, y_hi), device(z, 1 - y_hi), partner):
        pl.semaphore_signal(barrier, inc=1, device_id=peer, device_id_type=MESH)
    pl.semaphore_wait(barrier, 4)

    def chain_block(step, side, way):
        chain = length(way, side)
        if side == 0:
            target = lax.rem(z + chain - step, n_z)
        else:
            target = lax.rem(z + n_z - chain + step, n_z)
        return target * 2 + way

    order = []
    for step in range(longer):
        for side in range(2):
            for way in range(2):
                if step < length(way, side):
                    order.append(chain_block(step, side, way))
    order += [z * 2 + way for way in range(2)]
    handed = {}
    for index, block in enumerate(order):
        copy = pltpu.make_async_remote_copy(
            src_ref=part_ref.at[1, block],
            dst_ref=mate.at[block],
            send_sem=mate_sem.at[0, index],
            recv_sem=mate_sem.at[1, index],
            device_id=partner,
            device_id_type=MESH,
        )
        copy.start()
        handed[index] = copy
    ready = set()

    def own(index, span):
        if index not in ready:
            handed[index].wait_recv()
            ready.add(index)
        block = order[index]
        return part_ref[0, block, span] + mate[block, span]

    copies = {}
    for step in range(longer):
        for piece in range(n_pieces):
            span = pl.ds(piece * rows, rows)
            for side in range(2):
                for way in range(2):
                    if step >= length(way, side):
                        continue
                    dest = device(up, y_hi) if side == 0 else device(down, y_hi)
                    index = len([1 for st in range(step) for sd in range(2) for w in range(2)
                                 if st < length(w, sd)])
                    index += len([1 for sd in range(side) for w in range(2)
                                  if step < length(w, sd)])
                    index += len([1 for w in range(way) if step < length(w, side)])
                    if step == 0:
                        forward[side, way, step, piece] = own(index, span)
                    else:
                        copies[side, way, step - 1, piece].wait_recv()
                        forward[side, way, step, piece] = (
                            recv[side, way, step - 1, piece] + own(index, span)
                        )
                    source = forward.at[side, way, step, piece]
                    copy = pltpu.make_async_remote_copy(
                        src_ref=source,
                        dst_ref=recv.at[side, way, step, piece],
                        send_sem=send_sem.at[side, way, step, piece],
                        recv_sem=recv_sem.at[side, way, step, piece],
                        device_id=dest,
                        device_id_type=MESH,
                    )
                    copy.start()
                    copies[side, way, step, piece] = copy

    handoffs = []
    for piece in range(n_pieces):
        span = pl.ds(piece * rows, rows)
        for way in range(2):
            total = own(len(order) - 2 + way, span)
            for side in range(2):
                last = length(way, side) - 1
                copies[side, way, last, piece].wait_recv()
                total = total + recv[side, way, last, piece]
            final[way, piece] = total
        handoff = pltpu.make_async_remote_copy(
            src_ref=final.at[1 - y_hi, piece],
            dst_ref=cross.at[piece],
            send_sem=cross_sem.at[0, piece],
            recv_sem=cross_sem.at[1, piece],
            device_id=device(z, 1 - y_hi),
            device_id_type=MESH,
        )
        handoff.start()
        handoffs.append(handoff)
    for piece in range(n_pieces):
        handoffs[piece].wait_recv()
        out_ref[pl.ds(piece * rows, rows), :] = final[y_hi, piece] + cross[piece]
    for handoff in handoffs:
        handoff.wait_send()
    for copy in copies.values():
        copy.wait_send()
    for copy in handed.values():
        copy.wait_send()


def reduce_scatter(part, n_col, n_pieces=4):
    _, group, sims, tile = part.shape
    n_z = n_col // 2
    longer = n_z // 2
    rows = sims // n_pieces
    return pl.pallas_call(
        functools.partial(ring_kernel, n_z, n_pieces),
        out_shape=jax.ShapeDtypeStruct((sims, tile), jnp.float32),
        in_specs=[pl.BlockSpec(memory_space=pltpu.VMEM)],
        out_specs=pl.BlockSpec(memory_space=pltpu.VMEM),
        scratch_shapes=[
            pltpu.VMEM((2, 2, longer, n_pieces, rows, tile), jnp.float32),
            pltpu.VMEM((2, 2, longer, n_pieces, rows, tile), jnp.float32),
            pltpu.VMEM((2, n_pieces, rows, tile), jnp.float32),
            pltpu.VMEM((n_pieces, rows, tile), jnp.float32),
            pltpu.VMEM((group, sims, tile), jnp.float32),
            pltpu.SemaphoreType.DMA((2, 2, longer, n_pieces)),
            pltpu.SemaphoreType.DMA((2, 2, longer, n_pieces)),
            pltpu.SemaphoreType.DMA((2, n_pieces)),
            pltpu.SemaphoreType.DMA((2, group)),
        ],
        compiler_params=pltpu.CompilerParams(
            collective_id=0, has_side_effects=True, vmem_limit_bytes=48 * 1024 * 1024
        ),
    )(part)


def gather_kernel(n_x, piece_ref, out_ref, local_sem, send_sem, recv_sem):
    me = lax.axis_index("row")
    col = lax.axis_index("col")
    lag = lax.axis_index("lag")
    y = me // n_x
    x = me % n_x
    right = x + 1
    left = x + n_x - 1
    across = 1 - y
    half = piece_ref.shape[0] // 2

    def slot(yy, xx):
        return yy * n_x + lax.rem(xx, n_x)

    def device(yy, xx):
        return (slot(yy, xx), col, lag)

    few = 32
    sims = piece_ref.shape[1]

    def span(part):
        if part is None:
            return (slice(None),)
        if part < 2:
            return (pl.ds(part * half, half),)
        if part == 2:
            return (slice(None), pl.ds(0, few))
        return (slice(None), pl.ds(few, sims - few))

    def region(index, part):
        sem = recv_sem.at[index, 0 if part is None else part]
        return out_ref.at[(index,) + span(part)], sem

    barrier = pltpu.get_barrier_semaphore()
    for peer in (device(y, right), device(y, left), device(across, x)):
        pl.semaphore_signal(barrier, inc=1, device_id=peer, device_id_type=MESH)
    pl.semaphore_wait(barrier, 3)

    mine = slot(y, x)
    own = pltpu.make_async_copy(piece_ref, out_ref.at[mine], local_sem)
    own.start()
    sends = []

    def send(index, part, dest, from_input=False):
        target, sem = region(index, part)
        if from_input:
            source = piece_ref
        else:
            source = region(index, part)[0]
        copy = pltpu.make_async_remote_copy(
            src_ref=source,
            dst_ref=target,
            send_sem=send_sem.at[len(sends)],
            recv_sem=sem,
            device_id=dest,
            device_id_type=MESH,
        )
        copy.start()
        sends.append(copy)

    def arrive(index, part):
        target, sem = region(index, part)
        source = piece_ref.at[span(part)]
        pltpu.make_async_remote_copy(
            src_ref=source,
            dst_ref=target,
            send_sem=send_sem.at[0],
            recv_sem=sem,
            device_id=device(y, right),
            device_id_type=MESH,
        ).wait_recv()

    send(mine, None, device(across, x), from_input=True)
    send(mine, None, device(y, right), from_input=True)
    send(mine, None, device(y, left), from_input=True)
    arrive(slot(y, left), None)
    send(slot(y, left), 0, device(y, right))
    send(slot(y, left), 2, device(across, x))
    arrive(slot(y, right), None)
    send(slot(y, right), 1, device(y, left))
    send(slot(y, right), 2, device(across, x))
    arrive(slot(across, x), None)
    send(slot(across, x), 3, device(y, right))
    send(slot(across, x), 3, device(y, left))
    for part in range(2):
        arrive(slot(y, x + 2), part)
        send(slot(y, x + 2), part, device(across, x))
    for part in (2, 3):
        arrive(slot(across, left), part)
        arrive(slot(across, right), part)
    for part in range(2):
        arrive(slot(across, x + 2), part)
    own.wait()
    for copy in sends:
        copy.wait_send()


def all_gather_rows(piece, n_row):
    n_x = n_row // 2
    assert n_x == 4
    return pl.pallas_call(
        functools.partial(gather_kernel, n_x),
        out_shape=jax.ShapeDtypeStruct((n_row,) + piece.shape, piece.dtype),
        in_specs=[pl.BlockSpec(memory_space=pltpu.VMEM)],
        out_specs=pl.BlockSpec(memory_space=pl.ANY),
        scratch_shapes=[
            pltpu.SemaphoreType.DMA(()),
            pltpu.SemaphoreType.DMA((11,)),
            pltpu.SemaphoreType.DMA((n_row, 4)),
        ],
        compiler_params=pltpu.CompilerParams(collective_id=1, has_side_effects=True),
    )(piece)


def parts_kernel(n_lag, rows_ref, cols_ref, count_ref, lag_ref, hist_ref, tiles_ref, out_ref):
    lag = pl.program_id(0)
    slots = tiles_ref.shape[1]
    side = tiles_ref.shape[2]
    halves = hist_ref.shape[3] // side

    @pl.when(lag == 0)
    def _():
        out_ref[...] = jnp.zeros_like(out_ref)

    for k in range(slots):
        @pl.when(k < count_ref[lag])
        def _():
            col = cols_ref[lag, k]
            row = rows_ref[lag, k]
            both = hist_ref[col // halves, 0]
            history = jnp.where(col % halves == 0, both[:, :side], both[:, side:])
            contrib = lax.dot_general(
                history, tiles_ref[0, k], (((1,), (1,)), ((), ())),
                preferred_element_type=jnp.float32,
            )
            half = jnp.where(row % n_lag == lag_ref[0], 0, 1)
            out_ref[half, row // n_lag] += contrib


def stress_parts(history, tiles, rows, cols, count, n_col, n_lag):
    n_row, lags, sims, held = history.shape
    _, slots, side, _ = tiles.shape
    lag = lax.axis_index("lag").astype(jnp.int32).reshape(1)
    grid_spec = pltpu.PrefetchScalarGridSpec(
        num_scalar_prefetch=4,
        grid=(lags,),
        in_specs=[
            pl.BlockSpec((n_row, 1, sims, held), lambda l, *_: (0, l, 0, 0)),
            pl.BlockSpec((1, slots, side, side), lambda l, *_: (l, 0, 0, 0)),
        ],
        out_specs=pl.BlockSpec((2, n_col, sims, side), lambda l, *_: (0, 0, 0, 0)),
    )
    return pl.pallas_call(
        functools.partial(parts_kernel, n_lag),
        out_shape=jax.ShapeDtypeStruct((2, n_col, sims, side), jnp.float32),
        grid_spec=grid_spec,
        compiler_params=pltpu.CompilerParams(vmem_limit_bytes=48 * 1024 * 1024),
    )(rows, cols, count, lag, history, tiles)


def local(
    n_row,
    n_col,
    n_lag,
    history,
    kernel_tiles,
    tile_rows,
    tile_cols,
    tile_count,
    base_stress,
    prev_rate,
    direct_effect,
    state_var,
):
    gathered = all_gather_rows(history[:, 0], n_row)
    tile_side = kernel_tiles.shape[4]
    parts = stress_parts(gathered, kernel_tiles[0, 0], tile_rows[0, 0],
                         tile_cols[0, 0], tile_count[0, 0], n_col, n_lag)
    stress_change = reduce_scatter(parts, n_col)
    driving = base_stress + stress_change
    factor = jnp.exp(state_var) / 2.0
    velocity = prev_rate
    for step in range(NEWTON):
        scaled = velocity * factor
        misfit = direct_effect * inverse_sinh(scaled) + 0.5 * velocity - driving
        slope = direct_effect * factor / jnp.sqrt(1.0 + scaled * scaled) + 0.5
        velocity = velocity - misfit / slope
    return (stress_change, velocity)


def solution(mesh):
    return jax.shard_map(
        functools.partial(local, mesh.shape["row"], mesh.shape["col"], mesh.shape["lag"]),
        mesh=mesh,
        in_specs=(
            P("lag", "col", None, "row"),
            P("row", "col", "lag", None, None, None),
            P("row", "col", "lag", None),
            P("row", "col", "lag", None),
            P("row", "col", "lag"),
            P(None, ("row", "col", "lag")),
            P(None, ("row", "col", "lag")),
            P(None, ("row", "col", "lag")),
            P(None, ("row", "col", "lag")),
        ),
        out_specs=(P(None, ("row", "col", "lag")), P(None, ("row", "col", "lag"))),
        check_vma=False,
    )
```

```python
import functools

import jax
import jax.numpy as jnp
from jax import lax
from jax.experimental import pallas as pl
from jax.experimental.pallas import tpu as pltpu
from jax.sharding import PartitionSpec as P

NEWTON = 4
MESH = pl.DeviceIdType.MESH


def inverse_sinh(value):
    magnitude = jnp.abs(value)
    return jnp.sign(value) * jnp.log(magnitude + jnp.sqrt(1.0 + magnitude * magnitude))


def ring_kernel(n_z, n_pieces, part_ref, out_ref, recv, forward, final, cross, mate,
                send_sem, recv_sem, cross_sem, mate_sem):
    row = lax.axis_index("row")
    col = lax.axis_index("col")
    lag = lax.axis_index("lag")
    z = col // 2
    y_hi = col % 2
    up = lax.rem(z + 1, n_z)
    down = lax.rem(z + n_z - 1, n_z)
    rows = part_ref.shape[2] // n_pieces
    longer = n_z // 2
    shorter = n_z - 1 - longer

    def device(zz, yy):
        return (row, zz * 2 + yy, lag)

    def length(way, side):
        return longer if way == side else shorter

    partner = (row, col, 1 - lag)
    barrier = pltpu.get_barrier_semaphore()
    for peer in (device(up, y_hi), device(down, y_hi), device(z, 1 - y_hi), partner):
        pl.semaphore_signal(barrier, inc=1, device_id=peer, device_id_type=MESH)
    pl.semaphore_wait(barrier, 4)

    def chain_block(step, side, way):
        chain = length(way, side)
        if side == 0:
            target = lax.rem(z + chain - step, n_z)
        else:
            target = lax.rem(z + n_z - chain + step, n_z)
        return target * 2 + way

    order = []
    for step in range(longer):
        for side in range(2):
            for way in range(2):
                if step < length(way, side):
                    order.append(chain_block(step, side, way))
    order += [z * 2 + way for way in range(2)]
    handed = {}
    for index, block in enumerate(order):
        copy = pltpu.make_async_remote_copy(
            src_ref=part_ref.at[1, block],
            dst_ref=mate.at[block],
            send_sem=mate_sem.at[0, index],
            recv_sem=mate_sem.at[1, index],
            device_id=partner,
            device_id_type=MESH,
        )
        copy.start()
        handed[index] = copy
    ready = set()

    def own(index, span):
        if index not in ready:
            handed[index].wait_recv()
            ready.add(index)
        block = order[index]
        return part_ref[0, block, span] + mate[block, span]

    copies = {}
    for step in range(longer):
        for piece in range(n_pieces):
            span = pl.ds(piece * rows, rows)
            for side in range(2):
                for way in range(2):
                    if step >= length(way, side):
                        continue
                    dest = device(up, y_hi) if side == 0 else device(down, y_hi)
                    index = len([1 for st in range(step) for sd in range(2) for w in range(2)
                                 if st < length(w, sd)])
                    index += len([1 for sd in range(side) for w in range(2)
                                  if step < length(w, sd)])
                    index += len([1 for w in range(way) if step < length(w, side)])
                    if step == 0:
                        forward[side, way, step, piece] = own(index, span)
                    else:
                        copies[side, way, step - 1, piece].wait_recv()
                        forward[side, way, step, piece] = (
                            recv[side, way, step - 1, piece] + own(index, span)
                        )
                    source = forward.at[side, way, step, piece]
                    copy = pltpu.make_async_remote_copy(
                        src_ref=source,
                        dst_ref=recv.at[side, way, step, piece],
                        send_sem=send_sem.at[side, way, step, piece],
                        recv_sem=recv_sem.at[side, way, step, piece],
                        device_id=dest,
                        device_id_type=MESH,
                    )
                    copy.start()
                    copies[side, way, step, piece] = copy

    handoffs = []
    for piece in range(n_pieces):
        span = pl.ds(piece * rows, rows)
        for way in range(2):
            total = own(len(order) - 2 + way, span)
            for side in range(2):
                last = length(way, side) - 1
                copies[side, way, last, piece].wait_recv()
                total = total + recv[side, way, last, piece]
            final[way, piece] = total
        handoff = pltpu.make_async_remote_copy(
            src_ref=final.at[1 - y_hi, piece],
            dst_ref=cross.at[piece],
            send_sem=cross_sem.at[0, piece],
            recv_sem=cross_sem.at[1, piece],
            device_id=device(z, 1 - y_hi),
            device_id_type=MESH,
        )
        handoff.start()
        handoffs.append(handoff)
    for piece in range(n_pieces):
        handoffs[piece].wait_recv()
        out_ref[pl.ds(piece * rows, rows), :] = final[y_hi, piece] + cross[piece]
    for handoff in handoffs:
        handoff.wait_send()
    for copy in copies.values():
        copy.wait_send()
    for copy in handed.values():
        copy.wait_send()


def reduce_scatter(part, n_col, n_pieces=2):
    _, group, sims, tile = part.shape
    n_z = n_col // 2
    longer = n_z // 2
    rows = sims // n_pieces
    return pl.pallas_call(
        functools.partial(ring_kernel, n_z, n_pieces),
        out_shape=jax.ShapeDtypeStruct((sims, tile), jnp.float32),
        in_specs=[pl.BlockSpec(memory_space=pltpu.VMEM)],
        out_specs=pl.BlockSpec(memory_space=pltpu.VMEM),
        scratch_shapes=[
            pltpu.VMEM((2, 2, longer, n_pieces, rows, tile), jnp.float32),
            pltpu.VMEM((2, 2, longer, n_pieces, rows, tile), jnp.float32),
            pltpu.VMEM((2, n_pieces, rows, tile), jnp.float32),
            pltpu.VMEM((n_pieces, rows, tile), jnp.float32),
            pltpu.VMEM((group, sims, tile), jnp.float32),
            pltpu.SemaphoreType.DMA((2, 2, longer, n_pieces)),
            pltpu.SemaphoreType.DMA((2, 2, longer, n_pieces)),
            pltpu.SemaphoreType.DMA((2, n_pieces)),
            pltpu.SemaphoreType.DMA((2, group)),
        ],
        compiler_params=pltpu.CompilerParams(
            collective_id=0, has_side_effects=True, vmem_limit_bytes=48 * 1024 * 1024
        ),
    )(part)


def gather_kernel(n_x, piece_ref, out_ref, local_sem, send_sem, recv_sem):
    me = lax.axis_index("row")
    col = lax.axis_index("col")
    lag = lax.axis_index("lag")
    y = me // n_x
    x = me % n_x
    right = x + 1
    left = x + n_x - 1
    across = 1 - y
    half = piece_ref.shape[0] // 2

    def slot(yy, xx):
        return yy * n_x + lax.rem(xx, n_x)

    def device(yy, xx):
        return (slot(yy, xx), col, lag)

    few = 16
    sims = piece_ref.shape[1]

    def span(part):
        if part is None:
            return (slice(None),)
        if part < 2:
            return (pl.ds(part * half, half),)
        if part == 2:
            return (slice(None), pl.ds(0, few))
        return (slice(None), pl.ds(few, sims - few))

    def region(index, part):
        sem = recv_sem.at[index, 0 if part is None else part]
        return out_ref.at[(index,) + span(part)], sem

    barrier = pltpu.get_barrier_semaphore()
    for peer in (device(y, right), device(y, left), device(across, x)):
        pl.semaphore_signal(barrier, inc=1, device_id=peer, device_id_type=MESH)
    pl.semaphore_wait(barrier, 3)

    mine = slot(y, x)
    own = pltpu.make_async_copy(piece_ref, out_ref.at[mine], local_sem)
    own.start()
    sends = []

    def send(index, part, dest, from_input=False):
        target, sem = region(index, part)
        if from_input:
            source = piece_ref
        else:
            source = region(index, part)[0]
        copy = pltpu.make_async_remote_copy(
            src_ref=source,
            dst_ref=target,
            send_sem=send_sem.at[len(sends)],
            recv_sem=sem,
            device_id=dest,
            device_id_type=MESH,
        )
        copy.start()
        sends.append(copy)

    def arrive(index, part):
        target, sem = region(index, part)
        source = piece_ref.at[span(part)]
        pltpu.make_async_remote_copy(
            src_ref=source,
            dst_ref=target,
            send_sem=send_sem.at[0],
            recv_sem=sem,
            device_id=device(y, right),
            device_id_type=MESH,
        ).wait_recv()

    send(mine, None, device(across, x), from_input=True)
    send(mine, None, device(y, right), from_input=True)
    send(mine, None, device(y, left), from_input=True)
    arrive(slot(y, left), None)
    send(slot(y, left), 0, device(y, right))
    send(slot(y, left), 2, device(across, x))
    arrive(slot(y, right), None)
    send(slot(y, right), 1, device(y, left))
    send(slot(y, right), 2, device(across, x))
    arrive(slot(across, x), None)
    send(slot(across, x), 3, device(y, right))
    send(slot(across, x), 3, device(y, left))
    for part in range(2):
        arrive(slot(y, x + 2), part)
        send(slot(y, x + 2), part, device(across, x))
    for part in (2, 3):
        arrive(slot(across, left), part)
        arrive(slot(across, right), part)
    for part in range(2):
        arrive(slot(across, x + 2), part)
    own.wait()
    for copy in sends:
        copy.wait_send()


def all_gather_rows(piece, n_row):
    n_x = n_row // 2
    assert n_x == 4
    return pl.pallas_call(
        functools.partial(gather_kernel, n_x),
        out_shape=jax.ShapeDtypeStruct((n_row,) + piece.shape, piece.dtype),
        in_specs=[pl.BlockSpec(memory_space=pltpu.VMEM)],
        out_specs=pl.BlockSpec(memory_space=pl.ANY),
        scratch_shapes=[
            pltpu.SemaphoreType.DMA(()),
            pltpu.SemaphoreType.DMA((11,)),
            pltpu.SemaphoreType.DMA((n_row, 4)),
        ],
        compiler_params=pltpu.CompilerParams(collective_id=1, has_side_effects=True),
    )(piece)


def parts_kernel(n_lag, rows_ref, cols_ref, count_ref, lag_ref, hist_ref, tiles_ref, out_ref):
    lag = pl.program_id(0)
    slots = tiles_ref.shape[1]
    side = tiles_ref.shape[2]
    halves = hist_ref.shape[3] // side

    @pl.when(lag == 0)
    def _():
        out_ref[...] = jnp.zeros_like(out_ref)

    for k in range(slots):
        @pl.when(k < count_ref[lag])
        def _():
            col = cols_ref[lag, k]
            row = rows_ref[lag, k]
            both = hist_ref[col // halves, 0]
            history = jnp.where(col % halves == 0, both[:, :side], both[:, side:])
            contrib = lax.dot_general(
                history, tiles_ref[0, k], (((1,), (1,)), ((), ())),
                preferred_element_type=jnp.float32,
            )
            half = jnp.where(row % n_lag == lag_ref[0], 0, 1)
            out_ref[half, row // n_lag] += contrib


def stress_parts(history, tiles, rows, cols, count, n_col, n_lag):
    n_row, lags, sims, held = history.shape
    _, slots, side, _ = tiles.shape
    lag = lax.axis_index("lag").astype(jnp.int32).reshape(1)
    grid_spec = pltpu.PrefetchScalarGridSpec(
        num_scalar_prefetch=4,
        grid=(lags,),
        in_specs=[
            pl.BlockSpec((n_row, 1, sims, held), lambda l, *_: (0, l, 0, 0)),
            pl.BlockSpec((1, slots, side, side), lambda l, *_: (l, 0, 0, 0)),
        ],
        out_specs=pl.BlockSpec((2, n_col, sims, side), lambda l, *_: (0, 0, 0, 0)),
    )
    return pl.pallas_call(
        functools.partial(parts_kernel, n_lag),
        out_shape=jax.ShapeDtypeStruct((2, n_col, sims, side), jnp.float32),
        grid_spec=grid_spec,
        compiler_params=pltpu.CompilerParams(vmem_limit_bytes=48 * 1024 * 1024),
    )(rows, cols, count, lag, history, tiles)


def local(
    n_row,
    n_col,
    n_lag,
    history,
    kernel_tiles,
    tile_rows,
    tile_cols,
    tile_count,
    base_stress,
    prev_rate,
    direct_effect,
    state_var,
):
    gathered = all_gather_rows(history[:, 0], n_row)
    tile_side = kernel_tiles.shape[4]
    parts = stress_parts(gathered, kernel_tiles[0, 0], tile_rows[0, 0],
                         tile_cols[0, 0], tile_count[0, 0], n_col, n_lag)
    stress_change = reduce_scatter(parts, n_col)
    driving = base_stress + stress_change
    factor = jnp.exp(state_var) / 2.0
    velocity = prev_rate
    for step in range(NEWTON):
        scaled = velocity * factor
        misfit = direct_effect * inverse_sinh(scaled) + 0.5 * velocity - driving
        slope = direct_effect * factor / jnp.sqrt(1.0 + scaled * scaled) + 0.5
        velocity = velocity - misfit / slope
    return (stress_change, velocity)


def solution(mesh):
    return jax.shard_map(
        functools.partial(local, mesh.shape["row"], mesh.shape["col"], mesh.shape["lag"]),
        mesh=mesh,
        in_specs=(
            P("lag", "col", None, "row"),
            P("row", "col", "lag", None, None, None),
            P("row", "col", "lag", None),
            P("row", "col", "lag", None),
            P("row", "col", "lag"),
            P(None, ("row", "col", "lag")),
            P(None, ("row", "col", "lag")),
            P(None, ("row", "col", "lag")),
            P(None, ("row", "col", "lag")),
        ),
        out_specs=(P(None, ("row", "col", "lag")), P(None, ("row", "col", "lag"))),
        check_vma=False,
    )
```

```python
import functools

import jax
import jax.numpy as jnp
from jax import lax
from jax.experimental import pallas as pl
from jax.experimental.pallas import tpu as pltpu
from jax.sharding import PartitionSpec as P

NEWTON = 4
MESH = pl.DeviceIdType.MESH


def inverse_sinh(value):
    magnitude = jnp.abs(value)
    return jnp.sign(value) * jnp.log(magnitude + jnp.sqrt(1.0 + magnitude * magnitude))


def ring_kernel(n_z, n_pieces, part_ref, out_ref, recv, forward, final, cross, mate,
                send_sem, recv_sem, cross_sem, mate_sem):
    row = lax.axis_index("row")
    col = lax.axis_index("col")
    lag = lax.axis_index("lag")
    z = col // 2
    y_hi = col % 2
    up = lax.rem(z + 1, n_z)
    down = lax.rem(z + n_z - 1, n_z)
    rows = part_ref.shape[2] // n_pieces
    longer = n_z // 2
    shorter = n_z - 1 - longer

    def device(zz, yy):
        return (row, zz * 2 + yy, lag)

    def length(way, side):
        return longer if way == side else shorter

    partner = (row, col, 1 - lag)
    barrier = pltpu.get_barrier_semaphore()
    for peer in (device(up, y_hi), device(down, y_hi), device(z, 1 - y_hi), partner):
        pl.semaphore_signal(barrier, inc=1, device_id=peer, device_id_type=MESH)
    pl.semaphore_wait(barrier, 4)

    def chain_block(step, side, way):
        chain = length(way, side)
        if side == 0:
            target = lax.rem(z + chain - step, n_z)
        else:
            target = lax.rem(z + n_z - chain + step, n_z)
        return target * 2 + way

    order = []
    for step in range(longer):
        for side in range(2):
            for way in range(2):
                if step < length(way, side):
                    order.append(chain_block(step, side, way))
    order += [z * 2 + way for way in range(2)]
    handed = {}
    for index, block in enumerate(order):
        copy = pltpu.make_async_remote_copy(
            src_ref=part_ref.at[1, block],
            dst_ref=mate.at[block],
            send_sem=mate_sem.at[0, index],
            recv_sem=mate_sem.at[1, index],
            device_id=partner,
            device_id_type=MESH,
        )
        copy.start()
        handed[index] = copy
    ready = set()

    def own(index, span):
        if index not in ready:
            handed[index].wait_recv()
            ready.add(index)
        block = order[index]
        return part_ref[0, block, span] + mate[block, span]

    copies = {}
    for step in range(longer):
        for piece in range(n_pieces):
            span = pl.ds(piece * rows, rows)
            for side in range(2):
                for way in range(2):
                    if step >= length(way, side):
                        continue
                    dest = device(up, y_hi) if side == 0 else device(down, y_hi)
                    index = len([1 for st in range(step) for sd in range(2) for w in range(2)
                                 if st < length(w, sd)])
                    index += len([1 for sd in range(side) for w in range(2)
                                  if step < length(w, sd)])
                    index += len([1 for w in range(way) if step < length(w, side)])
                    if step == 0:
                        forward[side, way, step, piece] = own(index, span)
                    else:
                        copies[side, way, step - 1, piece].wait_recv()
                        forward[side, way, step, piece] = (
                            recv[side, way, step - 1, piece] + own(index, span)
                        )
                    source = forward.at[side, way, step, piece]
                    copy = pltpu.make_async_remote_copy(
                        src_ref=source,
                        dst_ref=recv.at[side, way, step, piece],
                        send_sem=send_sem.at[side, way, step, piece],
                        recv_sem=recv_sem.at[side, way, step, piece],
                        device_id=dest,
                        device_id_type=MESH,
                    )
                    copy.start()
                    copies[side, way, step, piece] = copy

    handoffs = []
    for piece in range(n_pieces):
        span = pl.ds(piece * rows, rows)
        for way in range(2):
            total = own(len(order) - 2 + way, span)
            for side in range(2):
                last = length(way, side) - 1
                copies[side, way, last, piece].wait_recv()
                total = total + recv[side, way, last, piece]
            final[way, piece] = total
        handoff = pltpu.make_async_remote_copy(
            src_ref=final.at[1 - y_hi, piece],
            dst_ref=cross.at[piece],
            send_sem=cross_sem.at[0, piece],
            recv_sem=cross_sem.at[1, piece],
            device_id=device(z, 1 - y_hi),
            device_id_type=MESH,
        )
        handoff.start()
        handoffs.append(handoff)
    for piece in range(n_pieces):
        handoffs[piece].wait_recv()
        out_ref[pl.ds(piece * rows, rows), :] = final[y_hi, piece] + cross[piece]
    for handoff in handoffs:
        handoff.wait_send()
    for copy in copies.values():
        copy.wait_send()
    for copy in handed.values():
        copy.wait_send()


def reduce_scatter(part, n_col, n_pieces=1):
    _, group, sims, tile = part.shape
    n_z = n_col // 2
    longer = n_z // 2
    rows = sims // n_pieces
    return pl.pallas_call(
        functools.partial(ring_kernel, n_z, n_pieces),
        out_shape=jax.ShapeDtypeStruct((sims, tile), jnp.float32),
        in_specs=[pl.BlockSpec(memory_space=pltpu.VMEM)],
        out_specs=pl.BlockSpec(memory_space=pltpu.VMEM),
        scratch_shapes=[
            pltpu.VMEM((2, 2, longer, n_pieces, rows, tile), jnp.float32),
            pltpu.VMEM((2, 2, longer, n_pieces, rows, tile), jnp.float32),
            pltpu.VMEM((2, n_pieces, rows, tile), jnp.float32),
            pltpu.VMEM((n_pieces, rows, tile), jnp.float32),
            pltpu.VMEM((group, sims, tile), jnp.float32),
            pltpu.SemaphoreType.DMA((2, 2, longer, n_pieces)),
            pltpu.SemaphoreType.DMA((2, 2, longer, n_pieces)),
            pltpu.SemaphoreType.DMA((2, n_pieces)),
            pltpu.SemaphoreType.DMA((2, group)),
        ],
        compiler_params=pltpu.CompilerParams(
            collective_id=0, has_side_effects=True, vmem_limit_bytes=48 * 1024 * 1024
        ),
    )(part)


def gather_kernel(n_x, piece_ref, out_ref, local_sem, send_sem, recv_sem):
    me = lax.axis_index("row")
    col = lax.axis_index("col")
    lag = lax.axis_index("lag")
    y = me // n_x
    x = me % n_x
    right = x + 1
    left = x + n_x - 1
    across = 1 - y
    half = piece_ref.shape[0] // 2

    def slot(yy, xx):
        return yy * n_x + lax.rem(xx, n_x)

    def device(yy, xx):
        return (slot(yy, xx), col, lag)

    few = 16
    sims = piece_ref.shape[1]

    def span(part):
        if part is None:
            return (slice(None),)
        if part < 2:
            return (pl.ds(part * half, half),)
        if part == 2:
            return (slice(None), pl.ds(0, few))
        return (slice(None), pl.ds(few, sims - few))

    def region(index, part):
        sem = recv_sem.at[index, 0 if part is None else part]
        return out_ref.at[(index,) + span(part)], sem

    barrier = pltpu.get_barrier_semaphore()
    for peer in (device(y, right), device(y, left), device(across, x)):
        pl.semaphore_signal(barrier, inc=1, device_id=peer, device_id_type=MESH)
    pl.semaphore_wait(barrier, 3)

    mine = slot(y, x)
    own = pltpu.make_async_copy(piece_ref, out_ref.at[mine], local_sem)
    own.start()
    sends = []

    def send(index, part, dest, from_input=False):
        target, sem = region(index, part)
        if from_input:
            source = piece_ref
        else:
            source = region(index, part)[0]
        copy = pltpu.make_async_remote_copy(
            src_ref=source,
            dst_ref=target,
            send_sem=send_sem.at[len(sends)],
            recv_sem=sem,
            device_id=dest,
            device_id_type=MESH,
        )
        copy.start()
        sends.append(copy)

    def arrive(index, part):
        target, sem = region(index, part)
        source = piece_ref.at[span(part)]
        pltpu.make_async_remote_copy(
            src_ref=source,
            dst_ref=target,
            send_sem=send_sem.at[0],
            recv_sem=sem,
            device_id=device(y, right),
            device_id_type=MESH,
        ).wait_recv()

    send(mine, None, device(across, x), from_input=True)
    send(mine, None, device(y, right), from_input=True)
    send(mine, None, device(y, left), from_input=True)
    arrive(slot(y, left), None)
    send(slot(y, left), 0, device(y, right))
    send(slot(y, left), 2, device(across, x))
    arrive(slot(y, right), None)
    send(slot(y, right), 1, device(y, left))
    send(slot(y, right), 2, device(across, x))
    arrive(slot(across, x), None)
    send(slot(across, x), 3, device(y, right))
    send(slot(across, x), 3, device(y, left))
    for part in range(2):
        arrive(slot(y, x + 2), part)
        send(slot(y, x + 2), part, device(across, x))
    for part in (2, 3):
        arrive(slot(across, left), part)
        arrive(slot(across, right), part)
    for part in range(2):
        arrive(slot(across, x + 2), part)
    own.wait()
    for copy in sends:
        copy.wait_send()


def all_gather_rows(piece, n_row):
    n_x = n_row // 2
    assert n_x == 4
    return pl.pallas_call(
        functools.partial(gather_kernel, n_x),
        out_shape=jax.ShapeDtypeStruct((n_row,) + piece.shape, piece.dtype),
        in_specs=[pl.BlockSpec(memory_space=pltpu.VMEM)],
        out_specs=pl.BlockSpec(memory_space=pl.ANY),
        scratch_shapes=[
            pltpu.SemaphoreType.DMA(()),
            pltpu.SemaphoreType.DMA((11,)),
            pltpu.SemaphoreType.DMA((n_row, 4)),
        ],
        compiler_params=pltpu.CompilerParams(collective_id=1, has_side_effects=True),
    )(piece)


def parts_kernel(n_lag, rows_ref, cols_ref, count_ref, lag_ref, hist_ref, tiles_ref, out_ref):
    lag = pl.program_id(0)
    slots = tiles_ref.shape[1]
    side = tiles_ref.shape[2]
    halves = hist_ref.shape[3] // side

    @pl.when(lag == 0)
    def _():
        out_ref[...] = jnp.zeros_like(out_ref)

    for k in range(slots):
        @pl.when(k < count_ref[lag])
        def _():
            col = cols_ref[lag, k]
            row = rows_ref[lag, k]
            both = hist_ref[col // halves, 0]
            history = jnp.where(col % halves == 0, both[:, :side], both[:, side:])
            contrib = lax.dot_general(
                history, tiles_ref[0, k], (((1,), (1,)), ((), ())),
                preferred_element_type=jnp.float32,
            )
            half = jnp.where(row % n_lag == lag_ref[0], 0, 1)
            out_ref[half, row // n_lag] += contrib


def stress_parts(history, tiles, rows, cols, count, n_col, n_lag):
    n_row, lags, sims, held = history.shape
    _, slots, side, _ = tiles.shape
    lag = lax.axis_index("lag").astype(jnp.int32).reshape(1)
    grid_spec = pltpu.PrefetchScalarGridSpec(
        num_scalar_prefetch=4,
        grid=(lags,),
        in_specs=[
            pl.BlockSpec((n_row, 1, sims, held), lambda l, *_: (0, l, 0, 0)),
            pl.BlockSpec((1, slots, side, side), lambda l, *_: (l, 0, 0, 0)),
        ],
        out_specs=pl.BlockSpec((2, n_col, sims, side), lambda l, *_: (0, 0, 0, 0)),
    )
    return pl.pallas_call(
        functools.partial(parts_kernel, n_lag),
        out_shape=jax.ShapeDtypeStruct((2, n_col, sims, side), jnp.float32),
        grid_spec=grid_spec,
        compiler_params=pltpu.CompilerParams(vmem_limit_bytes=48 * 1024 * 1024),
    )(rows, cols, count, lag, history, tiles)


def local(
    n_row,
    n_col,
    n_lag,
    history,
    kernel_tiles,
    tile_rows,
    tile_cols,
    tile_count,
    base_stress,
    prev_rate,
    direct_effect,
    state_var,
):
    gathered = all_gather_rows(history[:, 0], n_row)
    tile_side = kernel_tiles.shape[4]
    parts = stress_parts(gathered, kernel_tiles[0, 0], tile_rows[0, 0],
                         tile_cols[0, 0], tile_count[0, 0], n_col, n_lag)
    stress_change = reduce_scatter(parts, n_col)
    driving = base_stress + stress_change
    factor = jnp.exp(state_var) / 2.0
    velocity = prev_rate
    for step in range(NEWTON):
        scaled = velocity * factor
        misfit = direct_effect * inverse_sinh(scaled) + 0.5 * velocity - driving
        slope = direct_effect * factor / jnp.sqrt(1.0 + scaled * scaled) + 0.5
        velocity = velocity - misfit / slope
    return (stress_change, velocity)


def solution(mesh):
    return jax.shard_map(
        functools.partial(local, mesh.shape["row"], mesh.shape["col"], mesh.shape["lag"]),
        mesh=mesh,
        in_specs=(
            P("lag", "col", None, "row"),
            P("row", "col", "lag", None, None, None),
            P("row", "col", "lag", None),
            P("row", "col", "lag", None),
            P("row", "col", "lag"),
            P(None, ("row", "col", "lag")),
            P(None, ("row", "col", "lag")),
            P(None, ("row", "col", "lag")),
            P(None, ("row", "col", "lag")),
        ),
        out_specs=(P(None, ("row", "col", "lag")), P(None, ("row", "col", "lag"))),
        check_vma=False,
    )
```

```python
import functools

import jax
import jax.numpy as jnp
from jax import lax
from jax.experimental import pallas as pl
from jax.experimental.pallas import tpu as pltpu
from jax.sharding import PartitionSpec as P

NEWTON = 4
MESH = pl.DeviceIdType.MESH


def inverse_sinh(value):
    magnitude = jnp.abs(value)
    return jnp.sign(value) * jnp.log(magnitude + jnp.sqrt(1.0 + magnitude * magnitude))


def ring_kernel(n_z, n_pieces, part_ref, out_ref, recv, forward, final, cross, mate,
                send_sem, recv_sem, cross_sem, mate_sem):
    row = lax.axis_index("row")
    col = lax.axis_index("col")
    lag = lax.axis_index("lag")
    z = col // 2
    y_hi = col % 2
    up = lax.rem(z + 1, n_z)
    down = lax.rem(z + n_z - 1, n_z)
    rows = part_ref.shape[2] // n_pieces
    longer = n_z // 2
    shorter = n_z - 1 - longer

    def device(zz, yy):
        return (row, zz * 2 + yy, lag)

    def length(way, side):
        return longer if way == side else shorter

    partner = (row, col, 1 - lag)
    barrier = pltpu.get_barrier_semaphore()
    for peer in (device(up, y_hi), device(down, y_hi), device(z, 1 - y_hi), partner):
        pl.semaphore_signal(barrier, inc=1, device_id=peer, device_id_type=MESH)
    pl.semaphore_wait(barrier, 4)

    def chain_block(step, side, way):
        chain = length(way, side)
        if side == 0:
            target = lax.rem(z + chain - step, n_z)
        else:
            target = lax.rem(z + n_z - chain + step, n_z)
        return target * 2 + way

    order = []
    for step in range(longer):
        for side in range(2):
            for way in range(2):
                if step < length(way, side):
                    order.append(chain_block(step, side, way))
    order += [z * 2 + way for way in range(2)]
    handed = {}
    for index, block in enumerate(order):
        copy = pltpu.make_async_remote_copy(
            src_ref=part_ref.at[1, block],
            dst_ref=mate.at[block],
            send_sem=mate_sem.at[0, index],
            recv_sem=mate_sem.at[1, index],
            device_id=partner,
            device_id_type=MESH,
        )
        copy.start()
        handed[index] = copy
    ready = set()

    def own(index, span):
        if index not in ready:
            handed[index].wait_recv()
            ready.add(index)
        block = order[index]
        return part_ref[0, block, span] + mate[block, span]

    copies = {}
    for step in range(longer):
        for piece in range(n_pieces):
            span = pl.ds(piece * rows, rows)
            for side in range(2):
                for way in range(2):
                    if step >= length(way, side):
                        continue
                    dest = device(up, y_hi) if side == 0 else device(down, y_hi)
                    index = len([1 for st in range(step) for sd in range(2) for w in range(2)
                                 if st < length(w, sd)])
                    index += len([1 for sd in range(side) for w in range(2)
                                  if step < length(w, sd)])
                    index += len([1 for w in range(way) if step < length(w, side)])
                    if step == 0:
                        forward[side, way, step, piece] = own(index, span)
                    else:
                        copies[side, way, step - 1, piece].wait_recv()
                        forward[side, way, step, piece] = (
                            recv[side, way, step - 1, piece] + own(index, span)
                        )
                    source = forward.at[side, way, step, piece]
                    copy = pltpu.make_async_remote_copy(
                        src_ref=source,
                        dst_ref=recv.at[side, way, step, piece],
                        send_sem=send_sem.at[side, way, step, piece],
                        recv_sem=recv_sem.at[side, way, step, piece],
                        device_id=dest,
                        device_id_type=MESH,
                    )
                    copy.start()
                    copies[side, way, step, piece] = copy

    handoffs = []
    for piece in range(n_pieces):
        span = pl.ds(piece * rows, rows)
        for way in range(2):
            total = own(len(order) - 2 + way, span)
            for side in range(2):
                last = length(way, side) - 1
                copies[side, way, last, piece].wait_recv()
                total = total + recv[side, way, last, piece]
            final[way, piece] = total
        handoff = pltpu.make_async_remote_copy(
            src_ref=final.at[1 - y_hi, piece],
            dst_ref=cross.at[piece],
            send_sem=cross_sem.at[0, piece],
            recv_sem=cross_sem.at[1, piece],
            device_id=device(z, 1 - y_hi),
            device_id_type=MESH,
        )
        handoff.start()
        handoffs.append(handoff)
    for piece in range(n_pieces):
        handoffs[piece].wait_recv()
        out_ref[pl.ds(piece * rows, rows), :] = final[y_hi, piece] + cross[piece]
    for handoff in handoffs:
        handoff.wait_send()
    for copy in copies.values():
        copy.wait_send()
    for copy in handed.values():
        copy.wait_send()


def reduce_scatter(part, n_col, n_pieces=2):
    _, group, sims, tile = part.shape
    n_z = n_col // 2
    longer = n_z // 2
    rows = sims // n_pieces
    return pl.pallas_call(
        functools.partial(ring_kernel, n_z, n_pieces),
        out_shape=jax.ShapeDtypeStruct((sims, tile), jnp.float32),
        in_specs=[pl.BlockSpec(memory_space=pltpu.VMEM)],
        out_specs=pl.BlockSpec(memory_space=pltpu.VMEM),
        scratch_shapes=[
            pltpu.VMEM((2, 2, longer, n_pieces, rows, tile), jnp.float32),
            pltpu.VMEM((2, 2, longer, n_pieces, rows, tile), jnp.float32),
            pltpu.VMEM((2, n_pieces, rows, tile), jnp.float32),
            pltpu.VMEM((n_pieces, rows, tile), jnp.float32),
            pltpu.VMEM((group, sims, tile), jnp.float32),
            pltpu.SemaphoreType.DMA((2, 2, longer, n_pieces)),
            pltpu.SemaphoreType.DMA((2, 2, longer, n_pieces)),
            pltpu.SemaphoreType.DMA((2, n_pieces)),
            pltpu.SemaphoreType.DMA((2, group)),
        ],
        compiler_params=pltpu.CompilerParams(
            collective_id=0, has_side_effects=True, vmem_limit_bytes=48 * 1024 * 1024
        ),
    )(part)


def gather_kernel(n_x, piece_ref, out_ref, local_sem, send_sem, recv_sem):
    me = lax.axis_index("row")
    col = lax.axis_index("col")
    lag = lax.axis_index("lag")
    y = me // n_x
    x = me % n_x
    right = x + 1
    left = x + n_x - 1
    across = 1 - y
    half = piece_ref.shape[0] // 2

    def slot(yy, xx):
        return yy * n_x + lax.rem(xx, n_x)

    def device(yy, xx):
        return (slot(yy, xx), col, lag)

    few = 24
    sims = piece_ref.shape[1]

    def span(part):
        if part is None:
            return (slice(None),)
        if part < 2:
            return (pl.ds(part * half, half),)
        if part == 2:
            return (slice(None), pl.ds(0, few))
        return (slice(None), pl.ds(few, sims - few))

    def region(index, part):
        sem = recv_sem.at[index, 0 if part is None else part]
        return out_ref.at[(index,) + span(part)], sem

    barrier = pltpu.get_barrier_semaphore()
    for peer in (device(y, right), device(y, left), device(across, x)):
        pl.semaphore_signal(barrier, inc=1, device_id=peer, device_id_type=MESH)
    pl.semaphore_wait(barrier, 3)

    mine = slot(y, x)
    own = pltpu.make_async_copy(piece_ref, out_ref.at[mine], local_sem)
    own.start()
    sends = []

    def send(index, part, dest, from_input=False):
        target, sem = region(index, part)
        if from_input:
            source = piece_ref
        else:
            source = region(index, part)[0]
        copy = pltpu.make_async_remote_copy(
            src_ref=source,
            dst_ref=target,
            send_sem=send_sem.at[len(sends)],
            recv_sem=sem,
            device_id=dest,
            device_id_type=MESH,
        )
        copy.start()
        sends.append(copy)

    def arrive(index, part):
        target, sem = region(index, part)
        source = piece_ref.at[span(part)]
        pltpu.make_async_remote_copy(
            src_ref=source,
            dst_ref=target,
            send_sem=send_sem.at[0],
            recv_sem=sem,
            device_id=device(y, right),
            device_id_type=MESH,
        ).wait_recv()

    send(mine, None, device(across, x), from_input=True)
    send(mine, None, device(y, right), from_input=True)
    send(mine, None, device(y, left), from_input=True)
    arrive(slot(y, left), None)
    send(slot(y, left), 0, device(y, right))
    send(slot(y, left), 2, device(across, x))
    arrive(slot(y, right), None)
    send(slot(y, right), 1, device(y, left))
    send(slot(y, right), 2, device(across, x))
    arrive(slot(across, x), None)
    send(slot(across, x), 3, device(y, right))
    send(slot(across, x), 3, device(y, left))
    for part in range(2):
        arrive(slot(y, x + 2), part)
        send(slot(y, x + 2), part, device(across, x))
    for part in (2, 3):
        arrive(slot(across, left), part)
        arrive(slot(across, right), part)
    for part in range(2):
        arrive(slot(across, x + 2), part)
    own.wait()
    for copy in sends:
        copy.wait_send()


def all_gather_rows(piece, n_row):
    n_x = n_row // 2
    assert n_x == 4
    return pl.pallas_call(
        functools.partial(gather_kernel, n_x),
        out_shape=jax.ShapeDtypeStruct((n_row,) + piece.shape, piece.dtype),
        in_specs=[pl.BlockSpec(memory_space=pltpu.VMEM)],
        out_specs=pl.BlockSpec(memory_space=pl.ANY),
        scratch_shapes=[
            pltpu.SemaphoreType.DMA(()),
            pltpu.SemaphoreType.DMA((11,)),
            pltpu.SemaphoreType.DMA((n_row, 4)),
        ],
        compiler_params=pltpu.CompilerParams(collective_id=1, has_side_effects=True),
    )(piece)


def parts_kernel(n_lag, rows_ref, cols_ref, count_ref, lag_ref, hist_ref, tiles_ref, out_ref):
    lag = pl.program_id(0)
    slots = tiles_ref.shape[1]
    side = tiles_ref.shape[2]
    halves = hist_ref.shape[3] // side

    @pl.when(lag == 0)
    def _():
        out_ref[...] = jnp.zeros_like(out_ref)

    for k in range(slots):
        @pl.when(k < count_ref[lag])
        def _():
            col = cols_ref[lag, k]
            row = rows_ref[lag, k]
            both = hist_ref[col // halves, 0]
            history = jnp.where(col % halves == 0, both[:, :side], both[:, side:])
            contrib = lax.dot_general(
                history, tiles_ref[0, k], (((1,), (1,)), ((), ())),
                preferred_element_type=jnp.float32,
            )
            half = jnp.where(row % n_lag == lag_ref[0], 0, 1)
            out_ref[half, row // n_lag] += contrib


def stress_parts(history, tiles, rows, cols, count, n_col, n_lag):
    n_row, lags, sims, held = history.shape
    _, slots, side, _ = tiles.shape
    lag = lax.axis_index("lag").astype(jnp.int32).reshape(1)
    grid_spec = pltpu.PrefetchScalarGridSpec(
        num_scalar_prefetch=4,
        grid=(lags,),
        in_specs=[
            pl.BlockSpec((n_row, 1, sims, held), lambda l, *_: (0, l, 0, 0)),
            pl.BlockSpec((1, slots, side, side), lambda l, *_: (l, 0, 0, 0)),
        ],
        out_specs=pl.BlockSpec((2, n_col, sims, side), lambda l, *_: (0, 0, 0, 0)),
    )
    return pl.pallas_call(
        functools.partial(parts_kernel, n_lag),
        out_shape=jax.ShapeDtypeStruct((2, n_col, sims, side), jnp.float32),
        grid_spec=grid_spec,
        compiler_params=pltpu.CompilerParams(vmem_limit_bytes=48 * 1024 * 1024),
    )(rows, cols, count, lag, history, tiles)


def local(
    n_row,
    n_col,
    n_lag,
    history,
    kernel_tiles,
    tile_rows,
    tile_cols,
    tile_count,
    base_stress,
    prev_rate,
    direct_effect,
    state_var,
):
    gathered = all_gather_rows(history[:, 0], n_row)
    tile_side = kernel_tiles.shape[4]
    parts = stress_parts(gathered, kernel_tiles[0, 0], tile_rows[0, 0],
                         tile_cols[0, 0], tile_count[0, 0], n_col, n_lag)
    stress_change = reduce_scatter(parts, n_col)
    driving = base_stress + stress_change
    factor = jnp.exp(state_var) / 2.0
    velocity = prev_rate
    for step in range(NEWTON):
        scaled = velocity * factor
        misfit = direct_effect * inverse_sinh(scaled) + 0.5 * velocity - driving
        slope = direct_effect * factor / jnp.sqrt(1.0 + scaled * scaled) + 0.5
        velocity = velocity - misfit / slope
    return (stress_change, velocity)


def solution(mesh):
    return jax.shard_map(
        functools.partial(local, mesh.shape["row"], mesh.shape["col"], mesh.shape["lag"]),
        mesh=mesh,
        in_specs=(
            P("lag", "col", None, "row"),
            P("row", "col", "lag", None, None, None),
            P("row", "col", "lag", None),
            P("row", "col", "lag", None),
            P("row", "col", "lag"),
            P(None, ("row", "col", "lag")),
            P(None, ("row", "col", "lag")),
            P(None, ("row", "col", "lag")),
            P(None, ("row", "col", "lag")),
        ),
        out_specs=(P(None, ("row", "col", "lag")), P(None, ("row", "col", "lag"))),
        check_vma=False,
    )
```

```python
import functools

import jax
import jax.numpy as jnp
from jax import lax
from jax.experimental import pallas as pl
from jax.experimental.pallas import tpu as pltpu
from jax.sharding import PartitionSpec as P

NEWTON = 4
MESH = pl.DeviceIdType.MESH


def inverse_sinh(value):
    magnitude = jnp.abs(value)
    return jnp.sign(value) * jnp.log(magnitude + jnp.sqrt(1.0 + magnitude * magnitude))


def ring_kernel(n_z, n_pieces, part_ref, out_ref, recv, forward, final, cross, mate,
                send_sem, recv_sem, cross_sem, mate_sem):
    row = lax.axis_index("row")
    col = lax.axis_index("col")
    lag = lax.axis_index("lag")
    z = col // 2
    y_hi = col % 2
    up = lax.rem(z + 1, n_z)
    down = lax.rem(z + n_z - 1, n_z)
    rows = part_ref.shape[2] // n_pieces
    longer = n_z // 2
    shorter = n_z - 1 - longer

    def device(zz, yy):
        return (row, zz * 2 + yy, lag)

    def length(way, side):
        return longer if way == side else shorter

    partner = (row, col, 1 - lag)
    barrier = pltpu.get_barrier_semaphore()
    for peer in (device(up, y_hi), device(down, y_hi), device(z, 1 - y_hi), partner):
        pl.semaphore_signal(barrier, inc=1, device_id=peer, device_id_type=MESH)
    pl.semaphore_wait(barrier, 4)

    def chain_block(step, side, way):
        chain = length(way, side)
        if side == 0:
            target = lax.rem(z + chain - step, n_z)
        else:
            target = lax.rem(z + n_z - chain + step, n_z)
        return target * 2 + way

    order = []
    for step in range(longer):
        for side in range(2):
            for way in range(2):
                if step < length(way, side):
                    order.append(chain_block(step, side, way))
    order += [z * 2 + way for way in range(2)]
    handed = {}
    for index, block in enumerate(order):
        for piece in range(n_pieces):
            span = pl.ds(piece * rows, rows)
            copy = pltpu.make_async_remote_copy(
                src_ref=part_ref.at[1, block, span],
                dst_ref=mate.at[block, span],
                send_sem=mate_sem.at[0, index, piece],
                recv_sem=mate_sem.at[1, index, piece],
                device_id=partner,
                device_id_type=MESH,
            )
            copy.start()
            handed[index, piece] = copy

    def own(index, piece):
        handed[index, piece].wait_recv()
        span = pl.ds(piece * rows, rows)
        block = order[index]
        return part_ref[0, block, span] + mate[block, span]

    copies = {}
    for step in range(longer):
        for piece in range(n_pieces):
            span = pl.ds(piece * rows, rows)
            for side in range(2):
                for way in range(2):
                    if step >= length(way, side):
                        continue
                    dest = device(up, y_hi) if side == 0 else device(down, y_hi)
                    index = len([1 for st in range(step) for sd in range(2) for w in range(2)
                                 if st < length(w, sd)])
                    index += len([1 for sd in range(side) for w in range(2)
                                  if step < length(w, sd)])
                    index += len([1 for w in range(way) if step < length(w, side)])
                    if step == 0:
                        forward[side, way, step, piece] = own(index, piece)
                    else:
                        copies[side, way, step - 1, piece].wait_recv()
                        forward[side, way, step, piece] = (
                            recv[side, way, step - 1, piece] + own(index, piece)
                        )
                    source = forward.at[side, way, step, piece]
                    copy = pltpu.make_async_remote_copy(
                        src_ref=source,
                        dst_ref=recv.at[side, way, step, piece],
                        send_sem=send_sem.at[side, way, step, piece],
                        recv_sem=recv_sem.at[side, way, step, piece],
                        device_id=dest,
                        device_id_type=MESH,
                    )
                    copy.start()
                    copies[side, way, step, piece] = copy

    handoffs = []
    for piece in range(n_pieces):
        span = pl.ds(piece * rows, rows)
        for way in range(2):
            total = own(len(order) - 2 + way, piece)
            for side in range(2):
                last = length(way, side) - 1
                copies[side, way, last, piece].wait_recv()
                total = total + recv[side, way, last, piece]
            final[way, piece] = total
        handoff = pltpu.make_async_remote_copy(
            src_ref=final.at[1 - y_hi, piece],
            dst_ref=cross.at[piece],
            send_sem=cross_sem.at[0, piece],
            recv_sem=cross_sem.at[1, piece],
            device_id=device(z, 1 - y_hi),
            device_id_type=MESH,
        )
        handoff.start()
        handoffs.append(handoff)
    for piece in range(n_pieces):
        handoffs[piece].wait_recv()
        out_ref[pl.ds(piece * rows, rows), :] = final[y_hi, piece] + cross[piece]
    for handoff in handoffs:
        handoff.wait_send()
    for copy in copies.values():
        copy.wait_send()
    for copy in handed.values():
        copy.wait_send()


def reduce_scatter(part, n_col, n_pieces=2):
    _, group, sims, tile = part.shape
    n_z = n_col // 2
    longer = n_z // 2
    rows = sims // n_pieces
    return pl.pallas_call(
        functools.partial(ring_kernel, n_z, n_pieces),
        out_shape=jax.ShapeDtypeStruct((sims, tile), jnp.float32),
        in_specs=[pl.BlockSpec(memory_space=pltpu.VMEM)],
        out_specs=pl.BlockSpec(memory_space=pltpu.VMEM),
        scratch_shapes=[
            pltpu.VMEM((2, 2, longer, n_pieces, rows, tile), jnp.float32),
            pltpu.VMEM((2, 2, longer, n_pieces, rows, tile), jnp.float32),
            pltpu.VMEM((2, n_pieces, rows, tile), jnp.float32),
            pltpu.VMEM((n_pieces, rows, tile), jnp.float32),
            pltpu.VMEM((group, sims, tile), jnp.float32),
            pltpu.SemaphoreType.DMA((2, 2, longer, n_pieces)),
            pltpu.SemaphoreType.DMA((2, 2, longer, n_pieces)),
            pltpu.SemaphoreType.DMA((2, n_pieces)),
            pltpu.SemaphoreType.DMA((2, group, n_pieces)),
        ],
        compiler_params=pltpu.CompilerParams(
            collective_id=0, has_side_effects=True, vmem_limit_bytes=48 * 1024 * 1024
        ),
    )(part)


def gather_kernel(n_x, piece_ref, out_ref, local_sem, send_sem, recv_sem):
    me = lax.axis_index("row")
    col = lax.axis_index("col")
    lag = lax.axis_index("lag")
    y = me // n_x
    x = me % n_x
    right = x + 1
    left = x + n_x - 1
    across = 1 - y
    half = piece_ref.shape[0] // 2

    def slot(yy, xx):
        return yy * n_x + lax.rem(xx, n_x)

    def device(yy, xx):
        return (slot(yy, xx), col, lag)

    few = 16
    sims = piece_ref.shape[1]

    def span(part):
        if part is None:
            return (slice(None),)
        if part < 2:
            return (pl.ds(part * half, half),)
        if part == 2:
            return (slice(None), pl.ds(0, few))
        return (slice(None), pl.ds(few, sims - few))

    def region(index, part):
        sem = recv_sem.at[index, 0 if part is None else part]
        return out_ref.at[(index,) + span(part)], sem

    barrier = pltpu.get_barrier_semaphore()
    for peer in (device(y, right), device(y, left), device(across, x)):
        pl.semaphore_signal(barrier, inc=1, device_id=peer, device_id_type=MESH)
    pl.semaphore_wait(barrier, 3)

    mine = slot(y, x)
    own = pltpu.make_async_copy(piece_ref, out_ref.at[mine], local_sem)
    own.start()
    sends = []

    def send(index, part, dest, from_input=False):
        target, sem = region(index, part)
        if from_input:
            source = piece_ref
        else:
            source = region(index, part)[0]
        copy = pltpu.make_async_remote_copy(
            src_ref=source,
            dst_ref=target,
            send_sem=send_sem.at[len(sends)],
            recv_sem=sem,
            device_id=dest,
            device_id_type=MESH,
        )
        copy.start()
        sends.append(copy)

    def arrive(index, part):
        target, sem = region(index, part)
        source = piece_ref.at[span(part)]
        pltpu.make_async_remote_copy(
            src_ref=source,
            dst_ref=target,
            send_sem=send_sem.at[0],
            recv_sem=sem,
            device_id=device(y, right),
            device_id_type=MESH,
        ).wait_recv()

    send(mine, None, device(across, x), from_input=True)
    send(mine, None, device(y, right), from_input=True)
    send(mine, None, device(y, left), from_input=True)
    arrive(slot(y, left), None)
    send(slot(y, left), 0, device(y, right))
    send(slot(y, left), 2, device(across, x))
    arrive(slot(y, right), None)
    send(slot(y, right), 1, device(y, left))
    send(slot(y, right), 2, device(across, x))
    arrive(slot(across, x), None)
    send(slot(across, x), 3, device(y, right))
    send(slot(across, x), 3, device(y, left))
    for part in range(2):
        arrive(slot(y, x + 2), part)
        send(slot(y, x + 2), part, device(across, x))
    for part in (2, 3):
        arrive(slot(across, left), part)
        arrive(slot(across, right), part)
    for part in range(2):
        arrive(slot(across, x + 2), part)
    own.wait()
    for copy in sends:
        copy.wait_send()


def all_gather_rows(piece, n_row):
    n_x = n_row // 2
    assert n_x == 4
    return pl.pallas_call(
        functools.partial(gather_kernel, n_x),
        out_shape=jax.ShapeDtypeStruct((n_row,) + piece.shape, piece.dtype),
        in_specs=[pl.BlockSpec(memory_space=pltpu.VMEM)],
        out_specs=pl.BlockSpec(memory_space=pl.ANY),
        scratch_shapes=[
            pltpu.SemaphoreType.DMA(()),
            pltpu.SemaphoreType.DMA((11,)),
            pltpu.SemaphoreType.DMA((n_row, 4)),
        ],
        compiler_params=pltpu.CompilerParams(collective_id=1, has_side_effects=True),
    )(piece)


def parts_kernel(n_lag, rows_ref, cols_ref, count_ref, lag_ref, hist_ref, tiles_ref, out_ref):
    lag = pl.program_id(0)
    slots = tiles_ref.shape[1]
    side = tiles_ref.shape[2]
    halves = hist_ref.shape[3] // side

    @pl.when(lag == 0)
    def _():
        out_ref[...] = jnp.zeros_like(out_ref)

    for k in range(slots):
        @pl.when(k < count_ref[lag])
        def _():
            col = cols_ref[lag, k]
            row = rows_ref[lag, k]
            both = hist_ref[col // halves, 0]
            history = jnp.where(col % halves == 0, both[:, :side], both[:, side:])
            contrib = lax.dot_general(
                history, tiles_ref[0, k], (((1,), (1,)), ((), ())),
                preferred_element_type=jnp.float32,
            )
            half = jnp.where(row % n_lag == lag_ref[0], 0, 1)
            out_ref[half, row // n_lag] += contrib


def stress_parts(history, tiles, rows, cols, count, n_col, n_lag):
    n_row, lags, sims, held = history.shape
    _, slots, side, _ = tiles.shape
    lag = lax.axis_index("lag").astype(jnp.int32).reshape(1)
    grid_spec = pltpu.PrefetchScalarGridSpec(
        num_scalar_prefetch=4,
        grid=(lags,),
        in_specs=[
            pl.BlockSpec((n_row, 1, sims, held), lambda l, *_: (0, l, 0, 0)),
            pl.BlockSpec((1, slots, side, side), lambda l, *_: (l, 0, 0, 0)),
        ],
        out_specs=pl.BlockSpec((2, n_col, sims, side), lambda l, *_: (0, 0, 0, 0)),
    )
    return pl.pallas_call(
        functools.partial(parts_kernel, n_lag),
        out_shape=jax.ShapeDtypeStruct((2, n_col, sims, side), jnp.float32),
        grid_spec=grid_spec,
        compiler_params=pltpu.CompilerParams(vmem_limit_bytes=48 * 1024 * 1024),
    )(rows, cols, count, lag, history, tiles)


def local(
    n_row,
    n_col,
    n_lag,
    history,
    kernel_tiles,
    tile_rows,
    tile_cols,
    tile_count,
    base_stress,
    prev_rate,
    direct_effect,
    state_var,
):
    gathered = all_gather_rows(history[:, 0], n_row)
    tile_side = kernel_tiles.shape[4]
    parts = stress_parts(gathered, kernel_tiles[0, 0], tile_rows[0, 0],
                         tile_cols[0, 0], tile_count[0, 0], n_col, n_lag)
    stress_change = reduce_scatter(parts, n_col)
    driving = base_stress + stress_change
    factor = jnp.exp(state_var) / 2.0
    velocity = prev_rate
    for step in range(NEWTON):
        scaled = velocity * factor
        misfit = direct_effect * inverse_sinh(scaled) + 0.5 * velocity - driving
        slope = direct_effect * factor / jnp.sqrt(1.0 + scaled * scaled) + 0.5
        velocity = velocity - misfit / slope
    return (stress_change, velocity)


def solution(mesh):
    return jax.shard_map(
        functools.partial(local, mesh.shape["row"], mesh.shape["col"], mesh.shape["lag"]),
        mesh=mesh,
        in_specs=(
            P("lag", "col", None, "row"),
            P("row", "col", "lag", None, None, None),
            P("row", "col", "lag", None),
            P("row", "col", "lag", None),
            P("row", "col", "lag"),
            P(None, ("row", "col", "lag")),
            P(None, ("row", "col", "lag")),
            P(None, ("row", "col", "lag")),
            P(None, ("row", "col", "lag")),
        ),
        out_specs=(P(None, ("row", "col", "lag")), P(None, ("row", "col", "lag"))),
        check_vma=False,
    )
```
